128 devices in a mesh: dp: 16 (over x, z), expert: 8 (over y, core).
Axes of the slice: x: 4, y: 4, z: 4, core: 2. Of those that a mesh axis runs over, the one named last changes fastest.
Arguments:
- tokens: bfloat16 [65536, 1024], P(('dp', 'expert')), may hold values from -6 to 6
- block_expert: int32 [512], P(('dp', 'expert')), may hold values from 0 to 63, as said below
- gate_weight: bfloat16 [64, 1024, 384], P('expert'), may hold values from -0.1875 to 0.1875
- up_weight: bfloat16 [64, 1024, 384], P('expert'), may hold values from -0.1875 to 0.1875
Outputs:
- gram_factor: float32 [64, 384, 384], P('expert', 'dp')
The draws below stay inside these ranges and needn't reach their ends.
Inputs may be any that keep to these rules, and one draw needn't show every extreme that they name: `block_expert`: expert e is held by index e // 8 of the expert axis. Among the 4 blocks of one device, at most 1 name experts of any one index of the expert axis; in every group of devices along the expert axis, one index of the expert axis receives exactly 1 block from every device of the group.
All inputs are finite; a program needn't handle non-finite values.
Results may differ from the reference program's by a relative error of at most 0.0031.
Values may be sent and summed in bfloat16 or wider, within the bound.
No kernel may reach another device: no remote copies, remote signals or barrier semaphores. Data moves between devices by JAX's collectives and lax.ppermute only.
A program may use at most 128 MiB of HBM per device.

```python
import jax
import jax.numpy as jnp
from jax import lax

D = 1024
FF = 384
EXP_DEV = 8
BLOCK = 128
BLK_DEV = 4
CAP = 1
EXPERTS = 64
TOKENS = 65536
BLOCKS = 512
NORM_ROWS = 1024
N_DP = 16
N_EXPERT = 8


def draw_block_expert(key, part):
    devices = N_DP * N_EXPERT
    remaining = BLK_DEV - CAP
    spare_slots = (N_EXPERT - 1) * CAP
    key_hot, key_pick, key_local, key_order = jax.random.split(key, 4)
    hot_owner = jax.random.randint(key_hot, (N_DP, 1), 0, N_EXPERT)
    hot_owner = jnp.broadcast_to(hot_owner, (N_DP, N_EXPERT)).reshape(devices, 1)
    scores = jax.random.randint(key_pick, (devices, spare_slots), 0, 1 << 20) * spare_slots + jnp.arange(spare_slots)
    chosen = jnp.argsort(scores, axis=1)[:, :remaining]
    others = (hot_owner + 1 + chosen // CAP) % N_EXPERT
    owners_all = jnp.concatenate([jnp.broadcast_to(hot_owner, (devices, CAP)), others], axis=1)
    local_expert = jax.random.randint(key_local, (devices, BLK_DEV), 0, EXP_DEV)
    order_scores = jax.random.randint(key_order, (devices, BLK_DEV), 0, 1 << 20) * BLK_DEV + jnp.arange(BLK_DEV)
    shuffle = jnp.argsort(order_scores, axis=1)
    owners_all = jnp.take_along_axis(owners_all, shuffle, axis=1)
    return (owners_all * EXP_DEV + local_expert).reshape(-1).astype(jnp.int32)


def levels(stream_key, extent, pieces, low, high):
    def one(position, blocks):
        draws = jax.random.uniform(jax.random.fold_in(jax.random.fold_in(stream_key, 6), position), (blocks,), jnp.float32, low / len(pieces), high / len(pieces))
        return jnp.repeat(jnp.exp(draws), extent[position] // blocks).reshape((-1,) + (1,) * (len(extent) - position - 1))

    level = one(*pieces[0])
    for cut in pieces[1:]:
        level = level * one(*cut)
    return level


def bell_draw(stream_key, shape, deviation, bound, cuts=(), kind=jnp.bfloat16):
    result = jax.random.normal(stream_key, shape, jnp.float32) * deviation
    if len(cuts) > 0:
        result = levels(stream_key, shape, cuts, -0.22, 0.18) * result
    return jnp.clip(result, min=-bound, max=bound).astype(kind)


def setup_inputs(seed: int = 0) -> dict:
    key_list = jax.random.split(jax.random.key(seed), 5)
    tokens = bell_draw(key_list[0], (TOKENS, D), 1.0, 6.0, ((0, 128),))
    block_expert = draw_block_expert(jax.random.fold_in(key_list[4], 71), 0)
    gate_weight = bell_draw(key_list[2], (EXPERTS, D, FF), D ** -0.5, 0.1875, ((0, 8),))
    up_weight = bell_draw(key_list[3], (EXPERTS, D, FF), D ** -0.5, 0.1875, ((0, 8),))
    return dict(tokens=tokens, block_expert=block_expert, gate_weight=gate_weight, up_weight=up_weight)


RIDGE = 0.05

def reference(tokens, block_expert, gate_weight, up_weight):
    blocks = tokens.reshape(BLOCKS, BLOCK, D)

    def accumulate(gram_sum, entry):
        rows_in, expert = entry
        gate_matrix = lax.dynamic_index_in_dim(gate_weight, expert, 0, keepdims=False)
        up_matrix = lax.dynamic_index_in_dim(up_weight, expert, 0, keepdims=False)
        gate_proj = jnp.dot(rows_in.astype(jnp.float32), gate_matrix.astype(jnp.float32), preferred_element_type=jnp.float32)
        up_proj = jnp.dot(rows_in.astype(jnp.float32), up_matrix.astype(jnp.float32), preferred_element_type=jnp.float32)
        hidden = (jax.nn.silu(gate_proj) * up_proj).astype(jnp.bfloat16)
        product = jnp.dot(hidden.T.astype(jnp.float32), hidden.astype(jnp.float32), preferred_element_type=jnp.float32)
        current = lax.dynamic_index_in_dim(gram_sum, expert, 0, keepdims=False)
        gram_sum = lax.dynamic_update_index_in_dim(gram_sum, current + product, expert, 0)
        return (gram_sum, None)
    start_sum = jnp.zeros((EXPERTS, FF, FF), jnp.float32)
    gram_sum, unused = lax.scan(accumulate, start_sum, (blocks, block_expert.astype(jnp.int32)))
    gram = gram_sum * (1.0 / NORM_ROWS) + RIDGE * jnp.eye(FF, dtype=jnp.float32)
    lower_part = jnp.linalg.cholesky(gram)
    return jnp.swapaxes(lower_part, 1, 2)
```

```python
import jax
import jax.numpy as jnp
from jax import lax
from jax.experimental import pallas as pl
from jax.experimental.pallas import tpu as pltpu
from jax.sharding import PartitionSpec as P

BLOCK = 128
RIDGE = 0.05
LANE = 128
TAG = 16
F32 = jnp.float32
BF16 = jnp.bfloat16
HIGH = lax.Precision.HIGHEST
TN = (((0,), (0,)), ((), ()))
TILES = ((0, 0), (0, 1), (0, 2), (1, 1), (1, 2), (2, 2))


def pack_kernel(assign_ref, dest_ref, tok_ref, *rest, experts_each):
    slots = len(rest) - 2
    outs, tag_ref, sem = rest[:slots], rest[slots], rest[slots + 1]
    blocks, chunks = tok_ref.shape[0] // BLOCK, tok_ref.shape[1] // LANE
    copies = []
    for s in range(slots):
        block = jnp.int32(0)
        code = jnp.int32(0)
        for b in range(blocks):
            expert = assign_ref[b]
            owner = lax.div(expert, experts_each)
            hit = owner == dest_ref[s]
            block = jnp.where(hit, b, block)
            code = jnp.where(hit, expert - owner * experts_each + 1, code)
        tag_ref[s] = jnp.full((TAG, LANE), code.astype(F32), F32).astype(BF16)
        row = pl.multiple_of(block * BLOCK, BLOCK)
        for c in range(chunks):
            copies.append(
                pltpu.make_async_copy(
                    tok_ref.at[pl.ds(row, BLOCK), c * LANE : (c + 1) * LANE],
                    outs[s].at[c * BLOCK : (c + 1) * BLOCK, :],
                    sem.at[s, c],
                )
            )
        copies.append(
            pltpu.make_async_copy(
                tag_ref.at[s], outs[s].at[chunks * BLOCK : chunks * BLOCK + TAG, :], sem.at[s, chunks]
            )
        )
    for copy in copies:
        copy.start()
    for copy in copies:
        copy.wait()


def pack(assign, dest, tokens, experts_each):
    slots = dest.shape[0]
    rows = BLOCK * tokens.shape[1] // LANE + TAG
    return pl.pallas_call(
        lambda *refs: pack_kernel(*refs, experts_each=experts_each),
        grid_spec=pltpu.PrefetchScalarGridSpec(
            num_scalar_prefetch=2,
            grid=(1,),
            in_specs=[pl.BlockSpec(tokens.shape, lambda i, a, d: (0, 0))],
            out_specs=[pl.BlockSpec(memory_space=pl.ANY)] * slots,
            scratch_shapes=[
                pltpu.VMEM((slots, TAG, LANE), BF16),
                pltpu.SemaphoreType.DMA((slots, rows // BLOCK + 1)),
            ],
        ),
        out_shape=[jax.ShapeDtypeStruct((rows, LANE), BF16)] * slots,
        name="pack",
    )(assign, dest, tokens)


def gram_kernel(*refs, slots, model_width):
    xs = refs[:slots]
    gate_ref, up_ref, out_ref, gate_buf, up_buf, sem = refs[slots:]
    chunks = model_width // LANE
    ids = []
    for s in range(slots):
        tag = xs[s][chunks * BLOCK : chunks * BLOCK + TAG, :].astype(F32)
        ids.append(jnp.max(tag).astype(jnp.int32) - 1)

    def loads(s):
        e = jnp.maximum(ids[s], 0)
        return (
            pltpu.make_async_copy(gate_ref.at[e], gate_buf.at[s], sem.at[0, s]),
            pltpu.make_async_copy(up_ref.at[e], up_buf.at[s], sem.at[1, s]),
        )

    for s in range(slots):

        @pl.when(ids[s] >= 0)
        def _(s=s):
            for copy in loads(s):
                copy.start()

    out_ref[...] = jnp.zeros(out_ref.shape, F32)
    for s in range(slots):

        @pl.when(ids[s] >= 0)
        def _(s=s):
            for copy in loads(s):
                copy.wait()
            x = jnp.concatenate(
                [xs[s][c * BLOCK : (c + 1) * BLOCK, :] for c in range(chunks)], axis=1
            )
            gate = jnp.dot(x, gate_buf[s], preferred_element_type=F32)
            up = jnp.dot(x, up_buf[s], preferred_element_type=F32)
            hidden = (gate / (1.0 + jnp.exp(-gate)) * up).astype(BF16)
            base = 2 * ids[s]
            for i in range(3):
                part = lax.dot_general(
                    hidden[:, i * LANE : (i + 1) * LANE],
                    hidden[:, i * LANE :],
                    TN,
                    preferred_element_type=F32,
                )
                for j in range(i, 3):
                    t = TILES.index((i, j))
                    rows = slice((t % 3) * LANE, (t % 3 + 1) * LANE)
                    out_ref[base + t // 3, rows, :] += part[:, (j - i) * LANE : (j - i + 1) * LANE]


def gram(arrived, gate_weight, up_weight):
    slots = len(arrived)
    experts_each, model_width, hidden_width = gate_weight.shape
    return pl.pallas_call(
        lambda *refs: gram_kernel(*refs, slots=slots, model_width=model_width),
        in_specs=[pl.BlockSpec(memory_space=pltpu.VMEM)] * slots
        + [pl.BlockSpec(memory_space=pl.ANY)] * 2,
        out_specs=pl.BlockSpec(memory_space=pltpu.VMEM),
        out_shape=jax.ShapeDtypeStruct((2 * experts_each, hidden_width, LANE), F32),
        scratch_shapes=[
            pltpu.VMEM((slots, model_width, hidden_width), BF16),
            pltpu.VMEM((slots, model_width, hidden_width), BF16),
            pltpu.SemaphoreType.DMA((2, slots)),
        ],
        name="gram",
    )(*arrived, gate_weight, up_weight)


def factor_strip(strip, c, sub):
    groups = strip.shape[1] // LANE
    wide = lambda v: jnp.concatenate([v] * groups, axis=1) if groups > 1 else v
    cols = [jnp.broadcast_to(strip[:, c * 8 + j : c * 8 + j + 1], (8, LANE)) for j in range(8)]
    wide_sub = wide(sub)
    for k in range(8):
        inv = lax.rsqrt(cols[k][k : k + 1, :])
        mult = jnp.where(sub > k, cols[k] * inv, 0.0)
        row = strip[k : k + 1, :] * wide(inv)
        strip = jnp.where(wide_sub == k, row, strip - wide(mult) * row)
        for j in range(k + 1, 8):
            cols[j] = cols[j] - mult * (cols[j][k : k + 1, :] * inv)
    return strip


def factor_kernel(first_ref, second_ref, out_ref, work, *, scale):
    sub = lax.broadcasted_iota(jnp.int32, (8, LANE), 0)
    lane = lax.broadcasted_iota(jnp.int32, (8, LANE), 1)
    eye = lax.broadcasted_iota(jnp.int32, (LANE, LANE), 0) == lax.broadcasted_iota(
        jnp.int32, (LANE, LANE), 1
    )
    for t, (i, j) in enumerate(TILES):
        source = first_ref if t < 3 else second_ref
        tile = source[(t % 3) * LANE : (t % 3 + 1) * LANE, :] * scale
        if i == j:
            tile = tile + jnp.where(eye, RIDGE, 0.0)
        work[i * LANE : (i + 1) * LANE, j * LANE : (j + 1) * LANE] = tile
    for p in range(3):
        c0 = p * LANE
        for c in range(16):
            r0 = c0 + c * 8
            strip = factor_strip(work[r0 : r0 + 8, c0:], c, sub)
            diag = jnp.where(lane >= c * 8 + sub, strip[:, :LANE], 0.0)
            strip = jnp.concatenate([diag, strip[:, LANE:]], axis=1) if p < 2 else diag
            work[r0 : r0 + 8, c0:] = strip
            if c < 15:
                update = lax.dot_general(
                    diag, strip, TN, precision=HIGH, preferred_element_type=F32
                )
                work[r0 + 8 : c0 + LANE, c0:] = work[r0 + 8 : c0 + LANE, c0:] - update[c * 8 + 8 :]
        for q in range(p + 1, 3):
            rows = slice(q * LANE, (q + 1) * LANE)
            left = work[c0 : c0 + LANE, rows]
            right = work[c0 : c0 + LANE, q * LANE :]
            work[rows, q * LANE :] = work[rows, q * LANE :] - lax.dot_general(
                left, right, TN, precision=HIGH, preferred_element_type=F32
            )
    for p in range(3):
        rows = slice(p * LANE, (p + 1) * LANE)
        if p:
            out_ref[rows, : p * LANE] = jnp.zeros((LANE, p * LANE), out_ref.dtype)
        out_ref[rows, p * LANE :] = work[rows, p * LANE :].astype(out_ref.dtype)


def factor(first, second, scale):
    width = first.shape[0]
    return pl.pallas_call(
        lambda *refs: factor_kernel(*refs, scale=scale),
        out_shape=jax.ShapeDtypeStruct((width, width), F32),
        scratch_shapes=[pltpu.VMEM((width, width), F32)],
        name="factor",
    )(first, second)


def on_device(tokens, block_expert, gate_weight, up_weight):
    owners = lax.axis_size("expert")
    member = lax.axis_index("expert")
    replicas = lax.axis_size("dp")
    experts_each, model_width, hidden_width = gate_weight.shape
    chips = owners // 2
    shifts = [(dy, dc) for dy in range(chips) for dc in range(2)]
    dest = jnp.stack(
        [((member // 2 + dy) % chips) * 2 + (member % 2 + dc) % 2 for dy, dc in shifts]
    ).astype(jnp.int32)
    outgoing = pack(block_expert, dest, tokens, experts_each)
    arrived = []
    for (dy, dc), payload in zip(shifts, outgoing):
        route = [
            (y * 2 + c, ((y + dy) % chips) * 2 + (c + dc) % 2)
            for y in range(chips)
            for c in range(2)
        ]
        arrived.append(payload if dy == dc == 0 else lax.ppermute(payload, "expert", route))
    partial_gram = gram(arrived, gate_weight, up_weight)
    pieces = lax.all_to_all(partial_gram, "dp", split_axis=0, concat_axis=0, tiled=True)
    own = jnp.sum(pieces.reshape(replicas, hidden_width, LANE), axis=0)
    other = lax.ppermute(own, "dp", [(d, d ^ 1) for d in range(replicas)])
    mean_rows = tokens.shape[0] * replicas // experts_each
    result = factor(own, other, 1.0 / mean_rows)
    row_count = hidden_width // replicas
    sent = result.astype(BF16).reshape(replicas, row_count, hidden_width)
    returned = lax.all_to_all(sent, "dp", split_axis=0, concat_axis=0, tiled=True)
    returned = returned.reshape(experts_each, 2, row_count, hidden_width)
    return returned[:, 0].astype(F32)


def solution(mesh):
    placed = (
        P(("dp", "expert"), None),
        P(("dp", "expert")),
        P("expert", None, None),
        P("expert", None, None),
    )
    return jax.shard_map(
        on_device, mesh=mesh, in_specs=placed, out_specs=P("expert", "dp", None), check_vma=False
    )
```

```python
import jax
import jax.numpy as jnp
from jax import lax
from jax.experimental import pallas as pl
from jax.experimental.pallas import tpu as pltpu
from jax.sharding import PartitionSpec as P

BLOCK = 128
RIDGE = 0.05
LANE = 128
TAG = 16
SIDE = 4
GROUP = 2
F32 = jnp.float32
BF16 = jnp.bfloat16
HIGH = lax.Precision.HIGHEST
TN = (((0,), (0,)), ((), ()))
TILES = ((0, 0), (0, 1), (0, 2), (1, 1), (1, 2), (2, 2))


def pack_kernel(assign_ref, dest_ref, tok_ref, *rest, experts_each):
    slots = len(rest) - 2
    outs, tag_ref, sem = rest[:slots], rest[slots], rest[slots + 1]
    blocks, chunks = tok_ref.shape[0] // BLOCK, tok_ref.shape[1] // LANE
    copies = []
    for s in range(slots):
        block = jnp.int32(0)
        code = jnp.int32(0)
        for b in range(blocks):
            expert = assign_ref[b]
            owner = lax.div(expert, experts_each)
            hit = owner == dest_ref[s]
            block = jnp.where(hit, b, block)
            code = jnp.where(hit, expert - owner * experts_each + 1, code)
        tag_ref[s] = jnp.full((TAG, LANE), code.astype(F32), F32).astype(BF16)
        row = pl.multiple_of(block * BLOCK, BLOCK)
        for c in range(chunks):
            copies.append(
                pltpu.make_async_copy(
                    tok_ref.at[pl.ds(row, BLOCK), c * LANE : (c + 1) * LANE],
                    outs[s].at[c * BLOCK : (c + 1) * BLOCK, :],
                    sem.at[s, c],
                )
            )
        copies.append(
            pltpu.make_async_copy(
                tag_ref.at[s], outs[s].at[chunks * BLOCK : chunks * BLOCK + TAG, :], sem.at[s, chunks]
            )
        )
    for copy in copies:
        copy.start()
    for copy in copies:
        copy.wait()


def pack(assign, dest, tokens, experts_each):
    slots = dest.shape[0]
    rows = BLOCK * tokens.shape[1] // LANE + TAG
    return pl.pallas_call(
        lambda *refs: pack_kernel(*refs, experts_each=experts_each),
        grid_spec=pltpu.PrefetchScalarGridSpec(
            num_scalar_prefetch=2,
            grid=(1,),
            in_specs=[pl.BlockSpec(tokens.shape, lambda i, a, d: (0, 0))],
            out_specs=[pl.BlockSpec(memory_space=pl.ANY)] * slots,
            scratch_shapes=[
                pltpu.VMEM((slots, TAG, LANE), BF16),
                pltpu.SemaphoreType.DMA((slots, rows // BLOCK + 1)),
            ],
        ),
        out_shape=[jax.ShapeDtypeStruct((rows, LANE), BF16)] * slots,
        name="pack",
    )(assign, dest, tokens)


def hidden_kernel(*refs, slots, model_width):
    xs = refs[:slots]
    gate_ref, up_ref, out_ref, gate_buf, up_buf, sem = refs[slots:]
    chunks = model_width // LANE
    codes = []
    for s in range(slots):
        tag = xs[s][chunks * BLOCK : chunks * BLOCK + TAG, :].astype(F32)
        codes.append(jnp.max(tag).astype(jnp.int32))

    def loads(s):
        e = jnp.maximum(codes[s] - 1, 0)
        return (
            pltpu.make_async_copy(gate_ref.at[e], gate_buf.at[s], sem.at[0, s]),
            pltpu.make_async_copy(up_ref.at[e], up_buf.at[s], sem.at[1, s]),
        )

    for s in range(slots):

        @pl.when(codes[s] > 0)
        def _(s=s):
            for copy in loads(s):
                copy.start()

    width = out_ref.shape[1]
    lane = lax.broadcasted_iota(jnp.int32, (TAG, width), 1)
    tags = jnp.zeros((TAG, width), F32)
    for s in range(slots):
        tags = jnp.where(lane == s, codes[s].astype(F32), tags)
    out_ref[slots * BLOCK :, :] = tags.astype(BF16)
    for s in range(slots):

        @pl.when(codes[s] > 0)
        def _(s=s):
            for copy in loads(s):
                copy.wait()
            x = jnp.concatenate(
                [xs[s][c * BLOCK : (c + 1) * BLOCK, :] for c in range(chunks)], axis=1
            )
            gate = jnp.dot(x, gate_buf[s], preferred_element_type=F32)
            up = jnp.dot(x, up_buf[s], preferred_element_type=F32)
            hidden = gate / (1.0 + jnp.exp(-gate)) * up
            out_ref[s * BLOCK : (s + 1) * BLOCK, :] = hidden.astype(BF16)


def hidden_rows(arrived, gate_weight, up_weight):
    slots = len(arrived)
    _, model_width, hidden_width = gate_weight.shape
    return pl.pallas_call(
        lambda *refs: hidden_kernel(*refs, slots=slots, model_width=model_width),
        in_specs=[pl.BlockSpec(memory_space=pltpu.VMEM)] * slots
        + [pl.BlockSpec(memory_space=pl.ANY)] * 2,
        out_specs=pl.BlockSpec(memory_space=pltpu.VMEM),
        out_shape=jax.ShapeDtypeStruct((slots * BLOCK + TAG, hidden_width), BF16),
        scratch_shapes=[
            pltpu.VMEM((slots, model_width, hidden_width), BF16),
            pltpu.VMEM((slots, model_width, hidden_width), BF16),
            pltpu.SemaphoreType.DMA((2, slots)),
        ],
        name="hidden",
    )(*arrived, gate_weight, up_weight)


def gram_kernel(target_ref, *refs, counts, prior):
    groups = refs[: len(counts)]
    start = refs[len(counts) : len(refs) - 4]
    outs = refs[len(refs) - 4 :]
    for t in range(4):
        outs[t][...] = start[t][...] if prior else jnp.zeros(outs[t].shape, F32)
    codes = []
    for ref, slots in zip(groups, counts):
        tag = ref[slots * BLOCK : slots * BLOCK + TAG, :LANE].astype(F32)
        lane = lax.broadcasted_iota(jnp.int32, tag.shape, 1)
        for s in range(slots):
            codes.append(jnp.max(jnp.where(lane == s, tag, 0.0)).astype(jnp.int32))
    where = [(ref, s) for ref, slots in zip(groups, counts) for s in range(slots)]
    for code, (ref, s) in zip(codes, where):
        for o in range(2):

            @pl.when(code == target_ref[o])
            def _(ref=ref, s=s, o=o):
                hidden = ref[s * BLOCK : (s + 1) * BLOCK, :]
                for i in range(3):
                    part = lax.dot_general(
                        hidden[:, i * LANE : (i + 1) * LANE],
                        hidden[:, i * LANE :],
                        TN,
                        preferred_element_type=F32,
                    )
                    for j in range(i, 3):
                        t = TILES.index((i, j))
                        rows = slice((t % 3) * LANE, (t % 3 + 1) * LANE)
                        outs[2 * (t // 3) + o][rows, :] += part[:, (j - i) * LANE : (j - i + 1) * LANE]


def gram(target, groups, prior):
    counts = [(g.shape[0] - TAG) // BLOCK for g in groups]
    width = groups[0].shape[1]
    given = list(prior) if prior is not None else []
    return pl.pallas_call(
        lambda *refs: gram_kernel(*refs, counts=counts, prior=prior is not None),
        in_specs=[pl.BlockSpec(memory_space=pltpu.SMEM)]
        + [pl.BlockSpec(memory_space=pltpu.VMEM)] * (len(groups) + len(given)),
        out_specs=[pl.BlockSpec(memory_space=pltpu.VMEM)] * 4,
        out_shape=[jax.ShapeDtypeStruct((width, LANE), F32)] * 4,
        name="gram",
    )(target, *groups, *given)


def factor_strip(strip, c, sub):
    groups = strip.shape[1] // LANE
    wide = lambda v: jnp.concatenate([v] * groups, axis=1) if groups > 1 else v
    cols = [jnp.broadcast_to(strip[:, c * 8 + j : c * 8 + j + 1], (8, LANE)) for j in range(8)]
    wide_sub = wide(sub)
    for k in range(8):
        inv = lax.rsqrt(cols[k][k : k + 1, :])
        mult = jnp.where(sub > k, cols[k] * inv, 0.0)
        row = strip[k : k + 1, :] * wide(inv)
        strip = jnp.where(wide_sub == k, row, strip - wide(mult) * row)
        for j in range(k + 1, 8):
            cols[j] = cols[j] - mult * (cols[j][k : k + 1, :] * inv)
    return strip


def load_tile(refs, t, scale, eye):
    rows = slice((t % 3) * LANE, (t % 3 + 1) * LANE)
    tile = (refs[0][rows, :] + refs[1][rows, :]) + (refs[2][rows, :] + refs[3][rows, :])
    tile = tile * scale
    if TILES[t][0] == TILES[t][1]:
        tile = tile + jnp.where(eye, RIDGE, 0.0)
    return tile


def eye_tile():
    return lax.broadcasted_iota(jnp.int32, (LANE, LANE), 0) == lax.broadcasted_iota(
        jnp.int32, (LANE, LANE), 1
    )


def factor_panel(work):
    sub = lax.broadcasted_iota(jnp.int32, (8, LANE), 0)
    lane = lax.broadcasted_iota(jnp.int32, (8, LANE), 1)
    width = work.shape[1]
    for c in range(16):
        rows = slice(c * 8, c * 8 + 8)
        strip = factor_strip(work[rows, :], c, sub)
        diag = jnp.where(lane >= c * 8 + sub, strip[:, :LANE], 0.0)
        strip = jnp.concatenate([diag, strip[:, LANE:]], axis=1) if width > LANE else diag
        work[rows, :] = strip
        if c < 15:
            update = lax.dot_general(diag, strip, TN, precision=HIGH, preferred_element_type=F32)
            work[c * 8 + 8 :, :] = work[c * 8 + 8 :, :] - update[c * 8 + 8 :]


def first_panel_kernel(*refs, scale):
    parts, out_ref = refs[:4], refs[4]
    eye = eye_tile()
    for t in range(3):
        out_ref[:, t * LANE : (t + 1) * LANE] = load_tile(parts, t, scale, eye)
    factor_panel(out_ref)


def first_panel(parts, scale):
    width = parts[0].shape[0]
    return pl.pallas_call(
        lambda *refs: first_panel_kernel(*refs, scale=scale),
        out_shape=jax.ShapeDtypeStruct((LANE, width), F32),
        name="first_panel",
    )(*parts)


def rest_kernel(*refs, scale):
    parts, top_ref, out_ref, mid, low = refs[:4], *refs[4:]
    eye = eye_tile()
    dot = lambda a, b: lax.dot_general(a, b, TN, precision=HIGH, preferred_element_type=F32)
    top = top_ref[...]
    mid[...] = jnp.concatenate(
        [load_tile(parts, 3, scale, eye), load_tile(parts, 4, scale, eye)], axis=1
    ) - dot(top[:, LANE : 2 * LANE], top[:, LANE:])
    low[...] = load_tile(parts, 5, scale, eye) - dot(top[:, 2 * LANE :], top[:, 2 * LANE :])
    factor_panel(mid)
    right = mid[:, LANE:]
    low[...] = low[...] - dot(right, right)
    factor_panel(low)
    kind = out_ref.dtype
    out_ref[:LANE, :] = top.astype(kind)
    out_ref[LANE : 2 * LANE, :LANE] = jnp.zeros((LANE, LANE), kind)
    out_ref[LANE : 2 * LANE, LANE:] = mid[...].astype(kind)
    out_ref[2 * LANE :, : 2 * LANE] = jnp.zeros((LANE, 2 * LANE), kind)
    out_ref[2 * LANE :, 2 * LANE :] = low[...].astype(kind)


def rest_panels(parts, top, scale):
    width = parts[0].shape[0]
    return pl.pallas_call(
        lambda *refs: rest_kernel(*refs, scale=scale),
        out_shape=jax.ShapeDtypeStruct((width, width), BF16),
        scratch_shapes=[pltpu.VMEM((LANE, 2 * LANE), F32), pltpu.VMEM((LANE, LANE), F32)],
        name="rest_panels",
    )(*parts, top)


def on_device(tokens, block_expert, gate_weight, up_weight):
    owners = lax.axis_size("expert")
    member = lax.axis_index("expert")
    replicas = lax.axis_size("dp")
    place = lax.axis_index("dp")
    experts_each, model_width, hidden_width = gate_weight.shape
    chips = owners // 2
    side = replicas // SIDE
    shifts = [(0, 0), (0, 1)] + [(dy, dc) for dc in range(2) for dy in (1, chips - 1)]
    shifts += [(2, 0), (2, 1)]
    dest = jnp.stack(
        [((member // 2 + dy) % chips) * 2 + (member % 2 + dc) % 2 for dy, dc in shifts]
    ).astype(jnp.int32)
    outgoing = pack(block_expert, dest, tokens, experts_each)
    arrived = []
    for (dy, dc), payload in zip(shifts, outgoing):
        route = [
            (y * 2 + c, ((y + dy) % chips) * 2 + (c + dc) % 2)
            for y in range(chips)
            for c in range(2)
        ]
        arrived.append(payload if dy == dc == 0 else lax.ppermute(payload, "expert", route))
    along = place // SIDE
    late = (place % SIDE >= SIDE // 2).astype(jnp.int32)
    target = jnp.stack([2 * along + 2 - late, 2 * along + 1 + late]).astype(jnp.int32)
    gathered = []
    for g in range(0, len(arrived), GROUP):
        rows = hidden_rows(arrived[g : g + GROUP], gate_weight, up_weight)
        gathered.append([rows])
        for dx in (1, 3, 2):
            route = [
                (x * SIDE + z, ((x + dx) % side) * SIDE + z)
                for x in range(side)
                for z in range(SIDE)
            ]
            gathered[-1].append(lax.ppermute(rows, "dp", route))
    partial = gram(target, [rows for group in gathered[:-1] for rows in group], None)
    partial = gram(target, gathered[-1], partial)

    def to_owner(send, keep):
        lanes = [
            (send, [(1, 2), (3, 0)]),
            (keep, [(1, 0), (3, 2)]),
            (send, [(0, 2), (2, 0)]),
        ]
        parts = [keep]
        for value, hops in lanes:
            route = [(x * SIDE + a, x * SIDE + b) for x in range(side) for a, b in hops]
            parts.append(lax.ppermute(value, "dp", route))
        return parts

    early = to_owner(partial[0], partial[1])
    later = to_owner(partial[2], partial[3])
    scale = experts_each / (tokens.shape[0] * replicas)
    top = first_panel(early, scale)
    result = rest_panels(later, top, scale)
    row_count = hidden_width // replicas
    sent = result.reshape(replicas, row_count, hidden_width)
    returned = lax.all_to_all(sent, "dp", split_axis=0, concat_axis=0, tiled=True)
    returned = returned.reshape(experts_each, 2, row_count, hidden_width)
    return returned[:, 0].astype(F32)


def solution(mesh):
    placed = (
        P(("dp", "expert"), None),
        P(("dp", "expert")),
        P("expert", None, None),
        P("expert", None, None),
    )
    return jax.shard_map(
        on_device, mesh=mesh, in_specs=placed, out_specs=P("expert", "dp", None), check_vma=False
    )
```

```python
import jax
import jax.numpy as jnp
from jax import lax
from jax.experimental import pallas as pl
from jax.experimental.pallas import tpu as pltpu
from jax.sharding import PartitionSpec as P

BLOCK = 128
RIDGE = 0.05
LANE = 128
TAG = 16
LATE = 2
STRIP = 32
F32 = jnp.float32
BF16 = jnp.bfloat16
HIGH = lax.Precision.HIGHEST
TN = (((0,), (0,)), ((), ()))
TILES = ((0, 0), (0, 1), (0, 2), (1, 1), (1, 2), (2, 2))


def pack_kernel(assign_ref, member_ref, tok_ref, *outs, experts_each, shifts, chips):
    blocks, chunks = tok_ref.shape[0] // BLOCK, tok_ref.shape[1] // LANE
    chip = lax.div(member_ref[0], 2)
    core = lax.rem(member_ref[0], 2)
    for (dy, dc), out in zip(shifts, outs):
        dest = lax.rem(chip + dy, chips) * 2 + lax.rem(core + dc, 2)
        block = jnp.int32(0)
        code = jnp.int32(0)
        for b in range(blocks):
            expert = assign_ref[b]
            owner = lax.div(expert, experts_each)
            hit = owner == dest
            block = jnp.where(hit, b, block)
            code = jnp.where(hit, expert - owner * experts_each + 1, code)
        row = pl.multiple_of(block * BLOCK, BLOCK)
        for c in range(chunks):
            out[c * BLOCK : (c + 1) * BLOCK, :] = tok_ref[
                pl.ds(row, BLOCK), c * LANE : (c + 1) * LANE
            ]
        out[chunks * BLOCK :, :] = jnp.full((TAG, LANE), code.astype(F32), F32).astype(BF16)


def pack(assign, member, tokens, experts_each, shifts, chips):
    rows = BLOCK * tokens.shape[1] // LANE + TAG
    return pl.pallas_call(
        lambda *refs: pack_kernel(*refs, experts_each=experts_each, shifts=shifts, chips=chips),
        in_specs=[pl.BlockSpec(memory_space=pltpu.SMEM)] * 2
        + [pl.BlockSpec(memory_space=pltpu.VMEM)],
        out_specs=[pl.BlockSpec(memory_space=pltpu.VMEM)] * len(shifts),
        out_shape=[jax.ShapeDtypeStruct((rows, LANE), BF16)] * len(shifts),
        name="pack",
    )(assign, member, tokens)


def gram_kernel(*refs, slots, model_width, prior):
    xs = refs[:slots]
    gate_ref, up_ref = refs[slots : slots + 2]
    out_ref, gate_buf, up_buf, sem = refs[-4:]
    chunks = model_width // LANE
    ids = []
    for s in range(slots):
        tag = xs[s][chunks * BLOCK : chunks * BLOCK + TAG, :].astype(F32)
        ids.append(jnp.max(tag).astype(jnp.int32) - 1)

    def loads(s):
        e = jnp.maximum(ids[s], 0)
        return (
            pltpu.make_async_copy(gate_ref.at[e], gate_buf.at[s], sem.at[0, s]),
            pltpu.make_async_copy(up_ref.at[e], up_buf.at[s], sem.at[1, s]),
        )

    for s in range(slots):

        @pl.when(ids[s] >= 0)
        def _(s=s):
            for copy in loads(s):
                copy.start()

    out_ref[...] = refs[slots + 2][...] if prior else jnp.zeros(out_ref.shape, F32)
    for s in range(slots):

        @pl.when(ids[s] >= 0)
        def _(s=s):
            for copy in loads(s):
                copy.wait()
            x = jnp.concatenate(
                [xs[s][c * BLOCK : (c + 1) * BLOCK, :] for c in range(chunks)], axis=1
            )
            gate = jnp.dot(x, gate_buf[s], preferred_element_type=F32)
            up = jnp.dot(x, up_buf[s], preferred_element_type=F32)
            hidden = (gate / (1.0 + jnp.exp(-gate)) * up).astype(BF16)
            base = 2 * ids[s]
            for i in range(3):
                part = lax.dot_general(
                    hidden[:, i * LANE : (i + 1) * LANE],
                    hidden[:, i * LANE :],
                    TN,
                    preferred_element_type=F32,
                )
                for j in range(i, 3):
                    t = TILES.index((i, j))
                    rows = slice((t % 3) * LANE, (t % 3 + 1) * LANE)
                    out_ref[base + t // 3, rows, :] += part[:, (j - i) * LANE : (j - i + 1) * LANE]


def gram(arrived, gate_weight, up_weight, prior=()):
    slots = len(arrived)
    experts_each, model_width, hidden_width = gate_weight.shape
    return pl.pallas_call(
        lambda *refs: gram_kernel(
            *refs, slots=slots, model_width=model_width, prior=len(prior) > 0
        ),
        in_specs=[pl.BlockSpec(memory_space=pltpu.VMEM)] * slots
        + [pl.BlockSpec(memory_space=pl.ANY)] * 2
        + [pl.BlockSpec(memory_space=pltpu.VMEM)] * len(prior),
        out_specs=pl.BlockSpec(memory_space=pltpu.VMEM),
        out_shape=jax.ShapeDtypeStruct((2 * experts_each, hidden_width, LANE), F32),
        scratch_shapes=[
            pltpu.VMEM((slots, model_width, hidden_width), BF16),
            pltpu.VMEM((slots, model_width, hidden_width), BF16),
            pltpu.SemaphoreType.DMA((2, slots)),
        ],
        name="gram",
    )(*arrived, gate_weight, up_weight, *prior)


def factor_strip(groups, lane0, sub):
    wide = lambda v: jnp.concatenate([v] * (groups[0].shape[1] // LANE), axis=1)
    groups = list(groups)
    wide_sub = wide(sub)
    for b in range(len(groups)):
        base = lane0 + 8 * b
        cols = [
            [jnp.broadcast_to(g[:, base + j : base + j + 1], (8, LANE)) for g in groups[b:]]
            for j in range(8)
        ]
        for k in range(8):
            inv = lax.rsqrt(cols[k][0][k : k + 1, :])
            row = groups[b][k : k + 1, :] * wide(inv)
            mult = [c * inv for c in cols[k]]
            mult[0] = jnp.where(sub > k, mult[0], 0.0)
            for g, m in enumerate(mult):
                groups[b + g] = groups[b + g] - wide(m) * row
            groups[b] = jnp.where(wide_sub == k, row, groups[b])
            for j in range(k + 1, 8):
                top = cols[j][0][k : k + 1, :] * inv
                cols[j] = [c - m * top for c, m in zip(cols[j], mult)]
    return groups


def dot_high(a, b, dims):
    return lax.dot_general(a, b, dims, precision=HIGH, preferred_element_type=F32)


def factor_panel(work):
    sub = lax.broadcasted_iota(jnp.int32, (8, LANE), 0)
    lane = lax.broadcasted_iota(jnp.int32, (8, LANE), 1)
    width = work.shape[1]
    for r0 in range(0, LANE, STRIP):
        r1 = r0 + STRIP
        groups = factor_strip([work[r : r + 8, :] for r in range(r0, r1, 8)], r0, sub)
        diag = jnp.concatenate(
            [
                jnp.where(lane >= r0 + 8 * g + sub, rows[:, :LANE], 0.0)
                for g, rows in enumerate(groups)
            ],
            axis=0,
        )
        strip = diag
        if width > LANE:
            right = jnp.concatenate([rows[:, LANE:] for rows in groups], axis=0)
            strip = jnp.concatenate([diag, right], axis=1)
        work[r0:r1, :] = strip
        if r1 < LANE:
            work[r1:, :] = work[r1:, :] - dot_high(diag.T[r1:, :], strip, (((1,), (0,)), ((), ())))


def load_tile(ref, t, scale):
    tile = ref[(t % 3) * LANE : (t % 3 + 1) * LANE, :] * scale
    if TILES[t][0] == TILES[t][1]:
        eye = lax.broadcasted_iota(jnp.int32, tile.shape, 0) == lax.broadcasted_iota(
            jnp.int32, tile.shape, 1
        )
        tile = tile + jnp.where(eye, RIDGE, 0.0)
    return tile


def first_kernel(part_ref, out_ref, *, scale):
    for t in range(3):
        out_ref[:, t * LANE : (t + 1) * LANE] = load_tile(part_ref, t, scale)
    factor_panel(out_ref)


def first_panel(part, scale):
    return pl.pallas_call(
        lambda *refs: first_kernel(*refs, scale=scale),
        out_shape=jax.ShapeDtypeStruct((LANE, part.shape[0]), F32),
        name="first_panel",
    )(part)


def rest_kernel(part_ref, top_ref, out_ref, mid, low, *, scale):
    top = top_ref[...]
    mid[:, :LANE] = load_tile(part_ref, 3, scale)
    mid[:, LANE:] = load_tile(part_ref, 4, scale)
    mid[...] = mid[...] - dot_high(top[:, LANE : 2 * LANE], top[:, LANE:], TN)
    low[...] = load_tile(part_ref, 5, scale) - dot_high(top[:, 2 * LANE :], top[:, 2 * LANE :], TN)
    factor_panel(mid)
    right = mid[:, LANE:]
    low[...] = low[...] - dot_high(right, right, TN)
    factor_panel(low)
    kind = out_ref.dtype
    out_ref[:LANE, :] = top.astype(kind)
    out_ref[LANE : 2 * LANE, :LANE] = jnp.zeros((LANE, LANE), kind)
    out_ref[LANE : 2 * LANE, LANE:] = mid[...].astype(kind)
    out_ref[2 * LANE :, : 2 * LANE] = jnp.zeros((LANE, 2 * LANE), kind)
    out_ref[2 * LANE :, 2 * LANE :] = low[...].astype(kind)


def rest_panels(part, top, scale):
    width = part.shape[0]
    return pl.pallas_call(
        lambda *refs: rest_kernel(*refs, scale=scale),
        out_shape=jax.ShapeDtypeStruct((width, width), BF16),
        scratch_shapes=[pltpu.VMEM((LANE, 2 * LANE), F32), pltpu.VMEM((LANE, LANE), F32)],
        name="rest_panels",
    )(part, top)


def on_device(tokens, block_expert, gate_weight, up_weight):
    owners = lax.axis_size("expert")
    replicas = lax.axis_size("dp")
    experts_each, model_width, hidden_width = gate_weight.shape
    chips = owners // 2
    shifts = [(0, 0), (0, 1)] + [(dy, dc) for dc in range(2) for dy in (1, chips - 1)]
    shifts += [(2, 0), (2, 1)]
    member = lax.axis_index("expert").reshape(1)
    outgoing = pack(block_expert, member, tokens, experts_each, shifts, chips)
    arrived = []
    for (dy, dc), payload in zip(shifts, outgoing):
        route = [
            (y * 2 + c, ((y + dy) % chips) * 2 + (c + dc) % 2)
            for y in range(chips)
            for c in range(2)
        ]
        arrived.append(payload if dy == dc == 0 else lax.ppermute(payload, "expert", route))
    partial_gram = gram(arrived[:-LATE], gate_weight, up_weight)
    partial_gram = gram(arrived[-LATE:], gate_weight, up_weight, (partial_gram,))
    pieces = lax.all_to_all(partial_gram, "dp", split_axis=0, concat_axis=0, tiled=True)
    own = jnp.sum(pieces.reshape(replicas, hidden_width, LANE), axis=0)
    other = lax.ppermute(own, "dp", [(d + 1, d) for d in range(0, replicas, 2)])
    scale = experts_each / (tokens.shape[0] * replicas)
    top = first_panel(own, scale)
    result = rest_panels(other, top, scale)
    row_count = hidden_width // replicas
    sent = result.reshape(replicas, row_count, hidden_width)
    returned = lax.all_to_all(sent, "dp", split_axis=0, concat_axis=0, tiled=True)
    returned = returned.reshape(experts_each, 2, row_count, hidden_width)
    return returned[:, 0].astype(F32)


def solution(mesh):
    placed = (
        P(("dp", "expert"), None),
        P(("dp", "expert")),
        P("expert", None, None),
        P("expert", None, None),
    )
    return jax.shard_map(
        on_device, mesh=mesh, in_specs=placed, out_specs=P("expert", "dp", None), check_vma=False
    )
```

```python
import jax
import jax.numpy as jnp
from jax import lax
from jax.experimental import pallas as pl
from jax.experimental.pallas import tpu as pltpu
from jax.sharding import PartitionSpec as P

BLOCK = 128
RIDGE = 0.05
LANE = 128
TAG = 16
SIDE = 4
VMEM_BYTES = 20 << 20
EDGES = (0, 2, 6, 8)
STRIP = 32
F32 = jnp.float32
BF16 = jnp.bfloat16
HIGH = lax.Precision.HIGHEST
TN = (((0,), (0,)), ((), ()))
TILES = ((0, 0), (0, 1), (0, 2), (1, 1), (1, 2), (2, 2))


def near(x):
    return pltpu.with_memory_space_constraint(x, pltpu.VMEM)


def pack_kernel(assign_ref, member_ref, tok_ref, *outs, experts_each, shifts, chips):
    blocks, chunks = tok_ref.shape[0] // BLOCK, tok_ref.shape[1] // LANE
    chip = lax.div(member_ref[0], 2)
    core = lax.rem(member_ref[0], 2)
    for (dy, dc), out in zip(shifts, outs):
        dest = lax.rem(chip + dy, chips) * 2 + lax.rem(core + dc, 2)
        block = jnp.int32(0)
        code = jnp.int32(0)
        for b in range(blocks):
            expert = assign_ref[b]
            owner = lax.div(expert, experts_each)
            hit = owner == dest
            block = jnp.where(hit, b, block)
            code = jnp.where(hit, expert - owner * experts_each + 1, code)
        row = pl.multiple_of(block * BLOCK, BLOCK)
        for c in range(chunks):
            out[c * BLOCK : (c + 1) * BLOCK, :] = tok_ref[
                pl.ds(row, BLOCK), c * LANE : (c + 1) * LANE
            ]
        out[chunks * BLOCK :, :] = jnp.full((TAG, LANE), code.astype(F32), F32).astype(BF16)


def pack(assign, member, tokens, experts_each, shifts, chips):
    rows = BLOCK * tokens.shape[1] // LANE + TAG
    return pl.pallas_call(
        lambda *refs: pack_kernel(*refs, experts_each=experts_each, shifts=shifts, chips=chips),
        in_specs=[pl.BlockSpec(memory_space=pltpu.SMEM)] * 2
        + [pl.BlockSpec(memory_space=pltpu.VMEM)],
        out_specs=[pl.BlockSpec(memory_space=pltpu.VMEM)] * len(shifts),
        out_shape=[pltpu.VMEM((rows, LANE), BF16)] * len(shifts),
        compiler_params=pltpu.CompilerParams(vmem_limit_bytes=VMEM_BYTES),
        name="pack",
    )(assign, member, tokens)


def hidden_kernel(*refs, slots, model_width):
    xs = refs[:slots]
    gate_ref, up_ref, out_ref = refs[slots:]
    chunks = model_width // LANE
    codes = []
    for s in range(slots):
        tag = xs[s][chunks * BLOCK : chunks * BLOCK + TAG, :].astype(F32)
        codes.append(jnp.max(tag).astype(jnp.int32))

    width = out_ref.shape[1]
    lane = lax.broadcasted_iota(jnp.int32, (TAG, width), 1)
    tags = jnp.zeros((TAG, width), F32)
    for s in range(slots):
        tags = jnp.where(lane == s, codes[s].astype(F32), tags)
    out_ref[slots * BLOCK :, :] = tags.astype(BF16)
    for s in range(slots):

        @pl.when(codes[s] > 0)
        def _(s=s):
            expert = codes[s] - 1
            x = jnp.concatenate(
                [xs[s][c * BLOCK : (c + 1) * BLOCK, :] for c in range(chunks)], axis=1
            )
            gate = jnp.dot(x, gate_ref[expert], preferred_element_type=F32)
            up = jnp.dot(x, up_ref[expert], preferred_element_type=F32)
            hidden = gate / (1.0 + jnp.exp(-gate)) * up
            out_ref[s * BLOCK : (s + 1) * BLOCK, :] = hidden.astype(BF16)


def hidden_rows(arrived, gate_weight, up_weight):
    slots = len(arrived)
    _, model_width, hidden_width = gate_weight.shape
    return pl.pallas_call(
        lambda *refs: hidden_kernel(*refs, slots=slots, model_width=model_width),
        in_specs=[pl.BlockSpec(memory_space=pltpu.VMEM)] * (slots + 2),
        out_specs=pl.BlockSpec(memory_space=pltpu.VMEM),
        out_shape=pltpu.VMEM((slots * BLOCK + TAG, hidden_width), BF16),
        compiler_params=pltpu.CompilerParams(vmem_limit_bytes=VMEM_BYTES),
        name="hidden",
    )(*[near(x) for x in (*arrived, gate_weight, up_weight)])


def bring_kernel(_, gate_ref, up_ref, gate_out, up_out, sem):
    copies = [
        pltpu.make_async_copy(gate_ref, gate_out, sem.at[0]),
        pltpu.make_async_copy(up_ref, up_out, sem.at[1]),
    ]
    for copy in copies:
        copy.start()
    for copy in copies:
        copy.wait()


def bring(after, gate_weight, up_weight):
    return pl.pallas_call(
        bring_kernel,
        in_specs=[pl.BlockSpec(memory_space=pl.ANY)] * 3,
        out_specs=[pl.BlockSpec(memory_space=pltpu.VMEM)] * 2,
        out_shape=[pltpu.VMEM(w.shape, w.dtype) for w in (gate_weight, up_weight)],
        scratch_shapes=[pltpu.SemaphoreType.DMA((2,))],
        compiler_params=pltpu.CompilerParams(vmem_limit_bytes=VMEM_BYTES),
        name="bring",
    )(after, gate_weight, up_weight)


def gram_kernel(first_ref, *refs, counts, kept):
    groups, out_ref = refs[: len(counts)], refs[-1]
    out_ref[...] = refs[-2][...] if len(refs) > len(counts) + 1 else jnp.zeros(out_ref.shape, F32)
    lane = lax.broadcasted_iota(jnp.int32, (TAG, LANE), 1)
    where = [(ref, s, n) for ref, n in zip(groups, counts) for s in range(n)]
    codes = []
    for ref, s, n in where:
        tag = ref[n * BLOCK : n * BLOCK + TAG, :LANE].astype(F32)
        codes.append(jnp.max(jnp.where(lane == s, tag, 0.0)).astype(jnp.int32))
    for code, (ref, s, n) in zip(codes, where):
        local = code - 1 - first_ref[0]

        @pl.when((local >= 0) & (local < kept))
        def _(ref=ref, s=s, local=local):
            hidden = ref[s * BLOCK : (s + 1) * BLOCK, :]
            for i in range(3):
                part = lax.dot_general(
                    hidden[:, i * LANE : (i + 1) * LANE],
                    hidden[:, i * LANE :],
                    TN,
                    preferred_element_type=F32,
                )
                for j in range(i, 3):
                    t = TILES.index((i, j))
                    rows = slice((t % 3) * LANE, (t % 3 + 1) * LANE)
                    out_ref[2 * local + t // 3, rows, :] += part[:, (j - i) * LANE : (j - i + 1) * LANE]


def gram(first, kept, groups, prior=()):
    counts = [(g.shape[0] - TAG) // BLOCK for g in groups]
    return pl.pallas_call(
        lambda *refs: gram_kernel(*refs, counts=counts, kept=kept),
        in_specs=[pl.BlockSpec(memory_space=pltpu.SMEM)]
        + [pl.BlockSpec(memory_space=pltpu.VMEM)] * (len(groups) + len(prior)),
        out_specs=pl.BlockSpec(memory_space=pltpu.VMEM),
        out_shape=pltpu.VMEM((2 * kept, groups[0].shape[1], LANE), F32),
        compiler_params=pltpu.CompilerParams(vmem_limit_bytes=VMEM_BYTES),
        name="gram",
    )(first, *[near(x) for x in (*groups, *prior)])


def factor_strip(groups, lane0, sub):
    wide = lambda v: jnp.concatenate([v] * (groups[0].shape[1] // LANE), axis=1)
    groups = list(groups)
    wide_sub = wide(sub)
    for b in range(len(groups)):
        base = lane0 + 8 * b
        cols = [
            [jnp.broadcast_to(g[:, base + j : base + j + 1], (8, LANE)) for g in groups[b:]]
            for j in range(8)
        ]
        for k in range(8):
            inv = lax.rsqrt(cols[k][0][k : k + 1, :])
            row = groups[b][k : k + 1, :] * wide(inv)
            mult = [c * inv for c in cols[k]]
            mult[0] = jnp.where(sub > k, mult[0], 0.0)
            for g, m in enumerate(mult):
                groups[b + g] = groups[b + g] - wide(m) * row
            groups[b] = jnp.where(wide_sub == k, row, groups[b])
            for j in range(k + 1, 8):
                top = cols[j][0][k : k + 1, :] * inv
                cols[j] = [c - m * top for c, m in zip(cols[j], mult)]
    return groups


def dot_high(a, b, dims):
    return lax.dot_general(a, b, dims, precision=HIGH, preferred_element_type=F32)


def factor_panel(work):
    sub = lax.broadcasted_iota(jnp.int32, (8, LANE), 0)
    lane = lax.broadcasted_iota(jnp.int32, (8, LANE), 1)
    width = work.shape[1]
    for r0 in range(0, LANE, STRIP):
        r1 = r0 + STRIP
        groups = factor_strip([work[r : r + 8, :] for r in range(r0, r1, 8)], r0, sub)
        diag = jnp.concatenate(
            [
                jnp.where(lane >= r0 + 8 * g + sub, rows[:, :LANE], 0.0)
                for g, rows in enumerate(groups)
            ],
            axis=0,
        )
        strip = diag
        if width > LANE:
            right = jnp.concatenate([rows[:, LANE:] for rows in groups], axis=0)
            strip = jnp.concatenate([diag, right], axis=1)
        work[r0:r1, :] = strip
        if r1 < LANE:
            work[r1:, :] = work[r1:, :] - dot_high(diag.T[r1:, :], strip, (((1,), (0,)), ((), ())))


def load_tile(ref, t, scale):
    tile = ref[(t % 3) * LANE : (t % 3 + 1) * LANE, :] * scale
    if TILES[t][0] == TILES[t][1]:
        eye = lax.broadcasted_iota(jnp.int32, tile.shape, 0) == lax.broadcasted_iota(
            jnp.int32, tile.shape, 1
        )
        tile = tile + jnp.where(eye, RIDGE, 0.0)
    return tile


def first_kernel(part_ref, out_ref, *, scale):
    for t in range(3):
        out_ref[:, t * LANE : (t + 1) * LANE] = load_tile(part_ref, t, scale)
    factor_panel(out_ref)


def first_panel(part, scale):
    return pl.pallas_call(
        lambda *refs: first_kernel(*refs, scale=scale),
        out_shape=pltpu.VMEM((LANE, part.shape[0]), F32),
        compiler_params=pltpu.CompilerParams(vmem_limit_bytes=VMEM_BYTES),
        name="first_panel",
    )(near(part))


def rest_kernel(part_ref, top_ref, out_ref, mid, low, *, scale):
    top = top_ref[...]
    mid[:, :LANE] = load_tile(part_ref, 3, scale)
    mid[:, LANE:] = load_tile(part_ref, 4, scale)
    mid[...] = mid[...] - dot_high(top[:, LANE : 2 * LANE], top[:, LANE:], TN)
    low[...] = load_tile(part_ref, 5, scale) - dot_high(top[:, 2 * LANE :], top[:, 2 * LANE :], TN)
    factor_panel(mid)
    right = mid[:, LANE:]
    low[...] = low[...] - dot_high(right, right, TN)
    factor_panel(low)
    kind = out_ref.dtype
    out_ref[:LANE, :] = top.astype(kind)
    out_ref[LANE : 2 * LANE, :LANE] = jnp.zeros((LANE, LANE), kind)
    out_ref[LANE : 2 * LANE, LANE:] = mid[...].astype(kind)
    out_ref[2 * LANE :, : 2 * LANE] = jnp.zeros((LANE, 2 * LANE), kind)
    out_ref[2 * LANE :, 2 * LANE :] = low[...].astype(kind)


def rest_panels(part, top, scale):
    width = part.shape[0]
    return pl.pallas_call(
        lambda *refs: rest_kernel(*refs, scale=scale),
        out_shape=pltpu.VMEM((width, width), BF16),
        scratch_shapes=[pltpu.VMEM((LANE, 2 * LANE), F32), pltpu.VMEM((LANE, LANE), F32)],
        compiler_params=pltpu.CompilerParams(vmem_limit_bytes=VMEM_BYTES),
        name="rest_panels",
    )(near(part), near(top))


def on_device(tokens, block_expert, gate_weight, up_weight):
    owners = lax.axis_size("expert")
    replicas = lax.axis_size("dp")
    experts_each, model_width, hidden_width = gate_weight.shape
    chips = owners // 2
    shifts = [(0, 0), (0, 1)] + [(dy, dc) for dc in range(2) for dy in (1, chips - 1)]
    shifts += [(2, 0), (2, 1)]
    member = lax.axis_index("expert").reshape(1)
    outgoing = pack(block_expert, member, tokens, experts_each, shifts, chips)
    weights = bring(outgoing[0], gate_weight, up_weight)
    arrived = []
    for (dy, dc), payload in zip(shifts, outgoing):
        route = [
            (y * 2 + c, ((y + dy) % chips) * 2 + (c + dc) % 2)
            for y in range(chips)
            for c in range(2)
        ]
        arrived.append(payload if dy == dc == 0 else lax.ppermute(payload, "expert", route))
    gathered = []
    pairs = [(d, d ^ SIDE) for d in range(replicas)]
    for g0, g1 in zip(EDGES, EDGES[1:]):
        rows = hidden_rows(arrived[g0:g1], *weights)
        gathered.append([rows, lax.ppermute(rows, "dp", pairs)])
    kept = experts_each // 2
    first = (lax.axis_index("dp") // SIDE % 2 * kept).reshape(1)
    partial_gram = gram(first, kept, [rows for pair in gathered[:-1] for rows in pair])
    partial_gram = gram(first, kept, gathered[-1], (partial_gram,))
    classes = [[d for d in range(replicas) if d // SIDE % 2 == p] for p in range(2)]
    pieces = lax.all_to_all(
        partial_gram, "dp", split_axis=0, concat_axis=0, axis_index_groups=classes, tiled=True
    )
    own = jnp.sum(pieces, axis=0)
    other = lax.ppermute(own, "dp", [(d + 1, d) for d in range(0, replicas, 2)])
    scale = experts_each / (tokens.shape[0] * replicas)
    top = first_panel(own, scale)
    result = rest_panels(other, top, scale)
    row_count = hidden_width // replicas
    sent = result.reshape(replicas, row_count, hidden_width)
    returned = lax.all_to_all(sent, "dp", split_axis=0, concat_axis=0, tiled=True)
    returned = returned.reshape(2, 2, 2, 2, row_count, hidden_width)[:, :, :, 0]
    returned = jnp.swapaxes(returned, 0, 1).reshape(experts_each, row_count, hidden_width)
    return returned.astype(F32)


def solution(mesh):
    placed = (
        P(("dp", "expert"), None),
        P(("dp", "expert")),
        P("expert", None, None),
        P("expert", None, None),
    )
    return jax.shard_map(
        on_device, mesh=mesh, in_specs=placed, out_specs=P("expert", "dp", None), check_vma=False
    )
```

```python
import jax
import jax.numpy as jnp
from jax import lax
from jax.experimental import pallas as pl
from jax.experimental.pallas import tpu as pltpu
from jax.sharding import PartitionSpec as P

BLOCK = 128
RIDGE = 0.05
LANE = 128
TAG = 16
SIDE = 4
VMEM_BYTES = 20 << 20
EDGES = (0, 2, 6, 8)
STRIP = 32
F32 = jnp.float32
BF16 = jnp.bfloat16
HIGH = lax.Precision.HIGHEST
TN = (((0,), (0,)), ((), ()))
HALF = 64
TIP = 320
TIP_ODD = 256


def near(x):
    return pltpu.with_memory_space_constraint(x, pltpu.VMEM)


def far(x):
    return pltpu.with_memory_space_constraint(x, pltpu.HBM)


def pack_kernel(member_ref, assign_hbm, tok_hbm, *rest, experts_each, shifts, chips):
    outs = rest[: len(shifts)]
    assign_ref, tok_ref, sem = rest[len(shifts) :]
    blocks, chunks = tok_ref.shape[0] // BLOCK, tok_ref.shape[1] // LANE
    fetch = [
        pltpu.make_async_copy(assign_hbm, assign_ref, sem.at[0]),
        pltpu.make_async_copy(tok_hbm, tok_ref, sem.at[1]),
    ]
    for copy in fetch:
        copy.start()
    for copy in fetch:
        copy.wait()
    chip = lax.div(member_ref[0], 2)
    core = lax.rem(member_ref[0], 2)
    for (dy, dc), out in zip(shifts, outs):
        dest = lax.rem(chip + dy, chips) * 2 + lax.rem(core + dc, 2)
        block = jnp.int32(0)
        code = jnp.int32(0)
        for b in range(blocks):
            expert = assign_ref[b]
            owner = lax.div(expert, experts_each)
            hit = owner == dest
            block = jnp.where(hit, b, block)
            code = jnp.where(hit, expert - owner * experts_each + 1, code)
        row = pl.multiple_of(block * BLOCK, BLOCK)
        for c in range(chunks):
            out[c * BLOCK : (c + 1) * BLOCK, :] = tok_ref[
                pl.ds(row, BLOCK), c * LANE : (c + 1) * LANE
            ]
        out[chunks * BLOCK :, :] = jnp.full((TAG, LANE), code.astype(F32), F32).astype(BF16)


def pack(assign, member, tokens, experts_each, shifts, chips):
    rows = BLOCK * tokens.shape[1] // LANE + TAG
    return pl.pallas_call(
        lambda *refs: pack_kernel(*refs, experts_each=experts_each, shifts=shifts, chips=chips),
        in_specs=[pl.BlockSpec(memory_space=pltpu.SMEM)]
        + [pl.BlockSpec(memory_space=pl.ANY)] * 2,
        out_specs=[pl.BlockSpec(memory_space=pltpu.VMEM)] * len(shifts),
        out_shape=[pltpu.VMEM((rows, LANE), BF16)] * len(shifts),
        scratch_shapes=[
            pltpu.SMEM(assign.shape, assign.dtype),
            pltpu.VMEM(tokens.shape, tokens.dtype),
            pltpu.SemaphoreType.DMA((2,)),
        ],
        compiler_params=pltpu.CompilerParams(vmem_limit_bytes=VMEM_BYTES),
        name="pack",
    )(member, far(assign), far(tokens))


def hidden_kernel(*refs, slots, model_width):
    xs = refs[:slots]
    gate_ref, up_ref, out_ref = refs[slots:]
    chunks = model_width // LANE
    codes = []
    for s in range(slots):
        tag = xs[s][chunks * BLOCK : chunks * BLOCK + TAG, :].astype(F32)
        codes.append(jnp.max(tag).astype(jnp.int32))

    width = out_ref.shape[1]
    lane = lax.broadcasted_iota(jnp.int32, (TAG, width), 1)
    tags = jnp.zeros((TAG, width), F32)
    for s in range(slots):
        tags = jnp.where(lane == s, codes[s].astype(F32), tags)
    out_ref[slots * BLOCK :, :] = tags.astype(BF16)
    for s in range(slots):

        @pl.when(codes[s] > 0)
        def _(s=s):
            expert = codes[s] - 1
            x = jnp.concatenate(
                [xs[s][c * BLOCK : (c + 1) * BLOCK, :] for c in range(chunks)], axis=1
            )
            gate = jnp.dot(x, gate_ref[expert], preferred_element_type=F32)
            up = jnp.dot(x, up_ref[expert], preferred_element_type=F32)
            hidden = gate / (1.0 + jnp.exp(-gate)) * up
            out_ref[s * BLOCK : (s + 1) * BLOCK, :] = hidden.astype(BF16)


def hidden_rows(arrived, gate_weight, up_weight):
    slots = len(arrived)
    _, model_width, hidden_width = gate_weight.shape
    return pl.pallas_call(
        lambda *refs: hidden_kernel(*refs, slots=slots, model_width=model_width),
        in_specs=[pl.BlockSpec(memory_space=pltpu.VMEM)] * (slots + 2),
        out_specs=pl.BlockSpec(memory_space=pltpu.VMEM),
        out_shape=pltpu.VMEM((slots * BLOCK + TAG, hidden_width), BF16),
        compiler_params=pltpu.CompilerParams(vmem_limit_bytes=VMEM_BYTES),
        name="hidden",
    )(*[near(x) for x in (*arrived, gate_weight, up_weight)])


def bring_kernel(_, gate_ref, up_ref, gate_out, up_out, sem):
    copies = [
        pltpu.make_async_copy(gate_ref, gate_out, sem.at[0]),
        pltpu.make_async_copy(up_ref, up_out, sem.at[1]),
    ]
    for copy in copies:
        copy.start()
    for copy in copies:
        copy.wait()


def bring(after, gate_weight, up_weight):
    return pl.pallas_call(
        bring_kernel,
        in_specs=[pl.BlockSpec(memory_space=pl.ANY)] * 3,
        out_specs=[pl.BlockSpec(memory_space=pltpu.VMEM)] * 2,
        out_shape=[pltpu.VMEM(w.shape, w.dtype) for w in (gate_weight, up_weight)],
        scratch_shapes=[pltpu.SemaphoreType.DMA((2,))],
        compiler_params=pltpu.CompilerParams(vmem_limit_bytes=VMEM_BYTES),
        name="bring",
    )(after, far(gate_weight), far(up_weight))


def fold(tile):
    row = lax.broadcasted_iota(jnp.int32, (HALF, LANE), 0)
    lane = lax.broadcasted_iota(jnp.int32, (HALF, LANE), 1)
    upper, lower = tile[:HALF, :], tile[HALF:, :]
    folded = jnp.where((lane < HALF) & (lane < row), pltpu.roll(lower, HALF, 1), upper)
    corner = jnp.sum(jnp.where(lane == row + HALF, lower, 0.0), axis=0, keepdims=True)
    return folded, corner


def unfold(folded, corner):
    row = lax.broadcasted_iota(jnp.int32, (HALF, LANE), 0)
    lane = lax.broadcasted_iota(jnp.int32, (HALF, LANE), 1)
    flipped = jnp.concatenate([folded, jnp.zeros((HALF, LANE), F32)], axis=0).T
    upper = jnp.where(lane < row, flipped[:HALF, :], folded)
    below, above = pltpu.roll(folded, HALF, 1), pltpu.roll(flipped[:HALF, :], HALF, 1)
    inner = jnp.where(lane - HALF < row, below, jnp.where(lane - HALF == row, corner, above))
    return jnp.concatenate([upper, jnp.where(lane < HALF, flipped[HALF:, :], inner)], axis=0)


def gram_kernel(first_ref, *refs, counts, kept):
    groups, out_ref = refs[: len(counts)], refs[-1]
    out_ref[...] = refs[-2][...] if len(refs) > len(counts) + 1 else jnp.zeros(out_ref.shape, F32)
    lane = lax.broadcasted_iota(jnp.int32, (TAG, LANE), 1)
    where = [(ref, s, n) for ref, n in zip(groups, counts) for s in range(n)]
    codes = []
    for ref, s, n in where:
        tag = ref[n * BLOCK : n * BLOCK + TAG, :LANE].astype(F32)
        codes.append(jnp.max(jnp.where(lane == s, tag, 0.0)).astype(jnp.int32))
    for code, (ref, s, n) in zip(codes, where):
        local = code - 1 - first_ref[0]

        @pl.when((local >= 0) & (local < kept))
        def _(ref=ref, s=s, local=local):
            hidden = ref[s * BLOCK : (s + 1) * BLOCK, :]
            even, odd = 2 * local, 2 * local + 1
            for i, (chunk, base, tip, sides) in enumerate(
                ((even, 0, TIP, (HALF, HALF + LANE)), (odd, 0, TIP_ODD, (LANE,)), (odd, HALF, TIP_ODD + 1, ()))
            ):
                part = lax.dot_general(
                    hidden[:, i * LANE : (i + 1) * LANE],
                    hidden[:, i * LANE :],
                    TN,
                    preferred_element_type=F32,
                )
                folded, corner = fold(part[:, :LANE])
                out_ref[chunk, base : base + HALF, :] += folded
                out_ref[chunk, tip : tip + 1, :] += corner
                for j, side in enumerate(sides):
                    out_ref[chunk, side : side + LANE, :] += part[:, (j + 1) * LANE : (j + 2) * LANE]


def gram(first, kept, groups, prior=()):
    counts = [(g.shape[0] - TAG) // BLOCK for g in groups]
    return pl.pallas_call(
        lambda *refs: gram_kernel(*refs, counts=counts, kept=kept),
        in_specs=[pl.BlockSpec(memory_space=pltpu.SMEM)]
        + [pl.BlockSpec(memory_space=pltpu.VMEM)] * (len(groups) + len(prior)),
        out_specs=pl.BlockSpec(memory_space=pltpu.VMEM),
        out_shape=pltpu.VMEM((2 * kept, TIP + 8, LANE), F32),
        compiler_params=pltpu.CompilerParams(vmem_limit_bytes=VMEM_BYTES),
        name="gram",
    )(first, *[near(x) for x in (*groups, *prior)])


def factor_strip(groups, lane0, sub):
    wide = lambda v: jnp.concatenate([v] * (groups[0].shape[1] // LANE), axis=1)
    groups = list(groups)
    wide_sub = wide(sub)
    for b in range(len(groups)):
        base = lane0 + 8 * b
        cols = [
            [jnp.broadcast_to(g[:, base + j : base + j + 1], (8, LANE)) for g in groups[b:]]
            for j in range(8)
        ]
        for k in range(8):
            inv = lax.rsqrt(cols[k][0][k : k + 1, :])
            row = groups[b][k : k + 1, :] * wide(inv)
            mult = [c * inv for c in cols[k]]
            mult[0] = jnp.where(sub > k, mult[0], 0.0)
            for g, m in enumerate(mult):
                groups[b + g] = groups[b + g] - wide(m) * row
            groups[b] = jnp.where(wide_sub == k, row, groups[b])
            for j in range(k + 1, 8):
                top = cols[j][0][k : k + 1, :] * inv
                cols[j] = [c - m * top for c, m in zip(cols[j], mult)]
    return groups


def dot_high(a, b, dims):
    return lax.dot_general(a, b, dims, precision=HIGH, preferred_element_type=F32)


def factor_panel(work):
    sub = lax.broadcasted_iota(jnp.int32, (8, LANE), 0)
    lane = lax.broadcasted_iota(jnp.int32, (8, LANE), 1)
    width = work.shape[1]
    for r0 in range(0, LANE, STRIP):
        r1 = r0 + STRIP
        groups = factor_strip([work[r : r + 8, :] for r in range(r0, r1, 8)], r0, sub)
        diag = jnp.concatenate(
            [
                jnp.where(lane >= r0 + 8 * g + sub, rows[:, :LANE], 0.0)
                for g, rows in enumerate(groups)
            ],
            axis=0,
        )
        strip = diag
        if width > LANE:
            right = jnp.concatenate([rows[:, LANE:] for rows in groups], axis=0)
            strip = jnp.concatenate([diag, right], axis=1)
        work[r0:r1, :] = strip
        if r1 < LANE:
            work[r1:, :] = work[r1:, :] - dot_high(diag.T[r1:, :], strip, (((1,), (0,)), ((), ())))


def diagonal(ref, base, tip, scale):
    tile = unfold(ref[base : base + HALF, :] * scale, ref[tip : tip + 1, :] * scale)
    eye = lax.broadcasted_iota(jnp.int32, tile.shape, 0) == lax.broadcasted_iota(
        jnp.int32, tile.shape, 1
    )
    return tile + jnp.where(eye, RIDGE, 0.0)


def first_kernel(part_ref, out_ref, *, scale):
    out_ref[:, :LANE] = diagonal(part_ref, 0, TIP, scale)
    for t in range(2):
        side = part_ref[HALF + t * LANE : HALF + (t + 1) * LANE, :]
        out_ref[:, (t + 1) * LANE : (t + 2) * LANE] = side * scale
    factor_panel(out_ref)


def first_panel(part, width, scale):
    return pl.pallas_call(
        lambda *refs: first_kernel(*refs, scale=scale),
        out_shape=pltpu.VMEM((LANE, width), F32),
        compiler_params=pltpu.CompilerParams(vmem_limit_bytes=VMEM_BYTES),
        name="first_panel",
    )(near(part))


def rest_kernel(part_ref, top_ref, out_ref, mid, low, *, scale):
    top = top_ref[...]
    mid[:, :LANE] = diagonal(part_ref, 0, TIP_ODD, scale)
    mid[:, LANE:] = part_ref[LANE : 2 * LANE, :] * scale
    mid[...] = mid[...] - dot_high(top[:, LANE : 2 * LANE], top[:, LANE:], TN)
    low[...] = diagonal(part_ref, HALF, TIP_ODD + 1, scale) - dot_high(
        top[:, 2 * LANE :], top[:, 2 * LANE :], TN
    )
    factor_panel(mid)
    right = mid[:, LANE:]
    low[...] = low[...] - dot_high(right, right, TN)
    factor_panel(low)
    kind = out_ref.dtype
    out_ref[:LANE, :] = top.astype(kind)
    out_ref[LANE : 2 * LANE, :LANE] = jnp.zeros((LANE, LANE), kind)
    out_ref[LANE : 2 * LANE, LANE:] = mid[...].astype(kind)
    out_ref[2 * LANE :, : 2 * LANE] = jnp.zeros((LANE, 2 * LANE), kind)
    out_ref[2 * LANE :, 2 * LANE :] = low[...].astype(kind)


def rest_panels(part, top, scale):
    width = top.shape[1]
    return pl.pallas_call(
        lambda *refs: rest_kernel(*refs, scale=scale),
        out_shape=pltpu.VMEM((width, width), BF16),
        scratch_shapes=[pltpu.VMEM((LANE, 2 * LANE), F32), pltpu.VMEM((LANE, LANE), F32)],
        compiler_params=pltpu.CompilerParams(vmem_limit_bytes=VMEM_BYTES),
        name="rest_panels",
    )(near(part), near(top))


def on_device(tokens, block_expert, gate_weight, up_weight):
    owners = lax.axis_size("expert")
    replicas = lax.axis_size("dp")
    experts_each, model_width, hidden_width = gate_weight.shape
    chips = owners // 2
    shifts = [(0, 0), (0, 1)] + [(dy, dc) for dc in range(2) for dy in (1, chips - 1)]
    shifts += [(2, 0), (2, 1)]
    member = lax.axis_index("expert").reshape(1)
    outgoing = pack(block_expert, member, tokens, experts_each, shifts, chips)
    weights = bring(outgoing[0], gate_weight, up_weight)
    pairs = [(d, d ^ SIDE) for d in range(replicas)]
    arrived, gathered = [], []

    def swap_rows(g):
        blocks = arrived[EDGES[g] : EDGES[g + 1]]
        if g == 1:
            blocks[0], gathered[0][1] = lax.optimization_barrier((blocks[0], gathered[0][1]))
        rows = hidden_rows(blocks, *weights)
        gathered.append([rows, lax.ppermute(rows, "dp", pairs)])

    for (dy, dc), payload in zip(shifts, outgoing):
        route = [
            (y * 2 + c, ((y + dy) % chips) * 2 + (c + dc) % 2)
            for y in range(chips)
            for c in range(2)
        ]
        if len(arrived) == EDGES[-2]:
            swap_rows(0)
        if len(arrived) >= EDGES[-2]:
            payload, _ = lax.optimization_barrier((payload, gathered[0][0]))
        arrived.append(payload if dy == dc == 0 else lax.ppermute(payload, "expert", route))
    for g in range(1, len(EDGES) - 1):
        swap_rows(g)
    kept = experts_each // 2
    first = (lax.axis_index("dp") // SIDE % 2 * kept).reshape(1)
    partial_gram = gram(first, kept, [rows for pair in gathered[:-1] for rows in pair])
    partial_gram = gram(first, kept, gathered[-1], (partial_gram,))
    classes = [[d for d in range(replicas) if d // SIDE % 2 == p] for p in range(2)]
    pieces = lax.all_to_all(
        partial_gram, "dp", split_axis=0, concat_axis=0, axis_index_groups=classes, tiled=True
    )
    own = jnp.sum(pieces, axis=0)
    other = lax.ppermute(own[: TIP_ODD + 8], "dp", [(d + 1, d) for d in range(0, replicas, 2)])
    scale = experts_each / (tokens.shape[0] * replicas)
    top = first_panel(own, hidden_width, scale)
    result = rest_panels(other, top, scale)
    row_count = hidden_width // replicas
    sent = result.reshape(replicas, row_count, hidden_width)
    returned = lax.all_to_all(sent, "dp", split_axis=0, concat_axis=0, tiled=True)
    returned = returned.reshape(2, 2, 2, 2, row_count, hidden_width)[:, :, :, 0]
    returned = jnp.swapaxes(returned, 0, 1).reshape(experts_each, row_count, hidden_width)
    return returned.astype(F32)


def solution(mesh):
    placed = (
        P(("dp", "expert"), None),
        P(("dp", "expert")),
        P("expert", None, None),
        P("expert", None, None),
    )
    return jax.shard_map(
        on_device, mesh=mesh, in_specs=placed, out_specs=P("expert", "dp", None), check_vma=False
    )
```

```python
import jax
import jax.numpy as jnp
from jax import lax
from jax.experimental import pallas as pl
from jax.experimental.pallas import tpu as pltpu
from jax.sharding import PartitionSpec as P


BLOCK = 128
RIDGE = 0.05
LANE = 128
TAG = 16
SIDE = 4
VMEM_BYTES = 20 << 20
EDGES = (0, 2, 6, 7, 8)
STRIP = 64
F32 = jnp.float32
BF16 = jnp.bfloat16
HIGH = lax.Precision.HIGHEST
TN = (((0,), (0,)), ((), ()))
HALF = 64
TIP = 320
TIP_ODD = 256


def near(x):
    return pltpu.with_memory_space_constraint(x, pltpu.VMEM)


def far(x):
    return pltpu.with_memory_space_constraint(x, pltpu.HBM)


def pack_kernel(member_ref, assign_hbm, tok_hbm, *rest, experts_each, shifts, chips):
    outs = rest[: len(shifts)]
    assign_ref, tok_ref, sem = rest[len(shifts) :]
    blocks, chunks = tok_ref.shape[0] // BLOCK, tok_ref.shape[1] // LANE
    fetch = [
        pltpu.make_async_copy(assign_hbm, assign_ref, sem.at[0]),
        pltpu.make_async_copy(tok_hbm, tok_ref, sem.at[1]),
    ]
    for copy in fetch:
        copy.start()
    for copy in fetch:
        copy.wait()
    chip = lax.div(member_ref[0], 2)
    core = lax.rem(member_ref[0], 2)
    for (dy, dc), out in zip(shifts, outs):
        dest = lax.rem(chip + dy, chips) * 2 + lax.rem(core + dc, 2)
        block = jnp.int32(0)
        code = jnp.int32(0)
        for b in range(blocks):
            expert = assign_ref[b]
            owner = lax.div(expert, experts_each)
            hit = owner == dest
            block = jnp.where(hit, b, block)
            code = jnp.where(hit, expert - owner * experts_each + 1, code)
        row = pl.multiple_of(block * BLOCK, BLOCK)
        for c in range(chunks):
            out[c * BLOCK : (c + 1) * BLOCK, :] = tok_ref[
                pl.ds(row, BLOCK), c * LANE : (c + 1) * LANE
            ]
        out[chunks * BLOCK :, :] = jnp.full((TAG, LANE), code.astype(F32), F32).astype(BF16)


def pack(assign, member, tokens, experts_each, shifts, chips):
    rows = BLOCK * tokens.shape[1] // LANE + TAG
    return pl.pallas_call(
        lambda *refs: pack_kernel(*refs, experts_each=experts_each, shifts=shifts, chips=chips),
        in_specs=[pl.BlockSpec(memory_space=pltpu.SMEM)]
        + [pl.BlockSpec(memory_space=pl.ANY)] * 2,
        out_specs=[pl.BlockSpec(memory_space=pltpu.VMEM)] * len(shifts),
        out_shape=[pltpu.VMEM((rows, LANE), BF16)] * len(shifts),
        scratch_shapes=[
            pltpu.SMEM(assign.shape, assign.dtype),
            pltpu.VMEM(tokens.shape, tokens.dtype),
            pltpu.SemaphoreType.DMA((2,)),
        ],
        compiler_params=pltpu.CompilerParams(vmem_limit_bytes=VMEM_BYTES),
        name="pack",
    )(member, far(assign), far(tokens))


def hidden_kernel(*refs, slots, model_width):
    xs = refs[:slots]
    gate_ref, up_ref, out_ref = refs[slots:]
    chunks = model_width // LANE
    codes = []
    for s in range(slots):
        tag = xs[s][chunks * BLOCK : chunks * BLOCK + TAG, :].astype(F32)
        codes.append(jnp.max(tag).astype(jnp.int32))

    width = out_ref.shape[1]
    lane = lax.broadcasted_iota(jnp.int32, (TAG, width), 1)
    tags = jnp.zeros((TAG, width), F32)
    for s in range(slots):
        tags = jnp.where(lane == s, codes[s].astype(F32), tags)
    out_ref[slots * BLOCK :, :] = tags.astype(BF16)
    for s in range(slots):

        @pl.when(codes[s] > 0)
        def _(s=s):
            expert = codes[s] - 1
            x = jnp.concatenate(
                [xs[s][c * BLOCK : (c + 1) * BLOCK, :] for c in range(chunks)], axis=1
            )
            gate = jnp.dot(x, gate_ref[expert], preferred_element_type=F32)
            up = jnp.dot(x, up_ref[expert], preferred_element_type=F32)
            hidden = gate / (1.0 + jnp.exp(-gate)) * up
            out_ref[s * BLOCK : (s + 1) * BLOCK, :] = hidden.astype(BF16)


def hidden_rows(arrived, gate_weight, up_weight):
    slots = len(arrived)
    _, model_width, hidden_width = gate_weight.shape
    return pl.pallas_call(
        lambda *refs: hidden_kernel(*refs, slots=slots, model_width=model_width),
        in_specs=[pl.BlockSpec(memory_space=pltpu.VMEM)] * (slots + 2),
        out_specs=pl.BlockSpec(memory_space=pltpu.VMEM),
        out_shape=pltpu.VMEM((slots * BLOCK + TAG, hidden_width), BF16),
        compiler_params=pltpu.CompilerParams(vmem_limit_bytes=VMEM_BYTES),
        name="hidden",
    )(*[near(x) for x in (*arrived, gate_weight, up_weight)])


def bring_kernel(_, gate_ref, up_ref, gate_out, up_out, sem):
    copies = [
        pltpu.make_async_copy(gate_ref, gate_out, sem.at[0]),
        pltpu.make_async_copy(up_ref, up_out, sem.at[1]),
    ]
    for copy in copies:
        copy.start()
    for copy in copies:
        copy.wait()


def bring(after, gate_weight, up_weight):
    return pl.pallas_call(
        bring_kernel,
        in_specs=[pl.BlockSpec(memory_space=pl.ANY)] * 3,
        out_specs=[pl.BlockSpec(memory_space=pltpu.VMEM)] * 2,
        out_shape=[pltpu.VMEM(w.shape, w.dtype) for w in (gate_weight, up_weight)],
        scratch_shapes=[pltpu.SemaphoreType.DMA((2,))],
        compiler_params=pltpu.CompilerParams(vmem_limit_bytes=VMEM_BYTES),
        name="bring",
    )(after, far(gate_weight), far(up_weight))


def fold(tile):
    row = lax.broadcasted_iota(jnp.int32, (HALF, LANE), 0)
    lane = lax.broadcasted_iota(jnp.int32, (HALF, LANE), 1)
    upper, lower = tile[:HALF, :], tile[HALF:, :]
    folded = jnp.where((lane < HALF) & (lane < row), pltpu.roll(lower, HALF, 1), upper)
    corner = jnp.sum(jnp.where(lane == row + HALF, lower, 0.0), axis=0, keepdims=True)
    return folded, corner


def unfold(folded, corner):
    row = lax.broadcasted_iota(jnp.int32, (HALF, LANE), 0)
    lane = lax.broadcasted_iota(jnp.int32, (HALF, LANE), 1)
    flipped = jnp.concatenate([folded, jnp.zeros((HALF, LANE), F32)], axis=0).T
    upper = jnp.where(lane < row, flipped[:HALF, :], folded)
    below, above = pltpu.roll(folded, HALF, 1), pltpu.roll(flipped[:HALF, :], HALF, 1)
    inner = jnp.where(lane - HALF < row, below, jnp.where(lane - HALF == row, corner, above))
    return jnp.concatenate([upper, jnp.where(lane < HALF, flipped[HALF:, :], inner)], axis=0)


def gram_kernel(first_ref, *refs, counts, kept):
    groups, out_ref = refs[: len(counts)], refs[-1]
    out_ref[...] = refs[-2][...] if len(refs) > len(counts) + 1 else jnp.zeros(out_ref.shape, F32)
    lane = lax.broadcasted_iota(jnp.int32, (TAG, LANE), 1)
    where = [(ref, s, n) for ref, n in zip(groups, counts) for s in range(n)]
    codes = []
    for ref, s, n in where:
        tag = ref[n * BLOCK : n * BLOCK + TAG, :LANE].astype(F32)
        codes.append(jnp.max(jnp.where(lane == s, tag, 0.0)).astype(jnp.int32))
    for code, (ref, s, n) in zip(codes, where):
        local = code - 1 - first_ref[0]

        @pl.when((local >= 0) & (local < kept))
        def _(ref=ref, s=s, local=local):
            hidden = ref[s * BLOCK : (s + 1) * BLOCK, :]
            even, odd = 2 * local, 2 * local + 1
            for i, (chunk, base, tip, sides) in enumerate(
                ((even, 0, TIP, (HALF, HALF + LANE)), (odd, 0, TIP_ODD, (LANE,)), (odd, HALF, TIP_ODD + 1, ()))
            ):
                part = lax.dot_general(
                    hidden[:, i * LANE : (i + 1) * LANE],
                    hidden[:, i * LANE :],
                    TN,
                    preferred_element_type=F32,
                )
                folded, corner = fold(part[:, :LANE])
                out_ref[chunk, base : base + HALF, :] += folded
                out_ref[chunk, tip : tip + 1, :] += corner
                for j, side in enumerate(sides):
                    out_ref[chunk, side : side + LANE, :] += part[:, (j + 1) * LANE : (j + 2) * LANE]


def gram(first, kept, groups, prior=()):
    counts = [(g.shape[0] - TAG) // BLOCK for g in groups]
    return pl.pallas_call(
        lambda *refs: gram_kernel(*refs, counts=counts, kept=kept),
        in_specs=[pl.BlockSpec(memory_space=pltpu.SMEM)]
        + [pl.BlockSpec(memory_space=pltpu.VMEM)] * (len(groups) + len(prior)),
        out_specs=pl.BlockSpec(memory_space=pltpu.VMEM),
        out_shape=pltpu.VMEM((2 * kept, TIP + 8, LANE), F32),
        compiler_params=pltpu.CompilerParams(vmem_limit_bytes=VMEM_BYTES),
        name="gram",
    )(first, *[near(x) for x in (*groups, *prior)])


def factor_strip(groups, lane0, sub):
    wide = lambda v: jnp.concatenate([v] * (groups[0].shape[1] // LANE), axis=1)
    groups = list(groups)
    wide_sub = wide(sub)
    for b in range(len(groups)):
        base = lane0 + 8 * b
        cols = [
            [jnp.broadcast_to(g[:, base + j : base + j + 1], (8, LANE)) for g in groups[b:]]
            for j in range(8)
        ]
        for k in range(8):
            inv = lax.rsqrt(cols[k][0][k : k + 1, :])
            row = groups[b][k : k + 1, :] * wide(inv)
            mult = [jnp.where(sub > k, cols[k][0], 0.0)] + cols[k][1:]
            mult = [c * inv for c in mult]
            for g, m in enumerate(mult):
                groups[b + g] = groups[b + g] - wide(m) * row
            groups[b] = jnp.where(wide_sub == k, row, groups[b])
            for j in range(k + 1, 8):
                top = cols[j][0][k : k + 1, :] * inv
                cols[j] = [c - m * top for c, m in zip(cols[j], mult)]
    return groups


def dot_high(a, b, dims):
    return lax.dot_general(a, b, dims, precision=HIGH, preferred_element_type=F32)


def factor_panel(work):
    sub = lax.broadcasted_iota(jnp.int32, (8, LANE), 0)
    lane = lax.broadcasted_iota(jnp.int32, (8, LANE), 1)
    width = work.shape[1]
    for r0 in range(0, LANE, STRIP):
        r1 = r0 + STRIP
        groups = factor_strip([work[r : r + 8, :] for r in range(r0, r1, 8)], r0, sub)
        diag = jnp.concatenate(
            [
                jnp.where(lane >= r0 + 8 * g + sub, rows[:, :LANE], 0.0)
                for g, rows in enumerate(groups)
            ],
            axis=0,
        )
        strip = diag
        if width > LANE:
            right = jnp.concatenate([rows[:, LANE:] for rows in groups], axis=0)
            strip = jnp.concatenate([diag, right], axis=1)
        work[r0:r1, :] = strip
        if r1 < LANE:
            work[r1:, :] = work[r1:, :] - dot_high(diag.T[r1:, :], strip, (((1,), (0,)), ((), ())))


def diagonal(ref, base, tip, scale):
    tile = unfold(ref[base : base + HALF, :] * scale, ref[tip : tip + 1, :] * scale)
    eye = lax.broadcasted_iota(jnp.int32, tile.shape, 0) == lax.broadcasted_iota(
        jnp.int32, tile.shape, 1
    )
    return tile + jnp.where(eye, RIDGE, 0.0)


def first_kernel(part_ref, out_ref, *, scale):
    out_ref[:, :LANE] = diagonal(part_ref, 0, TIP, scale)
    for t in range(2):
        side = part_ref[HALF + t * LANE : HALF + (t + 1) * LANE, :]
        out_ref[:, (t + 1) * LANE : (t + 2) * LANE] = side * scale
    factor_panel(out_ref)


def first_panel(part, width, scale):
    return pl.pallas_call(
        lambda *refs: first_kernel(*refs, scale=scale),
        out_shape=pltpu.VMEM((LANE, width), F32),
        compiler_params=pltpu.CompilerParams(vmem_limit_bytes=VMEM_BYTES),
        name="first_panel",
    )(near(part))


def rest_kernel(part_ref, top_ref, out_ref, mid, low, *, scale):
    top = top_ref[...]
    mid[:, :LANE] = diagonal(part_ref, 0, TIP_ODD, scale)
    mid[:, LANE:] = part_ref[LANE : 2 * LANE, :] * scale
    mid[...] = mid[...] - dot_high(top[:, LANE : 2 * LANE], top[:, LANE:], TN)
    low[...] = diagonal(part_ref, HALF, TIP_ODD + 1, scale) - dot_high(
        top[:, 2 * LANE :], top[:, 2 * LANE :], TN
    )
    factor_panel(mid)
    right = mid[:, LANE:]
    low[...] = low[...] - dot_high(right, right, TN)
    factor_panel(low)
    kind = out_ref.dtype
    out_ref[:LANE, :] = top.astype(kind)
    out_ref[LANE : 2 * LANE, :LANE] = jnp.zeros((LANE, LANE), kind)
    out_ref[LANE : 2 * LANE, LANE:] = mid[...].astype(kind)
    out_ref[2 * LANE :, : 2 * LANE] = jnp.zeros((LANE, 2 * LANE), kind)
    out_ref[2 * LANE :, 2 * LANE :] = low[...].astype(kind)


def rest_panels(part, top, scale):
    width = top.shape[1]
    return pl.pallas_call(
        lambda *refs: rest_kernel(*refs, scale=scale),
        out_shape=pltpu.VMEM((width, width), BF16),
        scratch_shapes=[pltpu.VMEM((LANE, 2 * LANE), F32), pltpu.VMEM((LANE, LANE), F32)],
        compiler_params=pltpu.CompilerParams(vmem_limit_bytes=VMEM_BYTES),
        name="rest_panels",
    )(near(part), near(top))


def on_device(tokens, block_expert, gate_weight, up_weight):
    owners = lax.axis_size("expert")
    replicas = lax.axis_size("dp")
    experts_each, _, hidden_width = gate_weight.shape
    chips = owners // 2
    shifts = [(0, 0), (0, 1)] + [(dy, dc) for dc in range(2) for dy in (1, chips - 1)]
    shifts += [(2, 0), (2, 1)]
    member = lax.axis_index("expert").reshape(1)
    outgoing = pack(block_expert, member, tokens, experts_each, shifts, chips)
    pairs = [(d, d ^ SIDE) for d in range(replicas)]
    arrived, gathered = [], []
    for (dy, dc), payload in zip(shifts, outgoing):
        route = [
            (y * 2 + c, ((y + dy) % chips) * 2 + (c + dc) % 2)
            for y in range(chips)
            for c in range(2)
        ]
        if dy == 2:
            payload, arrived[1] = lax.optimization_barrier((payload, arrived[1]))
        arrived.append(payload if dy == dc == 0 else lax.ppermute(payload, "expert", route))
    weights = bring(arrived[1], gate_weight, up_weight)
    for g, (lo, hi) in enumerate(zip(EDGES, EDGES[1:])):
        blocks = arrived[lo:hi]
        if g == 1:
            blocks[0], gathered[0][1] = lax.optimization_barrier((blocks[0], gathered[0][1]))
        rows = hidden_rows(blocks, *weights)
        gathered.append([rows, lax.ppermute(rows, "dp", pairs)])
    kept = experts_each // 2
    first = (lax.axis_index("dp") // SIDE % 2 * kept).reshape(1)
    partial_gram = gram(first, kept, [rows for pair in gathered[:-1] for rows in pair])
    partial_gram = gram(first, kept, gathered[-1], (partial_gram,))
    classes = [[d for d in range(replicas) if d // SIDE % 2 == p] for p in range(2)]
    pieces = lax.all_to_all(
        partial_gram, "dp", split_axis=0, concat_axis=0, axis_index_groups=classes, tiled=True
    )
    own = jnp.sum(pieces, axis=0)
    other = lax.ppermute(own[: TIP_ODD + 8], "dp", [(d + 1, d) for d in range(0, replicas, 2)])
    scale = experts_each / (tokens.shape[0] * replicas)
    top = first_panel(own, hidden_width, scale)
    result = rest_panels(other, top, scale)
    row_count = hidden_width // replicas
    sent = result.reshape(replicas, row_count, hidden_width)
    returned = lax.all_to_all(sent, "dp", split_axis=0, concat_axis=0, tiled=True)
    returned = returned.reshape(2, 2, 2, 2, row_count, hidden_width)[:, :, :, 0]
    returned = jnp.swapaxes(returned, 0, 1).reshape(experts_each, row_count, hidden_width)
    return returned.astype(F32)


def solution(mesh):
    placed = (
        P(("dp", "expert"), None),
        P(("dp", "expert")),
        P("expert", None, None),
        P("expert", None, None),
    )

    return jax.shard_map(
        on_device, mesh=mesh, in_specs=placed, out_specs=P("expert", "dp", None), check_vma=False
    )
```

```python
import jax
import jax.numpy as jnp
from jax import lax
from jax.experimental import pallas as pl
from jax.experimental.pallas import tpu as pltpu
from jax.sharding import PartitionSpec as P


BLOCK = 128
RIDGE = 0.05
LANE = 128
TAG = 16
SIDE = 4
VMEM_BYTES = 20 << 20
EDGES = (0, 2, 4, 6, 7, 8)
STRIP = 64
F32 = jnp.float32
BF16 = jnp.bfloat16
HIGH = lax.Precision.HIGHEST
TN = (((0,), (0,)), ((), ()))
HALF = 64
TIP = 320
TIP_ODD = 256


def near(x):
    return pltpu.with_memory_space_constraint(x, pltpu.VMEM)


def far(x):
    return pltpu.with_memory_space_constraint(x, pltpu.HBM)


def pack_kernel(member_ref, assign_hbm, tok_hbm, *rest, experts_each, shifts, chips):
    outs = rest[: len(shifts)]
    assign_ref, tok_ref, sem = rest[len(shifts) :]
    blocks, chunks = tok_ref.shape[0] // BLOCK, tok_ref.shape[1] // LANE
    fetch = [
        pltpu.make_async_copy(assign_hbm, assign_ref, sem.at[0]),
        pltpu.make_async_copy(tok_hbm, tok_ref, sem.at[1]),
    ]
    for copy in fetch:
        copy.start()
    for copy in fetch:
        copy.wait()
    chip = lax.div(member_ref[0], 2)
    core = lax.rem(member_ref[0], 2)
    for (dy, dc), out in zip(shifts, outs):
        dest = lax.rem(chip + dy, chips) * 2 + lax.rem(core + dc, 2)
        block = jnp.int32(0)
        code = jnp.int32(0)
        for b in range(blocks):
            expert = assign_ref[b]
            owner = lax.div(expert, experts_each)
            hit = owner == dest
            block = jnp.where(hit, b, block)
            code = jnp.where(hit, expert - owner * experts_each + 1, code)
        row = pl.multiple_of(block * BLOCK, BLOCK)
        for c in range(chunks):
            out[c * BLOCK : (c + 1) * BLOCK, :] = tok_ref[
                pl.ds(row, BLOCK), c * LANE : (c + 1) * LANE
            ]
        out[chunks * BLOCK :, :] = jnp.full((TAG, LANE), code.astype(F32), F32).astype(BF16)


def pack(assign, member, tokens, experts_each, shifts, chips):
    rows = BLOCK * tokens.shape[1] // LANE + TAG
    return pl.pallas_call(
        lambda *refs: pack_kernel(*refs, experts_each=experts_each, shifts=shifts, chips=chips),
        in_specs=[pl.BlockSpec(memory_space=pltpu.SMEM)]
        + [pl.BlockSpec(memory_space=pl.ANY)] * 2,
        out_specs=[pl.BlockSpec(memory_space=pltpu.VMEM)] * len(shifts),
        out_shape=[pltpu.VMEM((rows, LANE), BF16)] * len(shifts),
        scratch_shapes=[
            pltpu.SMEM(assign.shape, assign.dtype),
            pltpu.VMEM(tokens.shape, tokens.dtype),
            pltpu.SemaphoreType.DMA((2,)),
        ],
        compiler_params=pltpu.CompilerParams(vmem_limit_bytes=VMEM_BYTES),
        name="pack",
    )(member, far(assign), far(tokens))


def hidden_kernel(*refs, slots, model_width):
    xs = refs[:slots]
    gate_ref, up_ref, out_ref = refs[slots:]
    chunks = model_width // LANE
    codes = []
    for s in range(slots):
        tag = xs[s][chunks * BLOCK : chunks * BLOCK + TAG, :].astype(F32)
        codes.append(jnp.max(tag).astype(jnp.int32))

    width = out_ref.shape[1]
    lane = lax.broadcasted_iota(jnp.int32, (TAG, width), 1)
    tags = jnp.zeros((TAG, width), F32)
    for s in range(slots):
        tags = jnp.where(lane == s, codes[s].astype(F32), tags)
    out_ref[slots * BLOCK :, :] = tags.astype(BF16)
    for s in range(slots):

        @pl.when(codes[s] > 0)
        def _(s=s):
            expert = codes[s] - 1
            x = jnp.concatenate(
                [xs[s][c * BLOCK : (c + 1) * BLOCK, :] for c in range(chunks)], axis=1
            )
            gate = jnp.dot(x, gate_ref[expert], preferred_element_type=F32)
            up = jnp.dot(x, up_ref[expert], preferred_element_type=F32)
            hidden = gate / (1.0 + jnp.exp(-gate)) * up
            out_ref[s * BLOCK : (s + 1) * BLOCK, :] = hidden.astype(BF16)


def hidden_rows(arrived, gate_weight, up_weight):
    slots = len(arrived)
    _, model_width, hidden_width = gate_weight.shape
    return pl.pallas_call(
        lambda *refs: hidden_kernel(*refs, slots=slots, model_width=model_width),
        in_specs=[pl.BlockSpec(memory_space=pltpu.VMEM)] * (slots + 2),
        out_specs=pl.BlockSpec(memory_space=pltpu.VMEM),
        out_shape=pltpu.VMEM((slots * BLOCK + TAG, hidden_width), BF16),
        compiler_params=pltpu.CompilerParams(vmem_limit_bytes=VMEM_BYTES),
        name="hidden",
    )(*[near(x) for x in (*arrived, gate_weight, up_weight)])


def bring_kernel(_, gate_ref, up_ref, gate_out, up_out, sem):
    copies = [
        pltpu.make_async_copy(gate_ref, gate_out, sem.at[0]),
        pltpu.make_async_copy(up_ref, up_out, sem.at[1]),
    ]
    for copy in copies:
        copy.start()
    for copy in copies:
        copy.wait()


def bring(after, gate_weight, up_weight):
    return pl.pallas_call(
        bring_kernel,
        in_specs=[pl.BlockSpec(memory_space=pl.ANY)] * 3,
        out_specs=[pl.BlockSpec(memory_space=pltpu.VMEM)] * 2,
        out_shape=[pltpu.VMEM(w.shape, w.dtype) for w in (gate_weight, up_weight)],
        scratch_shapes=[pltpu.SemaphoreType.DMA((2,))],
        compiler_params=pltpu.CompilerParams(vmem_limit_bytes=VMEM_BYTES),
        name="bring",
    )(after, far(gate_weight), far(up_weight))


def fold(tile):
    row = lax.broadcasted_iota(jnp.int32, (HALF, LANE), 0)
    lane = lax.broadcasted_iota(jnp.int32, (HALF, LANE), 1)
    upper, lower = tile[:HALF, :], tile[HALF:, :]
    folded = jnp.where((lane < HALF) & (lane < row), pltpu.roll(lower, HALF, 1), upper)
    corner = jnp.sum(jnp.where(lane == row + HALF, lower, 0.0), axis=0, keepdims=True)
    return folded, corner


def unfold(folded, corner):
    row = lax.broadcasted_iota(jnp.int32, (HALF, LANE), 0)
    lane = lax.broadcasted_iota(jnp.int32, (HALF, LANE), 1)
    flipped = jnp.concatenate([folded, jnp.zeros((HALF, LANE), F32)], axis=0).T
    upper = jnp.where(lane < row, flipped[:HALF, :], folded)
    below, above = pltpu.roll(folded, HALF, 1), pltpu.roll(flipped[:HALF, :], HALF, 1)
    inner = jnp.where(lane - HALF < row, below, jnp.where(lane - HALF == row, corner, above))
    return jnp.concatenate([upper, jnp.where(lane < HALF, flipped[HALF:, :], inner)], axis=0)


def gram_kernel(first_ref, *refs, counts, kept):
    groups, out_ref = refs[: len(counts)], refs[-1]
    out_ref[...] = refs[-2][...] if len(refs) > len(counts) + 1 else jnp.zeros(out_ref.shape, F32)
    lane = lax.broadcasted_iota(jnp.int32, (TAG, LANE), 1)
    where = [(ref, s, n) for ref, n in zip(groups, counts) for s in range(n)]
    codes = []
    for ref, s, n in where:
        tag = ref[n * BLOCK : n * BLOCK + TAG, :LANE].astype(F32)
        codes.append(jnp.max(jnp.where(lane == s, tag, 0.0)).astype(jnp.int32))
    for code, (ref, s, n) in zip(codes, where):
        local = code - 1 - first_ref[0]

        @pl.when((local >= 0) & (local < kept))
        def _(ref=ref, s=s, local=local):
            hidden = ref[s * BLOCK : (s + 1) * BLOCK, :]
            even, odd = 2 * local, 2 * local + 1
            for i, (chunk, base, tip, sides) in enumerate(
                ((even, 0, TIP, (HALF, HALF + LANE)), (odd, 0, TIP_ODD, (LANE,)), (odd, HALF, TIP_ODD + 1, ()))
            ):
                part = lax.dot_general(
                    hidden[:, i * LANE : (i + 1) * LANE],
                    hidden[:, i * LANE :],
                    TN,
                    preferred_element_type=F32,
                )
                folded, corner = fold(part[:, :LANE])
                out_ref[chunk, base : base + HALF, :] += folded
                out_ref[chunk, tip : tip + 1, :] += corner
                for j, side in enumerate(sides):
                    out_ref[chunk, side : side + LANE, :] += part[:, (j + 1) * LANE : (j + 2) * LANE]


def gram(first, kept, groups, prior=()):
    counts = [(g.shape[0] - TAG) // BLOCK for g in groups]
    return pl.pallas_call(
        lambda *refs: gram_kernel(*refs, counts=counts, kept=kept),
        in_specs=[pl.BlockSpec(memory_space=pltpu.SMEM)]
        + [pl.BlockSpec(memory_space=pltpu.VMEM)] * (len(groups) + len(prior)),
        out_specs=pl.BlockSpec(memory_space=pltpu.VMEM),
        out_shape=pltpu.VMEM((2 * kept, TIP + 8, LANE), F32),
        compiler_params=pltpu.CompilerParams(vmem_limit_bytes=VMEM_BYTES),
        name="gram",
    )(first, *[near(x) for x in (*groups, *prior)])


def factor_strip(groups, lane0, sub):
    wide = lambda v: jnp.concatenate([v] * (groups[0].shape[1] // LANE), axis=1)
    groups = list(groups)
    wide_sub = wide(sub)
    for b in range(len(groups)):
        base = lane0 + 8 * b
        cols = [
            [jnp.broadcast_to(g[:, base + j : base + j + 1], (8, LANE)) for g in groups[b:]]
            for j in range(8)
        ]
        for k in range(8):
            inv = lax.rsqrt(cols[k][0][k : k + 1, :])
            row = groups[b][k : k + 1, :] * wide(inv)
            mult = [jnp.where(sub > k, cols[k][0], 0.0)] + cols[k][1:]
            mult = [c * inv for c in mult]
            for g, m in enumerate(mult):
                groups[b + g] = groups[b + g] - wide(m) * row
            groups[b] = jnp.where(wide_sub == k, row, groups[b])
            for j in range(k + 1, 8):
                top = cols[j][0][k : k + 1, :] * inv
                cols[j] = [c - m * top for c, m in zip(cols[j], mult)]
    return groups


def dot_high(a, b, dims):
    return lax.dot_general(a, b, dims, precision=HIGH, preferred_element_type=F32)


def factor_panel(work):
    sub = lax.broadcasted_iota(jnp.int32, (8, LANE), 0)
    lane = lax.broadcasted_iota(jnp.int32, (8, LANE), 1)
    width = work.shape[1]
    for r0 in range(0, LANE, STRIP):
        r1 = r0 + STRIP
        groups = factor_strip([work[r : r + 8, :] for r in range(r0, r1, 8)], r0, sub)
        diag = jnp.concatenate(
            [
                jnp.where(lane >= r0 + 8 * g + sub, rows[:, :LANE], 0.0)
                for g, rows in enumerate(groups)
            ],
            axis=0,
        )
        strip = diag
        if width > LANE:
            right = jnp.concatenate([rows[:, LANE:] for rows in groups], axis=0)
            strip = jnp.concatenate([diag, right], axis=1)
        work[r0:r1, :] = strip
        if r1 < LANE:
            work[r1:, :] = work[r1:, :] - dot_high(diag.T[r1:, :], strip, (((1,), (0,)), ((), ())))


def diagonal(ref, base, tip, scale):
    tile = unfold(ref[base : base + HALF, :] * scale, ref[tip : tip + 1, :] * scale)
    eye = lax.broadcasted_iota(jnp.int32, tile.shape, 0) == lax.broadcasted_iota(
        jnp.int32, tile.shape, 1
    )
    return tile + jnp.where(eye, RIDGE, 0.0)


def first_kernel(part_ref, out_ref, *, scale):
    out_ref[:, :LANE] = diagonal(part_ref, 0, TIP, scale)
    for t in range(2):
        side = part_ref[HALF + t * LANE : HALF + (t + 1) * LANE, :]
        out_ref[:, (t + 1) * LANE : (t + 2) * LANE] = side * scale
    factor_panel(out_ref)


def first_panel(part, width, scale):
    return pl.pallas_call(
        lambda *refs: first_kernel(*refs, scale=scale),
        out_shape=pltpu.VMEM((LANE, width), F32),
        compiler_params=pltpu.CompilerParams(vmem_limit_bytes=VMEM_BYTES),
        name="first_panel",
    )(near(part))


def rest_kernel(part_ref, top_ref, out_ref, mid, low, *, scale):
    top = top_ref[...]
    mid[:, :LANE] = diagonal(part_ref, 0, TIP_ODD, scale)
    mid[:, LANE:] = part_ref[LANE : 2 * LANE, :] * scale
    mid[...] = mid[...] - dot_high(top[:, LANE : 2 * LANE], top[:, LANE:], TN)
    low[...] = diagonal(part_ref, HALF, TIP_ODD + 1, scale) - dot_high(
        top[:, 2 * LANE :], top[:, 2 * LANE :], TN
    )
    factor_panel(mid)
    right = mid[:, LANE:]
    low[...] = low[...] - dot_high(right, right, TN)
    factor_panel(low)
    kind = out_ref.dtype
    out_ref[:LANE, :] = top.astype(kind)
    out_ref[LANE : 2 * LANE, :LANE] = jnp.zeros((LANE, LANE), kind)
    out_ref[LANE : 2 * LANE, LANE:] = mid[...].astype(kind)
    out_ref[2 * LANE :, : 2 * LANE] = jnp.zeros((LANE, 2 * LANE), kind)
    out_ref[2 * LANE :, 2 * LANE :] = low[...].astype(kind)


def rest_panels(part, top, scale):
    width = top.shape[1]
    return pl.pallas_call(
        lambda *refs: rest_kernel(*refs, scale=scale),
        out_shape=pltpu.VMEM((width, width), BF16),
        scratch_shapes=[pltpu.VMEM((LANE, 2 * LANE), F32), pltpu.VMEM((LANE, LANE), F32)],
        compiler_params=pltpu.CompilerParams(vmem_limit_bytes=VMEM_BYTES),
        name="rest_panels",
    )(near(part), near(top))


def on_device(tokens, block_expert, gate_weight, up_weight):
    owners = lax.axis_size("expert")
    replicas = lax.axis_size("dp")
    experts_each, _, hidden_width = gate_weight.shape
    chips = owners // 2
    shifts = [(0, 0), (0, 1)] + [(dy, dc) for dc in range(2) for dy in (1, chips - 1)]
    shifts += [(2, 0), (2, 1)]
    member = lax.axis_index("expert").reshape(1)
    outgoing = pack(block_expert, member, tokens, experts_each, shifts, chips)
    pairs = [(d, d ^ SIDE) for d in range(replicas)]
    arrived, gathered = [], []
    weights = bring(outgoing[0], gate_weight, up_weight)

    def swap_rows(g):
        rows = hidden_rows(arrived[EDGES[g] : EDGES[g + 1]], *weights)
        gathered.append([rows, lax.ppermute(rows, "dp", pairs)])

    for (dy, dc), payload in zip(shifts, outgoing):
        route = [
            (y * 2 + c, ((y + dy) % chips) * 2 + (c + dc) % 2)
            for y in range(chips)
            for c in range(2)
        ]
        if dy == 2 and not gathered:
            swap_rows(0)
        if dy == 2:
            payload, _ = lax.optimization_barrier((payload, gathered[0][0]))
        arrived.append(payload if dy == dc == 0 else lax.ppermute(payload, "expert", route))
    for g in range(1, len(EDGES) - 1):
        swap_rows(g)
    kept = experts_each // 2
    first = (lax.axis_index("dp") // SIDE % 2 * kept).reshape(1)
    partial_gram = gram(first, kept, [rows for pair in gathered[:-1] for rows in pair])
    partial_gram = gram(first, kept, gathered[-1], (partial_gram,))
    classes = [[d for d in range(replicas) if d // SIDE % 2 == p] for p in range(2)]
    pieces = lax.all_to_all(
        partial_gram, "dp", split_axis=0, concat_axis=0, axis_index_groups=classes, tiled=True
    )
    own = jnp.sum(pieces, axis=0)
    other = lax.ppermute(own[: TIP_ODD + 8], "dp", [(d + 1, d) for d in range(0, replicas, 2)])
    scale = experts_each / (tokens.shape[0] * replicas)
    top = first_panel(own, hidden_width, scale)
    result = rest_panels(other, top, scale)
    row_count = hidden_width // replicas
    sent = result.reshape(replicas, row_count, hidden_width)
    returned = lax.all_to_all(sent, "dp", split_axis=0, concat_axis=0, tiled=True)
    returned = returned.reshape(2, 2, 2, 2, row_count, hidden_width)[:, :, :, 0]
    returned = jnp.swapaxes(returned, 0, 1).reshape(experts_each, row_count, hidden_width)
    return returned.astype(F32)


def solution(mesh):
    placed = (
        P(("dp", "expert"), None),
        P(("dp", "expert")),
        P("expert", None, None),
        P("expert", None, None),
    )

    return jax.shard_map(
        on_device, mesh=mesh, in_specs=placed, out_specs=P("expert", "dp", None), check_vma=False
    )
```

```python
import jax
import jax.numpy as jnp
from jax import lax
from jax.experimental import pallas as pl
from jax.experimental.pallas import tpu as pltpu
from jax.sharding import PartitionSpec as P


BLOCK = 128
RIDGE = 0.05
LANE = 128
TAG = 16
SIDE = 4
VMEM_BYTES = 20 << 20
EDGES = (0, 2, 4, 6, 7, 8)
STRIP = 64
F32 = jnp.float32
BF16 = jnp.bfloat16
HIGH = lax.Precision.HIGHEST
TN = (((0,), (0,)), ((), ()))
NN = (((1,), (0,)), ((), ()))
HALF = 64
QUARTER = 32
SECOND = HALF + LANE
THIRD = SECOND + HALF
TIP = THIRD + QUARTER


def near(x):
    return pltpu.with_memory_space_constraint(x, pltpu.VMEM)


def far(x):
    return pltpu.with_memory_space_constraint(x, pltpu.HBM)


def pack_kernel(member_ref, assign_hbm, tok_hbm, *rest, experts_each, shifts, chips):
    outs = rest[: len(shifts)]
    assign_ref, tok_ref, sem = rest[len(shifts) :]
    blocks, chunks = tok_ref.shape[0] // BLOCK, tok_ref.shape[1] // LANE
    fetch = [
        pltpu.make_async_copy(assign_hbm, assign_ref, sem.at[0]),
        pltpu.make_async_copy(tok_hbm, tok_ref, sem.at[1]),
    ]
    for copy in fetch:
        copy.start()
    for copy in fetch:
        copy.wait()
    chip = lax.div(member_ref[0], 2)
    core = lax.rem(member_ref[0], 2)
    for (dy, dc), out in zip(shifts, outs):
        dest = lax.rem(chip + dy, chips) * 2 + lax.rem(core + dc, 2)
        block = jnp.int32(0)
        code = jnp.int32(0)
        for b in range(blocks):
            expert = assign_ref[b]
            owner = lax.div(expert, experts_each)
            hit = owner == dest
            block = jnp.where(hit, b, block)
            code = jnp.where(hit, expert - owner * experts_each + 1, code)
        row = pl.multiple_of(block * BLOCK, BLOCK)
        for c in range(chunks):
            out[c * BLOCK : (c + 1) * BLOCK, :] = tok_ref[
                pl.ds(row, BLOCK), c * LANE : (c + 1) * LANE
            ]
        out[chunks * BLOCK :, :] = jnp.full((TAG, LANE), code.astype(F32), F32).astype(BF16)


def pack(assign, member, tokens, experts_each, shifts, chips):
    rows = BLOCK * tokens.shape[1] // LANE + TAG
    return pl.pallas_call(
        lambda *refs: pack_kernel(*refs, experts_each=experts_each, shifts=shifts, chips=chips),
        in_specs=[pl.BlockSpec(memory_space=pltpu.SMEM)]
        + [pl.BlockSpec(memory_space=pl.ANY)] * 2,
        out_specs=[pl.BlockSpec(memory_space=pltpu.VMEM)] * len(shifts),
        out_shape=[pltpu.VMEM((rows, LANE), BF16)] * len(shifts),
        scratch_shapes=[
            pltpu.SMEM(assign.shape, assign.dtype),
            pltpu.VMEM(tokens.shape, tokens.dtype),
            pltpu.SemaphoreType.DMA((2,)),
        ],
        compiler_params=pltpu.CompilerParams(vmem_limit_bytes=VMEM_BYTES),
        name="pack",
    )(member, far(assign), far(tokens))


def hidden_kernel(*refs, slots, model_width):
    xs = refs[:slots]
    gate_ref, up_ref, out_ref = refs[slots:]
    chunks = model_width // LANE
    codes = []
    for s in range(slots):
        tag = xs[s][chunks * BLOCK : chunks * BLOCK + TAG, :].astype(F32)
        codes.append(jnp.max(tag).astype(jnp.int32))

    width = out_ref.shape[1]
    lane = lax.broadcasted_iota(jnp.int32, (TAG, width), 1)
    tags = jnp.zeros((TAG, width), F32)
    for s in range(slots):
        tags = jnp.where(lane == s, codes[s].astype(F32), tags)
    out_ref[slots * BLOCK :, :] = tags.astype(BF16)
    for s in range(slots):

        @pl.when(codes[s] > 0)
        def _(s=s):
            expert = codes[s] - 1
            x = jnp.concatenate(
                [xs[s][c * BLOCK : (c + 1) * BLOCK, :] for c in range(chunks)], axis=1
            )
            gate = jnp.dot(x, gate_ref[expert], preferred_element_type=F32)
            up = jnp.dot(x, up_ref[expert], preferred_element_type=F32)
            hidden = gate / (1.0 + jnp.exp(-gate)) * up
            out_ref[s * BLOCK : (s + 1) * BLOCK, :] = hidden.astype(BF16)


def hidden_rows(arrived, gate_weight, up_weight):
    slots = len(arrived)
    _, model_width, hidden_width = gate_weight.shape
    return pl.pallas_call(
        lambda *refs: hidden_kernel(*refs, slots=slots, model_width=model_width),
        in_specs=[pl.BlockSpec(memory_space=pltpu.VMEM)] * (slots + 2),
        out_specs=pl.BlockSpec(memory_space=pltpu.VMEM),
        out_shape=pltpu.VMEM((slots * BLOCK + TAG, hidden_width), BF16),
        compiler_params=pltpu.CompilerParams(vmem_limit_bytes=VMEM_BYTES),
        name="hidden",
    )(*[near(x) for x in (*arrived, gate_weight, up_weight)])


def bring_kernel(_, gate_ref, up_ref, gate_out, up_out, sem):
    copies = [
        pltpu.make_async_copy(gate_ref, gate_out, sem.at[0]),
        pltpu.make_async_copy(up_ref, up_out, sem.at[1]),
    ]
    for copy in copies:
        copy.start()
    for copy in copies:
        copy.wait()


def bring(after, gate_weight, up_weight):
    return pl.pallas_call(
        bring_kernel,
        in_specs=[pl.BlockSpec(memory_space=pl.ANY)] * 3,
        out_specs=[pl.BlockSpec(memory_space=pltpu.VMEM)] * 2,
        out_shape=[pltpu.VMEM(w.shape, w.dtype) for w in (gate_weight, up_weight)],
        scratch_shapes=[pltpu.SemaphoreType.DMA((2,))],
        compiler_params=pltpu.CompilerParams(vmem_limit_bytes=VMEM_BYTES),
        name="bring",
    )(after, far(gate_weight), far(up_weight))


def fold(tile):
    row = lax.broadcasted_iota(jnp.int32, (HALF, LANE), 0)
    lane = lax.broadcasted_iota(jnp.int32, (HALF, LANE), 1)
    upper, lower = tile[:HALF, :], tile[HALF:, :]
    folded = jnp.where((lane < HALF) & (lane < row), pltpu.roll(lower, HALF, 1), upper)
    corner = jnp.sum(jnp.where(lane == row + HALF, lower, 0.0), axis=0, keepdims=True)
    return folded, corner


def unfold(folded, corner):
    row = lax.broadcasted_iota(jnp.int32, (HALF, LANE), 0)
    lane = lax.broadcasted_iota(jnp.int32, (HALF, LANE), 1)
    flipped = jnp.concatenate([folded, jnp.zeros((HALF, LANE), F32)], axis=0).T
    upper = jnp.where(lane < row, flipped[:HALF, :], folded)
    below, above = pltpu.roll(folded, HALF, 1), pltpu.roll(flipped[:HALF, :], HALF, 1)
    inner = jnp.where(lane - HALF < row, below, jnp.where(lane - HALF == row, corner, above))
    return jnp.concatenate([upper, jnp.where(lane < HALF, flipped[HALF:, :], inner)], axis=0)


def gram_kernel(first_ref, *refs, counts, kept):
    groups, out_ref = refs[: len(counts)], refs[-1]
    out_ref[...] = refs[-2][...] if len(refs) > len(counts) + 1 else jnp.zeros(out_ref.shape, F32)
    lane = lax.broadcasted_iota(jnp.int32, (TAG, LANE), 1)
    where = [(ref, s, n) for ref, n in zip(groups, counts) for s in range(n)]
    codes = []
    for ref, s, n in where:
        tag = ref[n * BLOCK : n * BLOCK + TAG, :LANE].astype(F32)
        codes.append(jnp.max(jnp.where(lane == s, tag, 0.0)).astype(jnp.int32))
    for code, (ref, s, n) in zip(codes, where):
        local = code - 1 - first_ref[0]

        @pl.when((local >= 0) & (local < kept))
        def _(ref=ref, s=s, local=local):
            hidden = ref[s * BLOCK : (s + 1) * BLOCK, :]
            even, odd = 2 * local, 2 * local + 1
            parts = [
                lax.dot_general(
                    hidden[:, i * LANE : (i + 1) * LANE],
                    hidden[:, i * LANE :],
                    TN,
                    preferred_element_type=F32,
                )
                for i in range(3)
            ]
            folds = [fold(part[:, :LANE]) for part in parts]
            for i, (_, corner) in enumerate(folds):
                out_ref[even, TIP + i : TIP + i + 1, :] += corner
            out_ref[even, :HALF, :] += folds[0][0]
            out_ref[even, HALF:SECOND, :] += parts[0][:, LANE : 2 * LANE]
            out_ref[even, SECOND:THIRD, :] += folds[1][0]
            out_ref[even, THIRD:TIP, :] += folds[2][0][:QUARTER, :]
            out_ref[odd, :LANE, :] += parts[0][:, 2 * LANE :]
            out_ref[odd, LANE : 2 * LANE, :] += parts[1][:, LANE:]
            out_ref[odd, THIRD:TIP, :] += folds[2][0][QUARTER:, :]


def gram(first, kept, groups, prior=()):
    counts = [(g.shape[0] - TAG) // BLOCK for g in groups]
    return pl.pallas_call(
        lambda *refs: gram_kernel(*refs, counts=counts, kept=kept),
        in_specs=[pl.BlockSpec(memory_space=pltpu.SMEM)]
        + [pl.BlockSpec(memory_space=pltpu.VMEM)] * (len(groups) + len(prior)),
        out_specs=pl.BlockSpec(memory_space=pltpu.VMEM),
        out_shape=pltpu.VMEM((2 * kept, TIP + 8, LANE), F32),
        compiler_params=pltpu.CompilerParams(vmem_limit_bytes=VMEM_BYTES),
        name="gram",
    )(first, *[near(x) for x in (*groups, *prior)])


def factor_strip(groups, lane0, sub):
    wide = lambda v: jnp.concatenate([v] * (groups[0].shape[1] // LANE), axis=1)
    groups = list(groups)
    wide_sub = wide(sub)
    for b in range(len(groups)):
        base = lane0 + 8 * b
        cols = [
            [jnp.broadcast_to(g[:, base + j : base + j + 1], (8, LANE)) for g in groups[b:]]
            for j in range(8)
        ]
        for k in range(8):
            inv = lax.rsqrt(cols[k][0][k : k + 1, :])
            row = groups[b][k : k + 1, :] * wide(inv)
            mult = [jnp.where(sub > k, cols[k][0], 0.0)] + cols[k][1:]
            mult = [c * inv for c in mult]
            for g, m in enumerate(mult):
                groups[b + g] = groups[b + g] - wide(m) * row
            groups[b] = jnp.where(wide_sub == k, row, groups[b])
            for j in range(k + 1, 8):
                top = cols[j][0][k : k + 1, :] * inv
                cols[j] = [c - m * top for c, m in zip(cols[j], mult)]
    return groups


def dot_high(a, b, dims):
    return lax.dot_general(a, b, dims, precision=HIGH, preferred_element_type=F32)


def factor_panel(work):
    sub = lax.broadcasted_iota(jnp.int32, (8, LANE), 0)
    lane = lax.broadcasted_iota(jnp.int32, (8, LANE), 1)
    width = work.shape[1]
    for r0 in range(0, LANE, STRIP):
        r1 = r0 + STRIP
        groups = factor_strip([work[r : r + 8, :] for r in range(r0, r1, 8)], r0, sub)
        diag = jnp.concatenate(
            [
                jnp.where(lane >= r0 + 8 * g + sub, rows[:, :LANE], 0.0)
                for g, rows in enumerate(groups)
            ],
            axis=0,
        )
        strip = diag
        if width > LANE:
            right = jnp.concatenate([rows[:, LANE:] for rows in groups], axis=0)
            strip = jnp.concatenate([diag, right], axis=1)
        work[r0:r1, :] = strip
        if r1 < LANE:
            work[r1:, :] = work[r1:, :] - dot_high(diag.T[r1:, :], strip, NN)


def identity_tile():
    shape = (LANE, LANE)
    rows, cols = (lax.broadcasted_iota(jnp.int32, shape, axis) for axis in range(2))
    return jnp.where(rows == cols, 1.0, 0.0)


def diagonal(folded, corner, scale):
    return unfold(folded * scale, corner * scale) + RIDGE * identity_tile()


def first_kernel(part_ref, top_ref, mid_ref, *, scale):
    tip = lambda i: part_ref[TIP + i : TIP + i + 1, :]
    top_ref[:, :LANE] = diagonal(part_ref[:HALF, :], tip(0), scale)
    top_ref[:, LANE : 2 * LANE] = part_ref[HALF:SECOND, :] * scale
    top_ref[:, 2 * LANE :] = identity_tile()
    factor_panel(top_ref)
    side = top_ref[:, LANE : 2 * LANE]
    mid_ref[:, :LANE] = diagonal(part_ref[SECOND:THIRD, :], tip(1), scale) - dot_high(side, side, TN)
    mid_ref[:, LANE:] = identity_tile()
    factor_panel(mid_ref)


def first_panels(part, scale):
    return pl.pallas_call(
        lambda *refs: first_kernel(*refs, scale=scale),
        out_shape=[pltpu.VMEM((LANE, 3 * LANE), F32), pltpu.VMEM((LANE, 2 * LANE), F32)],
        compiler_params=pltpu.CompilerParams(vmem_limit_bytes=VMEM_BYTES),
        name="first_panels",
    )(near(part))


def last_kernel(part_ref, other_ref, top_ref, mid_ref, out_ref, low, *, scale):
    right = dot_high(top_ref[:, 2 * LANE :], other_ref[:LANE, :] * scale, NN)
    rest = other_ref[LANE : 2 * LANE, :] * scale - dot_high(top_ref[:, LANE : 2 * LANE], right, TN)
    below = dot_high(mid_ref[:, LANE:], rest, NN)
    folded = jnp.concatenate([part_ref[THIRD:TIP, :], other_ref[THIRD:TIP, :]], axis=0)
    low[...] = (
        diagonal(folded, part_ref[TIP + 2 : TIP + 3, :], scale)
        - dot_high(right, right, TN)
        - dot_high(below, below, TN)
    )
    factor_panel(low)
    kind = out_ref.dtype
    out_ref[:LANE, : 2 * LANE] = top_ref[:, : 2 * LANE].astype(kind)
    out_ref[:LANE, 2 * LANE :] = right.astype(kind)
    out_ref[LANE : 2 * LANE, :LANE] = jnp.zeros((LANE, LANE), kind)
    out_ref[LANE : 2 * LANE, LANE : 2 * LANE] = mid_ref[:, :LANE].astype(kind)
    out_ref[LANE : 2 * LANE, 2 * LANE :] = below.astype(kind)
    out_ref[2 * LANE :, : 2 * LANE] = jnp.zeros((LANE, 2 * LANE), kind)
    out_ref[2 * LANE :, 2 * LANE :] = low[...].astype(kind)


def last_panel(part, other, top, mid, scale):
    width = top.shape[1]
    return pl.pallas_call(
        lambda *refs: last_kernel(*refs, scale=scale),
        out_shape=pltpu.VMEM((width, width), BF16),
        scratch_shapes=[pltpu.VMEM((LANE, LANE), F32)],
        compiler_params=pltpu.CompilerParams(vmem_limit_bytes=VMEM_BYTES),
        name="last_panel",
    )(near(part), near(other), near(top), near(mid))


def on_device(tokens, block_expert, gate_weight, up_weight):
    owners = lax.axis_size("expert")
    replicas = lax.axis_size("dp")
    experts_each, _, hidden_width = gate_weight.shape
    chips = owners // 2
    shifts = [(0, 0), (0, 1)] + [(dy, dc) for dc in range(2) for dy in (1, chips - 1)]
    shifts += [(2, 0), (2, 1)]
    member = lax.axis_index("expert").reshape(1)
    outgoing = pack(block_expert, member, tokens, experts_each, shifts, chips)
    pairs = [(d, d ^ SIDE) for d in range(replicas)]
    arrived, gathered = [], []
    weights = bring(outgoing[0], gate_weight, up_weight)

    def swap_rows(g):
        rows = hidden_rows(arrived[EDGES[g] : EDGES[g + 1]], *weights)
        gathered.append([rows, lax.ppermute(rows, "dp", pairs)])

    for (dy, dc), payload in zip(shifts, outgoing):
        route = [
            (y * 2 + c, ((y + dy) % chips) * 2 + (c + dc) % 2)
            for y in range(chips)
            for c in range(2)
        ]
        if dy == 2 and not gathered:
            swap_rows(0)
        if dy == 2:
            payload, _ = lax.optimization_barrier((payload, gathered[0][0]))
        arrived.append(payload if dy == dc == 0 else lax.ppermute(payload, "expert", route))
    for g in range(1, len(EDGES) - 1):
        swap_rows(g)
    kept = experts_each // 2
    first = (lax.axis_index("dp") // SIDE % 2 * kept).reshape(1)
    partial_gram = gram(first, kept, [rows for pair in gathered[:-2] for rows in pair])
    tail = [rows for pair in gathered[-2:] for rows in pair]
    partial_gram = gram(first, kept, tail, (partial_gram,))
    classes = [[d for d in range(replicas) if d // SIDE % 2 == p] for p in range(2)]
    pieces = lax.all_to_all(
        partial_gram, "dp", split_axis=0, concat_axis=0, axis_index_groups=classes, tiled=True
    )
    own = jnp.sum(pieces, axis=0)
    other = lax.ppermute(own[:TIP], "dp", [(d + 1, d) for d in range(0, replicas, 2)])
    scale = experts_each / (tokens.shape[0] * replicas)
    top, mid = first_panels(own, scale)
    result = last_panel(own, other, top, mid, scale)
    row_count = hidden_width // replicas
    sent = result.reshape(replicas, row_count, hidden_width)
    returned = lax.all_to_all(sent, "dp", split_axis=0, concat_axis=0, tiled=True)
    returned = returned.reshape(2, 2, 2, 2, row_count, hidden_width)[:, :, :, 0]
    returned = jnp.swapaxes(returned, 0, 1).reshape(experts_each, row_count, hidden_width)
    return returned.astype(F32)


def solution(mesh):
    placed = (
        P(("dp", "expert"), None),
        P(("dp", "expert")),
        P("expert", None, None),
        P("expert", None, None),
    )

    return jax.shard_map(
        on_device, mesh=mesh, in_specs=placed, out_specs=P("expert", "dp", None), check_vma=False
    )
```

```python
import jax
import jax.numpy as jnp
from jax import lax
from jax.experimental import pallas as pl
from jax.experimental.pallas import tpu as pltpu
from jax.sharding import PartitionSpec as P


BLOCK = 128
RIDGE = 0.05
LANE = 128
TAG = 16
SIDE = 4
VMEM_BYTES = 20 << 20
EDGES = (0, 2, 4, 6, 7, 8)
STRIP = 64
F32 = jnp.float32
BF16 = jnp.bfloat16
HIGH = lax.Precision.HIGHEST
TN = (((0,), (0,)), ((), ()))
NN = (((1,), (0,)), ((), ()))
HALF = 64
QUARTER = 32
SECOND = HALF + LANE
THIRD = SECOND + HALF
TIP = THIRD + QUARTER


def near(x):
    return pltpu.with_memory_space_constraint(x, pltpu.VMEM)


def far(x):
    return pltpu.with_memory_space_constraint(x, pltpu.HBM)


def pack_kernel(member_ref, assign_hbm, tok_hbm, *rest, experts_each, shifts, chips):
    outs = rest[: len(shifts)]
    assign_ref, tok_ref, sem = rest[len(shifts) :]
    blocks, chunks = tok_ref.shape[0] // BLOCK, tok_ref.shape[1] // LANE
    fetch = [
        pltpu.make_async_copy(assign_hbm, assign_ref, sem.at[0]),
        pltpu.make_async_copy(tok_hbm, tok_ref, sem.at[1]),
    ]
    for copy in fetch:
        copy.start()
    for copy in fetch:
        copy.wait()
    chip = lax.div(member_ref[0], 2)
    core = lax.rem(member_ref[0], 2)
    for (dy, dc), out in zip(shifts, outs):
        dest = lax.rem(chip + dy, chips) * 2 + lax.rem(core + dc, 2)
        block = jnp.int32(0)
        code = jnp.int32(0)
        for b in range(blocks):
            expert = assign_ref[b]
            owner = lax.div(expert, experts_each)
            hit = owner == dest
            block = jnp.where(hit, b, block)
            code = jnp.where(hit, expert - owner * experts_each + 1, code)
        row = pl.multiple_of(block * BLOCK, BLOCK)
        for c in range(chunks):
            out[c * BLOCK : (c + 1) * BLOCK, :] = tok_ref[
                pl.ds(row, BLOCK), c * LANE : (c + 1) * LANE
            ]
        out[chunks * BLOCK :, :] = jnp.full((TAG, LANE), code.astype(F32), F32).astype(BF16)


def pack(assign, member, tokens, experts_each, shifts, chips):
    rows = BLOCK * tokens.shape[1] // LANE + TAG
    return pl.pallas_call(
        lambda *refs: pack_kernel(*refs, experts_each=experts_each, shifts=shifts, chips=chips),
        in_specs=[pl.BlockSpec(memory_space=pltpu.SMEM)]
        + [pl.BlockSpec(memory_space=pl.ANY)] * 2,
        out_specs=[pl.BlockSpec(memory_space=pltpu.VMEM)] * len(shifts),
        out_shape=[pltpu.VMEM((rows, LANE), BF16)] * len(shifts),
        scratch_shapes=[
            pltpu.SMEM(assign.shape, assign.dtype),
            pltpu.VMEM(tokens.shape, tokens.dtype),
            pltpu.SemaphoreType.DMA((2,)),
        ],
        compiler_params=pltpu.CompilerParams(vmem_limit_bytes=VMEM_BYTES),
        name="pack",
    )(member, far(assign), far(tokens))


def hidden_kernel(*refs, slots, model_width):
    xs = refs[:slots]
    gate_ref, up_ref, out_ref = refs[slots:]
    chunks = model_width // LANE
    codes = []
    for s in range(slots):
        tag = xs[s][chunks * BLOCK : chunks * BLOCK + TAG, :].astype(F32)
        codes.append(jnp.max(tag).astype(jnp.int32))

    width = out_ref.shape[1]
    lane = lax.broadcasted_iota(jnp.int32, (TAG, width), 1)
    tags = jnp.zeros((TAG, width), F32)
    for s in range(slots):
        tags = jnp.where(lane == s, codes[s].astype(F32), tags)
    out_ref[slots * BLOCK :, :] = tags.astype(BF16)
    for s in range(slots):

        @pl.when(codes[s] > 0)
        def _(s=s):
            expert = codes[s] - 1
            x = jnp.concatenate(
                [xs[s][c * BLOCK : (c + 1) * BLOCK, :] for c in range(chunks)], axis=1
            )
            gate = jnp.dot(x, gate_ref[expert], preferred_element_type=F32)
            up = jnp.dot(x, up_ref[expert], preferred_element_type=F32)
            hidden = gate / (1.0 + jnp.exp(-gate)) * up
            out_ref[s * BLOCK : (s + 1) * BLOCK, :] = hidden.astype(BF16)


def hidden_rows(arrived, gate_weight, up_weight):
    slots = len(arrived)
    _, model_width, hidden_width = gate_weight.shape
    return pl.pallas_call(
        lambda *refs: hidden_kernel(*refs, slots=slots, model_width=model_width),
        in_specs=[pl.BlockSpec(memory_space=pltpu.VMEM)] * (slots + 2),
        out_specs=pl.BlockSpec(memory_space=pltpu.VMEM),
        out_shape=pltpu.VMEM((slots * BLOCK + TAG, hidden_width), BF16),
        compiler_params=pltpu.CompilerParams(vmem_limit_bytes=VMEM_BYTES),
        name="hidden",
    )(*[near(x) for x in (*arrived, gate_weight, up_weight)])


def bring_kernel(_, gate_ref, up_ref, gate_out, up_out, sem):
    copies = [
        pltpu.make_async_copy(gate_ref, gate_out, sem.at[0]),
        pltpu.make_async_copy(up_ref, up_out, sem.at[1]),
    ]
    for copy in copies:
        copy.start()
    for copy in copies:
        copy.wait()


def bring(after, gate_weight, up_weight):
    return pl.pallas_call(
        bring_kernel,
        in_specs=[pl.BlockSpec(memory_space=pl.ANY)] * 3,
        out_specs=[pl.BlockSpec(memory_space=pltpu.VMEM)] * 2,
        out_shape=[pltpu.VMEM(w.shape, w.dtype) for w in (gate_weight, up_weight)],
        scratch_shapes=[pltpu.SemaphoreType.DMA((2,))],
        compiler_params=pltpu.CompilerParams(vmem_limit_bytes=VMEM_BYTES),
        name="bring",
    )(after, far(gate_weight), far(up_weight))


def fold(tile):
    row = lax.broadcasted_iota(jnp.int32, (HALF, LANE), 0)
    lane = lax.broadcasted_iota(jnp.int32, (HALF, LANE), 1)
    upper, lower = tile[:HALF, :], tile[HALF:, :]
    folded = jnp.where((lane < HALF) & (lane < row), pltpu.roll(lower, HALF, 1), upper)
    corner = jnp.sum(jnp.where(lane == row + HALF, lower, 0.0), axis=0, keepdims=True)
    return folded, corner


def unfold(folded, corner):
    row = lax.broadcasted_iota(jnp.int32, (HALF, LANE), 0)
    lane = lax.broadcasted_iota(jnp.int32, (HALF, LANE), 1)
    flipped = jnp.concatenate([folded, jnp.zeros((HALF, LANE), F32)], axis=0).T
    upper = jnp.where(lane < row, flipped[:HALF, :], folded)
    below, above = pltpu.roll(folded, HALF, 1), pltpu.roll(flipped[:HALF, :], HALF, 1)
    inner = jnp.where(lane - HALF < row, below, jnp.where(lane - HALF == row, corner, above))
    return jnp.concatenate([upper, jnp.where(lane < HALF, flipped[HALF:, :], inner)], axis=0)


def gram_kernel(first_ref, *refs, counts, kept):
    groups, out_ref = refs[: len(counts)], refs[-1]
    out_ref[...] = refs[-2][...] if len(refs) > len(counts) + 1 else jnp.zeros(out_ref.shape, F32)
    lane = lax.broadcasted_iota(jnp.int32, (TAG, LANE), 1)
    where = [(ref, s, n) for ref, n in zip(groups, counts) for s in range(n)]
    codes = []
    for ref, s, n in where:
        tag = ref[n * BLOCK : n * BLOCK + TAG, :LANE].astype(F32)
        codes.append(jnp.max(jnp.where(lane == s, tag, 0.0)).astype(jnp.int32))
    for code, (ref, s, n) in zip(codes, where):
        local = code - 1 - first_ref[0]

        @pl.when((local >= 0) & (local < kept))
        def _(ref=ref, s=s, local=local):
            hidden = ref[s * BLOCK : (s + 1) * BLOCK, :]
            even, odd = 2 * local, 2 * local + 1
            parts = [
                lax.dot_general(
                    hidden[:, i * LANE : (i + 1) * LANE],
                    hidden[:, i * LANE :],
                    TN,
                    preferred_element_type=F32,
                )
                for i in range(3)
            ]
            folds = [fold(part[:, :LANE]) for part in parts]
            for i, (_, corner) in enumerate(folds):
                out_ref[even, TIP + i : TIP + i + 1, :] += corner
            out_ref[even, :HALF, :] += folds[0][0]
            out_ref[even, HALF:SECOND, :] += parts[0][:, LANE : 2 * LANE]
            out_ref[even, SECOND:THIRD, :] += folds[1][0]
            out_ref[even, THIRD:TIP, :] += folds[2][0][:QUARTER, :]
            out_ref[odd, :LANE, :] += parts[0][:, 2 * LANE :]
            out_ref[odd, LANE : 2 * LANE, :] += parts[1][:, LANE:]
            out_ref[odd, THIRD:TIP, :] += folds[2][0][QUARTER:, :]


def gram(first, kept, groups, prior=()):
    counts = [(g.shape[0] - TAG) // BLOCK for g in groups]
    return pl.pallas_call(
        lambda *refs: gram_kernel(*refs, counts=counts, kept=kept),
        in_specs=[pl.BlockSpec(memory_space=pltpu.SMEM)]
        + [pl.BlockSpec(memory_space=pltpu.VMEM)] * (len(groups) + len(prior)),
        out_specs=pl.BlockSpec(memory_space=pltpu.VMEM),
        out_shape=pltpu.VMEM((2 * kept, TIP + 8, LANE), F32),
        compiler_params=pltpu.CompilerParams(vmem_limit_bytes=VMEM_BYTES),
        name="gram",
    )(first, *[near(x) for x in (*groups, *prior)])


def factor_strip(groups, lane0, sub):
    wide = lambda v: jnp.concatenate([v] * (groups[0].shape[1] // LANE), axis=1)
    groups = list(groups)
    wide_sub = wide(sub)
    for b in range(len(groups)):
        base = lane0 + 8 * b
        cols = [
            [jnp.broadcast_to(g[:, base + j : base + j + 1], (8, LANE)) for g in groups[b:]]
            for j in range(8)
        ]
        for k in range(8):
            inv = lax.rsqrt(cols[k][0][k : k + 1, :])
            row = groups[b][k : k + 1, :] * wide(inv)
            mult = [jnp.where(sub > k, cols[k][0], 0.0)] + cols[k][1:]
            mult = [c * inv for c in mult]
            for g, m in enumerate(mult):
                groups[b + g] = groups[b + g] - wide(m) * row
            groups[b] = jnp.where(wide_sub == k, row, groups[b])
            for j in range(k + 1, 8):
                top = cols[j][0][k : k + 1, :] * inv
                cols[j] = [c - m * top for c, m in zip(cols[j], mult)]
    return groups


def dot_high(a, b, dims):
    return lax.dot_general(a, b, dims, precision=HIGH, preferred_element_type=F32)


def factor_panel(work):
    sub = lax.broadcasted_iota(jnp.int32, (8, LANE), 0)
    lane = lax.broadcasted_iota(jnp.int32, (8, LANE), 1)
    width = work.shape[1]
    for r0 in range(0, LANE, STRIP):
        r1 = r0 + STRIP
        groups = factor_strip([work[r : r + 8, :] for r in range(r0, r1, 8)], r0, sub)
        diag = jnp.concatenate(
            [
                jnp.where(lane >= r0 + 8 * g + sub, rows[:, :LANE], 0.0)
                for g, rows in enumerate(groups)
            ],
            axis=0,
        )
        strip = diag
        if width > LANE:
            right = jnp.concatenate([rows[:, LANE:] for rows in groups], axis=0)
            strip = jnp.concatenate([diag, right], axis=1)
        work[r0:r1, :] = strip
        if r1 < LANE:
            work[r1:, :] = work[r1:, :] - dot_high(diag.T[r1:, :], strip, NN)


def identity_tile():
    shape = (LANE, LANE)
    rows, cols = (lax.broadcasted_iota(jnp.int32, shape, axis) for axis in range(2))
    return jnp.where(rows == cols, 1.0, 0.0)


def diagonal(folded, corner, scale):
    return unfold(folded * scale, corner * scale) + RIDGE * identity_tile()


def first_kernel(part_ref, top_ref, mid_ref, *, scale):
    tip = lambda i: part_ref[TIP + i : TIP + i + 1, :]
    top_ref[:, :LANE] = diagonal(part_ref[:HALF, :], tip(0), scale)
    top_ref[:, LANE : 2 * LANE] = part_ref[HALF:SECOND, :] * scale
    top_ref[:, 2 * LANE :] = identity_tile()
    factor_panel(top_ref)
    side = top_ref[:, LANE : 2 * LANE]
    mid_ref[:, :LANE] = diagonal(part_ref[SECOND:THIRD, :], tip(1), scale) - dot_high(side, side, TN)
    mid_ref[:, LANE:] = identity_tile()
    factor_panel(mid_ref)


def first_panels(part, scale):
    return pl.pallas_call(
        lambda *refs: first_kernel(*refs, scale=scale),
        out_shape=[pltpu.VMEM((LANE, 3 * LANE), F32), pltpu.VMEM((LANE, 2 * LANE), F32)],
        compiler_params=pltpu.CompilerParams(vmem_limit_bytes=VMEM_BYTES),
        name="first_panels",
    )(near(part))


def last_kernel(part_ref, other_ref, top_ref, mid_ref, out_ref, low, *, scale):
    right = dot_high(top_ref[:, 2 * LANE :], other_ref[:LANE, :] * scale, NN)
    rest = other_ref[LANE : 2 * LANE, :] * scale - dot_high(top_ref[:, LANE : 2 * LANE], right, TN)
    below = dot_high(mid_ref[:, LANE:], rest, NN)
    folded = jnp.concatenate([part_ref[THIRD:TIP, :], other_ref[THIRD:TIP, :]], axis=0)
    low[...] = (
        diagonal(folded, part_ref[TIP + 2 : TIP + 3, :], scale)
        - dot_high(right, right, TN)
        - dot_high(below, below, TN)
    )
    factor_panel(low)
    kind = out_ref.dtype
    out_ref[:LANE, : 2 * LANE] = top_ref[:, : 2 * LANE].astype(kind)
    out_ref[:LANE, 2 * LANE :] = right.astype(kind)
    out_ref[LANE : 2 * LANE, :LANE] = jnp.zeros((LANE, LANE), kind)
    out_ref[LANE : 2 * LANE, LANE : 2 * LANE] = mid_ref[:, :LANE].astype(kind)
    out_ref[LANE : 2 * LANE, 2 * LANE :] = below.astype(kind)
    out_ref[2 * LANE :, : 2 * LANE] = jnp.zeros((LANE, 2 * LANE), kind)
    out_ref[2 * LANE :, 2 * LANE :] = low[...].astype(kind)


def last_panel(part, other, top, mid, scale):
    width = top.shape[1]
    return pl.pallas_call(
        lambda *refs: last_kernel(*refs, scale=scale),
        out_shape=pltpu.VMEM((width, width), BF16),
        scratch_shapes=[pltpu.VMEM((LANE, LANE), F32)],
        compiler_params=pltpu.CompilerParams(vmem_limit_bytes=VMEM_BYTES),
        name="last_panel",
    )(near(part), near(other), near(top), near(mid))


def on_device(tokens, block_expert, gate_weight, up_weight):
    owners = lax.axis_size("expert")
    replicas = lax.axis_size("dp")
    experts_each, _, hidden_width = gate_weight.shape
    chips = owners // 2
    shifts = [(0, 0), (0, 1)] + [(dy, dc) for dc in range(2) for dy in (1, chips - 1)]
    shifts += [(2, 0), (2, 1)]
    member = lax.axis_index("expert").reshape(1)
    outgoing = pack(block_expert, member, tokens, experts_each, shifts, chips)
    pairs = [(d, d ^ 1) for d in range(replicas)]
    arrived, gathered = [], []
    weights = bring(outgoing[0], gate_weight, up_weight)

    def swap_rows(g):
        rows = hidden_rows(arrived[EDGES[g] : EDGES[g + 1]], *weights)
        gathered.append([rows, lax.ppermute(rows, "dp", pairs)])

    for (dy, dc), payload in zip(shifts, outgoing):
        route = [
            (y * 2 + c, ((y + dy) % chips) * 2 + (c + dc) % 2)
            for y in range(chips)
            for c in range(2)
        ]
        if dy == 2 and not gathered:
            swap_rows(0)
        if dy == 2:
            payload, _ = lax.optimization_barrier((payload, gathered[0][0]))
        arrived.append(payload if dy == dc == 0 else lax.ppermute(payload, "expert", route))
    for g in range(1, len(EDGES) - 1):
        swap_rows(g)
    kept = experts_each // 2
    first = (lax.axis_index("dp") % 2 * kept).reshape(1)
    partial_gram = gram(first, kept, [rows for pair in gathered[:-2] for rows in pair])
    tail = [rows for pair in gathered[-2:] for rows in pair]
    partial_gram = gram(first, kept, tail, (partial_gram,))
    side = replicas // SIDE
    classes = [[x * SIDE + z for z in range(p, SIDE, 2) for x in range(side)] for p in range(2)]
    pieces = lax.all_to_all(
        partial_gram, "dp", split_axis=0, concat_axis=0, axis_index_groups=classes, tiled=True
    )
    own = jnp.sum(pieces, axis=0)
    halves = [(d + SIDE, d) for d in range(replicas) if d // SIDE % 2 == 0]
    other = lax.ppermute(own[:TIP], "dp", halves)
    scale = experts_each / (tokens.shape[0] * replicas)
    top, mid = first_panels(own, scale)
    result = last_panel(own, other, top, mid, scale)
    row_count = hidden_width // replicas
    sent = result.reshape(replicas, row_count, hidden_width)
    returned = lax.all_to_all(sent, "dp", split_axis=0, concat_axis=0, tiled=True)
    returned = returned.reshape(2, 2, 2, 2, row_count, hidden_width)[:, 0]
    returned = jnp.transpose(returned, (2, 1, 0, 3, 4))
    returned = returned.reshape(experts_each, row_count, hidden_width)
    return returned.astype(F32)


def solution(mesh):
    placed = (
        P(("dp", "expert"), None),
        P(("dp", "expert")),
        P("expert", None, None),
        P("expert", None, None),
    )

    return jax.shard_map(
        on_device, mesh=mesh, in_specs=placed, out_specs=P("expert", "dp", None), check_vma=False
    )
```

```python
import jax
import jax.numpy as jnp
from jax import lax
from jax.experimental import pallas as pl
from jax.experimental.pallas import tpu as pltpu
from jax.sharding import PartitionSpec as P


BLOCK = 128
RIDGE = 0.05
LANE = 128
TAG = 16
SIDE = 4
VMEM_BYTES = 20 << 20
EDGES = (0, 2, 4, 6, 8)
STRIP = 64
F32 = jnp.float32
BF16 = jnp.bfloat16
HIGH = lax.Precision.HIGHEST
TN = (((0,), (0,)), ((), ()))
NN = (((1,), (0,)), ((), ()))
HALF = 64
QUARTER = 32
SECOND = HALF + LANE
THIRD = SECOND + HALF
TIP = THIRD + QUARTER


def near(x):
    return pltpu.with_memory_space_constraint(x, pltpu.VMEM)


def far(x):
    return pltpu.with_memory_space_constraint(x, pltpu.HBM)


def pack_kernel(member_ref, assign_hbm, tok_hbm, *rest, experts_each, shifts, chips):
    outs = rest[: len(shifts)]
    assign_ref, tok_ref, sem = rest[len(shifts) :]
    blocks, chunks = tok_ref.shape[0] // BLOCK, tok_ref.shape[1] // LANE
    fetch = [
        pltpu.make_async_copy(assign_hbm, assign_ref, sem.at[0]),
        pltpu.make_async_copy(tok_hbm, tok_ref, sem.at[1]),
    ]
    for copy in fetch:
        copy.start()
    for copy in fetch:
        copy.wait()
    chip = lax.div(member_ref[0], 2)
    core = lax.rem(member_ref[0], 2)
    for (dy, dc), out in zip(shifts, outs):
        dest = lax.rem(chip + dy, chips) * 2 + lax.rem(core + dc, 2)
        block = jnp.int32(0)
        code = jnp.int32(0)
        for b in range(blocks):
            expert = assign_ref[b]
            owner = lax.div(expert, experts_each)
            hit = owner == dest
            block = jnp.where(hit, b, block)
            code = jnp.where(hit, expert - owner * experts_each + 1, code)
        row = pl.multiple_of(block * BLOCK, BLOCK)
        for c in range(chunks):
            out[c * BLOCK : (c + 1) * BLOCK, :] = tok_ref[
                pl.ds(row, BLOCK), c * LANE : (c + 1) * LANE
            ]
        out[chunks * BLOCK :, :] = jnp.full((TAG, LANE), code.astype(F32), F32).astype(BF16)


def pack(assign, member, tokens, experts_each, shifts, chips):
    rows = BLOCK * tokens.shape[1] // LANE + TAG
    return pl.pallas_call(
        lambda *refs: pack_kernel(*refs, experts_each=experts_each, shifts=shifts, chips=chips),
        in_specs=[pl.BlockSpec(memory_space=pltpu.SMEM)]
        + [pl.BlockSpec(memory_space=pl.ANY)] * 2,
        out_specs=[pl.BlockSpec(memory_space=pltpu.VMEM)] * len(shifts),
        out_shape=[pltpu.VMEM((rows, LANE), BF16)] * len(shifts),
        scratch_shapes=[
            pltpu.SMEM(assign.shape, assign.dtype),
            pltpu.VMEM(tokens.shape, tokens.dtype),
            pltpu.SemaphoreType.DMA((2,)),
        ],
        compiler_params=pltpu.CompilerParams(vmem_limit_bytes=VMEM_BYTES),
        name="pack",
    )(member, far(assign), far(tokens))


def hidden_kernel(*refs, slots, model_width):
    xs = refs[:slots]
    gate_ref, up_ref, out_ref = refs[slots:]
    chunks = model_width // LANE
    codes = []
    for s in range(slots):
        tag = xs[s][chunks * BLOCK : chunks * BLOCK + TAG, :].astype(F32)
        codes.append(jnp.max(tag).astype(jnp.int32))

    width = out_ref.shape[1]
    lane = lax.broadcasted_iota(jnp.int32, (TAG, width), 1)
    tags = jnp.zeros((TAG, width), F32)
    for s in range(slots):
        tags = jnp.where(lane == s, codes[s].astype(F32), tags)
    out_ref[slots * BLOCK :, :] = tags.astype(BF16)
    for s in range(slots):

        @pl.when(codes[s] > 0)
        def _(s=s):
            expert = codes[s] - 1
            x = jnp.concatenate(
                [xs[s][c * BLOCK : (c + 1) * BLOCK, :] for c in range(chunks)], axis=1
            )
            gate = jnp.dot(x, gate_ref[expert], preferred_element_type=F32)
            up = jnp.dot(x, up_ref[expert], preferred_element_type=F32)
            hidden = gate / (1.0 + jnp.exp(-gate)) * up
            out_ref[s * BLOCK : (s + 1) * BLOCK, :] = hidden.astype(BF16)


def hidden_rows(arrived, gate_weight, up_weight):
    slots = len(arrived)
    _, model_width, hidden_width = gate_weight.shape
    return pl.pallas_call(
        lambda *refs: hidden_kernel(*refs, slots=slots, model_width=model_width),
        in_specs=[pl.BlockSpec(memory_space=pltpu.VMEM)] * (slots + 2),
        out_specs=pl.BlockSpec(memory_space=pltpu.VMEM),
        out_shape=pltpu.VMEM((slots * BLOCK + TAG, hidden_width), BF16),
        compiler_params=pltpu.CompilerParams(vmem_limit_bytes=VMEM_BYTES),
        name="hidden",
    )(*[near(x) for x in (*arrived, gate_weight, up_weight)])


def bring_kernel(_, gate_ref, up_ref, gate_out, up_out, sem):
    copies = [
        pltpu.make_async_copy(gate_ref, gate_out, sem.at[0]),
        pltpu.make_async_copy(up_ref, up_out, sem.at[1]),
    ]
    for copy in copies:
        copy.start()
    for copy in copies:
        copy.wait()


def bring(after, gate_weight, up_weight):
    return pl.pallas_call(
        bring_kernel,
        in_specs=[pl.BlockSpec(memory_space=pl.ANY)] * 3,
        out_specs=[pl.BlockSpec(memory_space=pltpu.VMEM)] * 2,
        out_shape=[pltpu.VMEM(w.shape, w.dtype) for w in (gate_weight, up_weight)],
        scratch_shapes=[pltpu.SemaphoreType.DMA((2,))],
        compiler_params=pltpu.CompilerParams(vmem_limit_bytes=VMEM_BYTES),
        name="bring",
    )(after, far(gate_weight), far(up_weight))


def fold(tile):
    row = lax.broadcasted_iota(jnp.int32, (HALF, LANE), 0)
    lane = lax.broadcasted_iota(jnp.int32, (HALF, LANE), 1)
    upper, lower = tile[:HALF, :], tile[HALF:, :]
    folded = jnp.where((lane < HALF) & (lane < row), pltpu.roll(lower, HALF, 1), upper)
    corner = jnp.sum(jnp.where(lane == row + HALF, lower, 0.0), axis=0, keepdims=True)
    return folded, corner


def unfold(folded, corner):
    row = lax.broadcasted_iota(jnp.int32, (HALF, LANE), 0)
    lane = lax.broadcasted_iota(jnp.int32, (HALF, LANE), 1)
    flipped = jnp.concatenate([folded, jnp.zeros((HALF, LANE), F32)], axis=0).T
    upper = jnp.where(lane < row, flipped[:HALF, :], folded)
    below, above = pltpu.roll(folded, HALF, 1), pltpu.roll(flipped[:HALF, :], HALF, 1)
    inner = jnp.where(lane - HALF < row, below, jnp.where(lane - HALF == row, corner, above))
    return jnp.concatenate([upper, jnp.where(lane < HALF, flipped[HALF:, :], inner)], axis=0)


def gram_kernel(first_ref, *refs, counts, kept):
    groups, out_ref = refs[: len(counts)], refs[-1]
    out_ref[...] = refs[-2][...] if len(refs) > len(counts) + 1 else jnp.zeros(out_ref.shape, F32)
    lane = lax.broadcasted_iota(jnp.int32, (TAG, LANE), 1)
    where = [(ref, s, n) for ref, n in zip(groups, counts) for s in range(n)]
    codes = []
    for ref, s, n in where:
        tag = ref[n * BLOCK : n * BLOCK + TAG, :LANE].astype(F32)
        codes.append(jnp.max(jnp.where(lane == s, tag, 0.0)).astype(jnp.int32))
    for code, (ref, s, n) in zip(codes, where):
        local = code - 1 - first_ref[0]

        @pl.when((local >= 0) & (local < kept))
        def _(ref=ref, s=s, local=local):
            hidden = ref[s * BLOCK : (s + 1) * BLOCK, :]
            even, odd = 2 * local, 2 * local + 1
            parts = [
                lax.dot_general(
                    hidden[:, i * LANE : (i + 1) * LANE],
                    hidden[:, i * LANE :],
                    TN,
                    preferred_element_type=F32,
                )
                for i in range(3)
            ]
            folds = [fold(part[:, :LANE]) for part in parts]
            for i, (_, corner) in enumerate(folds):
                out_ref[even, TIP + i : TIP + i + 1, :] += corner
            out_ref[even, :HALF, :] += folds[0][0]
            out_ref[even, HALF:SECOND, :] += parts[0][:, LANE : 2 * LANE]
            out_ref[even, SECOND:THIRD, :] += folds[1][0]
            out_ref[even, THIRD:TIP, :] += folds[2][0][:QUARTER, :]
            out_ref[odd, :LANE, :] += parts[0][:, 2 * LANE :]
            out_ref[odd, LANE : 2 * LANE, :] += parts[1][:, LANE:]
            out_ref[odd, THIRD:TIP, :] += folds[2][0][QUARTER:, :]


def gram(first, kept, groups, prior=()):
    counts = [(g.shape[0] - TAG) // BLOCK for g in groups]
    return pl.pallas_call(
        lambda *refs: gram_kernel(*refs, counts=counts, kept=kept),
        in_specs=[pl.BlockSpec(memory_space=pltpu.SMEM)]
        + [pl.BlockSpec(memory_space=pltpu.VMEM)] * (len(groups) + len(prior)),
        out_specs=pl.BlockSpec(memory_space=pltpu.VMEM),
        out_shape=pltpu.VMEM((2 * kept, TIP + 8, LANE), F32),
        compiler_params=pltpu.CompilerParams(vmem_limit_bytes=VMEM_BYTES),
        name="gram",
    )(first, *[near(x) for x in (*groups, *prior)])


def factor_strip(groups, lane0, sub):
    wide = lambda v: jnp.concatenate([v] * (groups[0].shape[1] // LANE), axis=1)
    groups = list(groups)
    wide_sub = wide(sub)
    for b in range(len(groups)):
        base = lane0 + 8 * b
        cols = [
            [jnp.broadcast_to(g[:, base + j : base + j + 1], (8, LANE)) for g in groups[b:]]
            for j in range(8)
        ]
        for k in range(8):
            inv = lax.rsqrt(cols[k][0][k : k + 1, :])
            row = groups[b][k : k + 1, :] * wide(inv)
            mult = [jnp.where(sub > k, cols[k][0], 0.0)] + cols[k][1:]
            mult = [c * inv for c in mult]
            for g, m in enumerate(mult):
                groups[b + g] = groups[b + g] - wide(m) * row
            groups[b] = jnp.where(wide_sub == k, row, groups[b])
            for j in range(k + 1, 8):
                top = cols[j][0][k : k + 1, :] * inv
                cols[j] = [c - m * top for c, m in zip(cols[j], mult)]
    return groups


def dot_high(a, b, dims):
    return lax.dot_general(a, b, dims, precision=HIGH, preferred_element_type=F32)


def factor_panel(work):
    sub = lax.broadcasted_iota(jnp.int32, (8, LANE), 0)
    lane = lax.broadcasted_iota(jnp.int32, (8, LANE), 1)
    width = work.shape[1]
    for r0 in range(0, LANE, STRIP):
        r1 = r0 + STRIP
        groups = factor_strip([work[r : r + 8, :] for r in range(r0, r1, 8)], r0, sub)
        diag = jnp.concatenate(
            [
                jnp.where(lane >= r0 + 8 * g + sub, rows[:, :LANE], 0.0)
                for g, rows in enumerate(groups)
            ],
            axis=0,
        )
        strip = diag
        if width > LANE:
            right = jnp.concatenate([rows[:, LANE:] for rows in groups], axis=0)
            strip = jnp.concatenate([diag, right], axis=1)
        work[r0:r1, :] = strip
        if r1 < LANE:
            work[r1:, :] = work[r1:, :] - dot_high(diag.T[r1:, :], strip, NN)


def identity_tile():
    shape = (LANE, LANE)
    rows, cols = (lax.broadcasted_iota(jnp.int32, shape, axis) for axis in range(2))
    return jnp.where(rows == cols, 1.0, 0.0)


def diagonal(folded, corner, scale):
    return unfold(folded * scale, corner * scale) + RIDGE * identity_tile()


def first_kernel(part_ref, top_ref, mid_ref, *, scale):
    tip = lambda i: part_ref[TIP + i : TIP + i + 1, :]
    top_ref[:, :LANE] = diagonal(part_ref[:HALF, :], tip(0), scale)
    top_ref[:, LANE : 2 * LANE] = part_ref[HALF:SECOND, :] * scale
    top_ref[:, 2 * LANE :] = identity_tile()
    factor_panel(top_ref)
    side = top_ref[:, LANE : 2 * LANE]
    mid_ref[:, :LANE] = diagonal(part_ref[SECOND:THIRD, :], tip(1), scale) - dot_high(side, side, TN)
    mid_ref[:, LANE:] = identity_tile()
    factor_panel(mid_ref)


def first_panels(part, scale):
    return pl.pallas_call(
        lambda *refs: first_kernel(*refs, scale=scale),
        out_shape=[pltpu.VMEM((LANE, 3 * LANE), F32), pltpu.VMEM((LANE, 2 * LANE), F32)],
        compiler_params=pltpu.CompilerParams(vmem_limit_bytes=VMEM_BYTES),
        name="first_panels",
    )(near(part))


def last_kernel(part_ref, other_ref, top_ref, mid_ref, out_ref, low, *, scale):
    right = dot_high(top_ref[:, 2 * LANE :], other_ref[:LANE, :] * scale, NN)
    rest = other_ref[LANE : 2 * LANE, :] * scale - dot_high(top_ref[:, LANE : 2 * LANE], right, TN)
    below = dot_high(mid_ref[:, LANE:], rest, NN)
    folded = jnp.concatenate([part_ref[THIRD:TIP, :], other_ref[THIRD:TIP, :]], axis=0)
    low[...] = (
        diagonal(folded, part_ref[TIP + 2 : TIP + 3, :], scale)
        - dot_high(right, right, TN)
        - dot_high(below, below, TN)
    )
    factor_panel(low)
    kind = out_ref.dtype
    out_ref[:LANE, : 2 * LANE] = top_ref[:, : 2 * LANE].astype(kind)
    out_ref[:LANE, 2 * LANE :] = right.astype(kind)
    out_ref[LANE : 2 * LANE, :LANE] = jnp.zeros((LANE, LANE), kind)
    out_ref[LANE : 2 * LANE, LANE : 2 * LANE] = mid_ref[:, :LANE].astype(kind)
    out_ref[LANE : 2 * LANE, 2 * LANE :] = below.astype(kind)
    out_ref[2 * LANE :, : 2 * LANE] = jnp.zeros((LANE, 2 * LANE), kind)
    out_ref[2 * LANE :, 2 * LANE :] = low[...].astype(kind)


def last_panel(part, other, top, mid, scale):
    width = top.shape[1]
    return pl.pallas_call(
        lambda *refs: last_kernel(*refs, scale=scale),
        out_shape=pltpu.VMEM((width, width), BF16),
        scratch_shapes=[pltpu.VMEM((LANE, LANE), F32)],
        compiler_params=pltpu.CompilerParams(vmem_limit_bytes=VMEM_BYTES),
        name="last_panel",
    )(near(part), near(other), near(top), near(mid))


def on_device(tokens, block_expert, gate_weight, up_weight):
    owners = lax.axis_size("expert")
    replicas = lax.axis_size("dp")
    experts_each, _, hidden_width = gate_weight.shape
    chips = owners // 2
    shifts = [(0, 0), (0, 1)] + [(dy, dc) for dc in range(2) for dy in (1, chips - 1)]
    shifts += [(2, 0), (2, 1)]
    member = lax.axis_index("expert").reshape(1)
    outgoing = pack(block_expert, member, tokens, experts_each, shifts, chips)
    pairs = [(d, d ^ 1) for d in range(replicas)]
    arrived, gathered = [], []
    weights = bring(outgoing[0], gate_weight, up_weight)

    def swap_rows(g):
        rows = hidden_rows(arrived[EDGES[g] : EDGES[g + 1]], *weights)
        gathered.append([rows, lax.ppermute(rows, "dp", pairs)])

    def send(payload, dy, dc):
        route = [
            (y * 2 + c, ((y + dy) % chips) * 2 + (c + dc) % 2)
            for y in range(chips)
            for c in range(2)
        ]
        return lax.ppermute(payload, "expert", route)

    half_way = {}
    for slot, step in ((6, 1), (7, -1)):
        half_way[slot] = send(outgoing[slot], step, 0)
    for slot, (dy, dc) in enumerate(shifts):
        if slot == 0:
            arrived.append(outgoing[0])
        elif slot in half_way:
            arrived.append(send(half_way[slot], 1 if slot == 6 else -1, dc))
        else:
            arrived.append(send(outgoing[slot], dy, dc))
    for g in range(len(EDGES) - 1):
        swap_rows(g)
    kept = experts_each // 2
    first = (lax.axis_index("dp") % 2 * kept).reshape(1)
    partial_gram = gram(first, kept, [rows for pair in gathered[:-1] for rows in pair])
    partial_gram = gram(first, kept, gathered[-1], (partial_gram,))
    side = replicas // SIDE
    classes = [[x * SIDE + z for z in range(p, SIDE, 2) for x in range(side)] for p in range(2)]
    pieces = lax.all_to_all(
        partial_gram, "dp", split_axis=0, concat_axis=0, axis_index_groups=classes, tiled=True
    )
    own = jnp.sum(pieces, axis=0)
    halves = [(d + SIDE, d) for d in range(replicas) if d // SIDE % 2 == 0]
    other = lax.ppermute(own[:TIP], "dp", halves)
    scale = experts_each / (tokens.shape[0] * replicas)
    top, mid = first_panels(own, scale)
    result = last_panel(own, other, top, mid, scale)
    row_count = hidden_width // replicas
    sent = result.reshape(replicas, row_count, hidden_width)
    returned = lax.all_to_all(sent, "dp", split_axis=0, concat_axis=0, tiled=True)
    returned = returned.reshape(2, 2, 2, 2, row_count, hidden_width)[:, 0]
    returned = jnp.transpose(returned, (2, 1, 0, 3, 4))
    returned = returned.reshape(experts_each, row_count, hidden_width)
    return returned.astype(F32)


def solution(mesh):
    placed = (
        P(("dp", "expert"), None),
        P(("dp", "expert")),
        P("expert", None, None),
        P("expert", None, None),
    )

    return jax.shard_map(
        on_device, mesh=mesh, in_specs=placed, out_specs=P("expert", "dp", None), check_vma=False
    )
```

```python
import jax
import jax.numpy as jnp
from jax import lax
from jax.experimental import pallas as pl
from jax.experimental.pallas import tpu as pltpu
from jax.sharding import PartitionSpec as P


BLOCK = 128
RIDGE = 0.05
LANE = 128
TAG = 16
SIDE = 4
VMEM_BYTES = 20 << 20
EDGES = (0, 2, 4, 6, 7, 8)
STRIP = 64
F32 = jnp.float32
BF16 = jnp.bfloat16
HIGH = lax.Precision.HIGHEST
TN = (((0,), (0,)), ((), ()))
NN = (((1,), (0,)), ((), ()))
HALF = 64
QUARTER = 32
SECOND = HALF + LANE
THIRD = SECOND + HALF
TIP = THIRD + QUARTER


def near(x):
    return pltpu.with_memory_space_constraint(x, pltpu.VMEM)


def far(x):
    return pltpu.with_memory_space_constraint(x, pltpu.HBM)


def pack_kernel(member_ref, assign_hbm, tok_hbm, *rest, experts_each, shifts, chips):
    outs = rest[: len(shifts)]
    assign_ref, tok_ref, sem = rest[len(shifts) :]
    blocks, chunks = tok_ref.shape[0] // BLOCK, tok_ref.shape[1] // LANE
    fetch = [
        pltpu.make_async_copy(assign_hbm, assign_ref, sem.at[0]),
        pltpu.make_async_copy(tok_hbm, tok_ref, sem.at[1]),
    ]
    for copy in fetch:
        copy.start()
    for copy in fetch:
        copy.wait()
    chip = lax.div(member_ref[0], 2)
    core = lax.rem(member_ref[0], 2)
    for (dy, dc), out in zip(shifts, outs):
        dest = lax.rem(chip + dy, chips) * 2 + lax.rem(core + dc, 2)
        block = jnp.int32(0)
        code = jnp.int32(0)
        for b in range(blocks):
            expert = assign_ref[b]
            owner = lax.div(expert, experts_each)
            hit = owner == dest
            block = jnp.where(hit, b, block)
            code = jnp.where(hit, expert - owner * experts_each + 1, code)
        row = pl.multiple_of(block * BLOCK, BLOCK)
        for c in range(chunks):
            out[c * BLOCK : (c + 1) * BLOCK, :] = tok_ref[
                pl.ds(row, BLOCK), c * LANE : (c + 1) * LANE
            ]
        out[chunks * BLOCK :, :] = jnp.full((TAG, LANE), code.astype(F32), F32).astype(BF16)


def pack(assign, member, tokens, experts_each, shifts, chips):
    rows = BLOCK * tokens.shape[1] // LANE + TAG
    return pl.pallas_call(
        lambda *refs: pack_kernel(*refs, experts_each=experts_each, shifts=shifts, chips=chips),
        in_specs=[pl.BlockSpec(memory_space=pltpu.SMEM)]
        + [pl.BlockSpec(memory_space=pl.ANY)] * 2,
        out_specs=[pl.BlockSpec(memory_space=pltpu.VMEM)] * len(shifts),
        out_shape=[pltpu.VMEM((rows, LANE), BF16)] * len(shifts),
        scratch_shapes=[
            pltpu.SMEM(assign.shape, assign.dtype),
            pltpu.VMEM(tokens.shape, tokens.dtype),
            pltpu.SemaphoreType.DMA((2,)),
        ],
        compiler_params=pltpu.CompilerParams(vmem_limit_bytes=VMEM_BYTES),
        name="pack",
    )(member, far(assign), far(tokens))


def hidden_kernel(*refs, slots, model_width, fetch):
    xs = refs[:slots]
    gate_ref, up_ref, out_ref = refs[slots : slots + 3]
    chunks = model_width // LANE
    codes = []
    for s in range(slots):
        tag = xs[s][chunks * BLOCK : chunks * BLOCK + TAG, :].astype(F32)
        codes.append(jnp.max(tag).astype(jnp.int32))
    experts = [jnp.maximum(code - 1, 0) for code in codes]
    if fetch:
        gate_buf, up_buf, sem = refs[slots + 3 :]
        copies = []
        for s in range(slots):
            copies.append(
                (
                    pltpu.make_async_copy(gate_ref.at[experts[s]], gate_buf.at[s], sem.at[0, s]),
                    pltpu.make_async_copy(up_ref.at[experts[s]], up_buf.at[s], sem.at[1, s]),
                )
            )
            for copy in copies[-1]:
                copy.start()

    width = out_ref.shape[1]
    lane = lax.broadcasted_iota(jnp.int32, (TAG, width), 1)
    tags = jnp.zeros((TAG, width), F32)
    for s in range(slots):
        tags = jnp.where(lane == s, codes[s].astype(F32), tags)
    out_ref[slots * BLOCK :, :] = tags.astype(BF16)
    for s in range(slots):
        if fetch:
            for copy in copies[s]:
                copy.wait()

        @pl.when(codes[s] > 0)
        def _(s=s):
            x = jnp.concatenate(
                [xs[s][c * BLOCK : (c + 1) * BLOCK, :] for c in range(chunks)], axis=1
            )
            gate_part = gate_buf[s] if fetch else gate_ref[experts[s]]
            up_part = up_buf[s] if fetch else up_ref[experts[s]]
            gate = jnp.dot(x, gate_part, preferred_element_type=F32)
            up = jnp.dot(x, up_part, preferred_element_type=F32)
            hidden = gate / (1.0 + jnp.exp(-gate)) * up
            out_ref[s * BLOCK : (s + 1) * BLOCK, :] = hidden.astype(BF16)


def hidden_rows(arrived, gate_weight, up_weight, fetch=False):
    slots = len(arrived)
    _, model_width, hidden_width = gate_weight.shape
    place = far if fetch else near
    held = [pltpu.VMEM((slots, model_width, hidden_width), BF16)] * 2
    return pl.pallas_call(
        lambda *refs: hidden_kernel(*refs, slots=slots, model_width=model_width, fetch=fetch),
        in_specs=[pl.BlockSpec(memory_space=pltpu.VMEM)] * slots
        + [pl.BlockSpec(memory_space=pl.ANY if fetch else pltpu.VMEM)] * 2,
        out_specs=pl.BlockSpec(memory_space=pltpu.VMEM),
        out_shape=pltpu.VMEM((slots * BLOCK + TAG, hidden_width), BF16),
        scratch_shapes=held + [pltpu.SemaphoreType.DMA((2, slots))] if fetch else [],
        compiler_params=pltpu.CompilerParams(vmem_limit_bytes=VMEM_BYTES),
        name="hidden",
    )(*[near(x) for x in arrived], place(gate_weight), place(up_weight))


def bring_kernel(_, gate_ref, up_ref, gate_out, up_out, sem):
    copies = [
        pltpu.make_async_copy(gate_ref, gate_out, sem.at[0]),
        pltpu.make_async_copy(up_ref, up_out, sem.at[1]),
    ]
    for copy in copies:
        copy.start()
    for copy in copies:
        copy.wait()


def bring(after, gate_weight, up_weight):
    return pl.pallas_call(
        bring_kernel,
        in_specs=[pl.BlockSpec(memory_space=pl.ANY)] * 3,
        out_specs=[pl.BlockSpec(memory_space=pltpu.VMEM)] * 2,
        out_shape=[pltpu.VMEM(w.shape, w.dtype) for w in (gate_weight, up_weight)],
        scratch_shapes=[pltpu.SemaphoreType.DMA((2,))],
        compiler_params=pltpu.CompilerParams(vmem_limit_bytes=VMEM_BYTES),
        name="bring",
    )(after, far(gate_weight), far(up_weight))


def fold(tile):
    row = lax.broadcasted_iota(jnp.int32, (HALF, LANE), 0)
    lane = lax.broadcasted_iota(jnp.int32, (HALF, LANE), 1)
    upper, lower = tile[:HALF, :], tile[HALF:, :]
    folded = jnp.where((lane < HALF) & (lane < row), pltpu.roll(lower, HALF, 1), upper)
    corner = jnp.sum(jnp.where(lane == row + HALF, lower, 0.0), axis=0, keepdims=True)
    return folded, corner


def unfold(folded, corner):
    row = lax.broadcasted_iota(jnp.int32, (HALF, LANE), 0)
    lane = lax.broadcasted_iota(jnp.int32, (HALF, LANE), 1)
    flipped = jnp.concatenate([folded, jnp.zeros((HALF, LANE), F32)], axis=0).T
    upper = jnp.where(lane < row, flipped[:HALF, :], folded)
    below, above = pltpu.roll(folded, HALF, 1), pltpu.roll(flipped[:HALF, :], HALF, 1)
    inner = jnp.where(lane - HALF < row, below, jnp.where(lane - HALF == row, corner, above))
    return jnp.concatenate([upper, jnp.where(lane < HALF, flipped[HALF:, :], inner)], axis=0)


def gram_kernel(first_ref, *refs, counts, kept):
    groups, out_ref = refs[: len(counts)], refs[-1]
    out_ref[...] = refs[-2][...] if len(refs) > len(counts) + 1 else jnp.zeros(out_ref.shape, F32)
    lane = lax.broadcasted_iota(jnp.int32, (TAG, LANE), 1)
    where = [(ref, s, n) for ref, n in zip(groups, counts) for s in range(n)]
    codes = []
    for ref, s, n in where:
        tag = ref[n * BLOCK : n * BLOCK + TAG, :LANE].astype(F32)
        codes.append(jnp.max(jnp.where(lane == s, tag, 0.0)).astype(jnp.int32))
    for code, (ref, s, n) in zip(codes, where):
        local = code - 1 - first_ref[0]

        @pl.when((local >= 0) & (local < kept))
        def _(ref=ref, s=s, local=local):
            hidden = ref[s * BLOCK : (s + 1) * BLOCK, :]
            even, odd = 2 * local, 2 * local + 1
            parts = [
                lax.dot_general(
                    hidden[:, i * LANE : (i + 1) * LANE],
                    hidden[:, i * LANE :],
                    TN,
                    preferred_element_type=F32,
                )
                for i in range(3)
            ]
            folds = [fold(part[:, :LANE]) for part in parts]
            for i, (_, corner) in enumerate(folds):
                out_ref[even, TIP + i : TIP + i + 1, :] += corner
            out_ref[even, :HALF, :] += folds[0][0]
            out_ref[even, HALF:SECOND, :] += parts[0][:, LANE : 2 * LANE]
            out_ref[even, SECOND:THIRD, :] += folds[1][0]
            out_ref[even, THIRD:TIP, :] += folds[2][0][:QUARTER, :]
            out_ref[odd, :LANE, :] += parts[0][:, 2 * LANE :]
            out_ref[odd, LANE : 2 * LANE, :] += parts[1][:, LANE:]
            out_ref[odd, THIRD:TIP, :] += folds[2][0][QUARTER:, :]


def gram(first, kept, groups, prior=()):
    counts = [(g.shape[0] - TAG) // BLOCK for g in groups]
    return pl.pallas_call(
        lambda *refs: gram_kernel(*refs, counts=counts, kept=kept),
        in_specs=[pl.BlockSpec(memory_space=pltpu.SMEM)]
        + [pl.BlockSpec(memory_space=pltpu.VMEM)] * (len(groups) + len(prior)),
        out_specs=pl.BlockSpec(memory_space=pltpu.VMEM),
        out_shape=pltpu.VMEM((2 * kept, TIP + 8, LANE), F32),
        compiler_params=pltpu.CompilerParams(vmem_limit_bytes=VMEM_BYTES),
        name="gram",
    )(first, *[near(x) for x in (*groups, *prior)])


def factor_strip(groups, lane0, sub):
    wide = lambda v: jnp.concatenate([v] * (groups[0].shape[1] // LANE), axis=1)
    groups = list(groups)
    wide_sub = wide(sub)
    for b in range(len(groups)):
        base = lane0 + 8 * b
        cols = [
            [jnp.broadcast_to(g[:, base + j : base + j + 1], (8, LANE)) for g in groups[b:]]
            for j in range(8)
        ]
        for k in range(8):
            inv = lax.rsqrt(cols[k][0][k : k + 1, :])
            row = groups[b][k : k + 1, :] * wide(inv)
            mult = [jnp.where(sub > k, cols[k][0], 0.0)] + cols[k][1:]
            mult = [c * inv for c in mult]
            for g, m in enumerate(mult):
                groups[b + g] = groups[b + g] - wide(m) * row
            groups[b] = jnp.where(wide_sub == k, row, groups[b])
            for j in range(k + 1, 8):
                top = cols[j][0][k : k + 1, :] * inv
                cols[j] = [c - m * top for c, m in zip(cols[j], mult)]
    return groups


def dot_high(a, b, dims):
    return lax.dot_general(a, b, dims, precision=HIGH, preferred_element_type=F32)


def factor_panel(work):
    sub = lax.broadcasted_iota(jnp.int32, (8, LANE), 0)
    lane = lax.broadcasted_iota(jnp.int32, (8, LANE), 1)
    width = work.shape[1]
    for r0 in range(0, LANE, STRIP):
        r1 = r0 + STRIP
        groups = factor_strip([work[r : r + 8, :] for r in range(r0, r1, 8)], r0, sub)
        diag = jnp.concatenate(
            [
                jnp.where(lane >= r0 + 8 * g + sub, rows[:, :LANE], 0.0)
                for g, rows in enumerate(groups)
            ],
            axis=0,
        )
        strip = diag
        if width > LANE:
            right = jnp.concatenate([rows[:, LANE:] for rows in groups], axis=0)
            strip = jnp.concatenate([diag, right], axis=1)
        work[r0:r1, :] = strip
        if r1 < LANE:
            work[r1:, :] = work[r1:, :] - dot_high(diag.T[r1:, :], strip, NN)


def identity_tile():
    shape = (LANE, LANE)
    rows, cols = (lax.broadcasted_iota(jnp.int32, shape, axis) for axis in range(2))
    return jnp.where(rows == cols, 1.0, 0.0)


def diagonal(folded, corner, scale):
    return unfold(folded * scale, corner * scale) + RIDGE * identity_tile()


def first_kernel(part_ref, top_ref, mid_ref, *, scale):
    tip = lambda i: part_ref[TIP + i : TIP + i + 1, :]
    top_ref[:, :LANE] = diagonal(part_ref[:HALF, :], tip(0), scale)
    top_ref[:, LANE : 2 * LANE] = part_ref[HALF:SECOND, :] * scale
    top_ref[:, 2 * LANE :] = identity_tile()
    factor_panel(top_ref)
    side = top_ref[:, LANE : 2 * LANE]
    mid_ref[:, :LANE] = diagonal(part_ref[SECOND:THIRD, :], tip(1), scale) - dot_high(side, side, TN)
    mid_ref[:, LANE:] = identity_tile()
    factor_panel(mid_ref)


def first_panels(part, scale):
    return pl.pallas_call(
        lambda *refs: first_kernel(*refs, scale=scale),
        out_shape=[pltpu.VMEM((LANE, 3 * LANE), F32), pltpu.VMEM((LANE, 2 * LANE), F32)],
        compiler_params=pltpu.CompilerParams(vmem_limit_bytes=VMEM_BYTES),
        name="first_panels",
    )(near(part))


def last_kernel(part_ref, other_ref, top_ref, mid_ref, out_ref, low, *, scale):
    right = dot_high(top_ref[:, 2 * LANE :], other_ref[:LANE, :] * scale, NN)
    rest = other_ref[LANE : 2 * LANE, :] * scale - dot_high(top_ref[:, LANE : 2 * LANE], right, TN)
    below = dot_high(mid_ref[:, LANE:], rest, NN)
    folded = jnp.concatenate([part_ref[THIRD:TIP, :], other_ref[THIRD:TIP, :]], axis=0)
    low[...] = (
        diagonal(folded, part_ref[TIP + 2 : TIP + 3, :], scale)
        - dot_high(right, right, TN)
        - dot_high(below, below, TN)
    )
    factor_panel(low)
    kind = out_ref.dtype
    out_ref[:LANE, : 2 * LANE] = top_ref[:, : 2 * LANE].astype(kind)
    out_ref[:LANE, 2 * LANE :] = right.astype(kind)
    out_ref[LANE : 2 * LANE, :LANE] = jnp.zeros((LANE, LANE), kind)
    out_ref[LANE : 2 * LANE, LANE : 2 * LANE] = mid_ref[:, :LANE].astype(kind)
    out_ref[LANE : 2 * LANE, 2 * LANE :] = below.astype(kind)
    out_ref[2 * LANE :, : 2 * LANE] = jnp.zeros((LANE, 2 * LANE), kind)
    out_ref[2 * LANE :, 2 * LANE :] = low[...].astype(kind)


def last_panel(part, other, top, mid, scale):
    width = top.shape[1]
    return pl.pallas_call(
        lambda *refs: last_kernel(*refs, scale=scale),
        out_shape=pltpu.VMEM((width, width), BF16),
        scratch_shapes=[pltpu.VMEM((LANE, LANE), F32)],
        compiler_params=pltpu.CompilerParams(vmem_limit_bytes=VMEM_BYTES),
        name="last_panel",
    )(near(part), near(other), near(top), near(mid))


def on_device(tokens, block_expert, gate_weight, up_weight):
    owners = lax.axis_size("expert")
    replicas = lax.axis_size("dp")
    experts_each, _, hidden_width = gate_weight.shape
    chips = owners // 2
    shifts = [(0, 0), (0, 1)] + [(dy, dc) for dc in range(2) for dy in (1, chips - 1)]
    shifts += [(2, 0), (2, 1)]
    member = lax.axis_index("expert").reshape(1)
    outgoing = pack(block_expert, member, tokens, experts_each, shifts, chips)
    pairs = [(d, d ^ 1) for d in range(replicas)]
    arrived, gathered = [], []
    weights = (gate_weight, up_weight)

    def swap_rows(g):
        rows = hidden_rows(arrived[EDGES[g] : EDGES[g + 1]], *weights, fetch=g == 0)
        gathered.append([rows, lax.ppermute(rows, "dp", pairs)])

    for (dy, dc), payload in zip(shifts, outgoing):
        route = [
            (y * 2 + c, ((y + dy) % chips) * 2 + (c + dc) % 2)
            for y in range(chips)
            for c in range(2)
        ]
        if dy == 2 and not gathered:
            swap_rows(0)
            weights = bring(gathered[0][0], gate_weight, up_weight)
        if dy == 2:
            payload, _ = lax.optimization_barrier((payload, gathered[0][0]))
        arrived.append(payload if dy == dc == 0 else lax.ppermute(payload, "expert", route))
    for g in range(1, len(EDGES) - 1):
        swap_rows(g)
    kept = experts_each // 2
    first = (lax.axis_index("dp") % 2 * kept).reshape(1)
    partial_gram = gram(first, kept, [rows for pair in gathered[:-2] for rows in pair])
    tail = [rows for pair in gathered[-2:] for rows in pair]
    partial_gram = gram(first, kept, tail, (partial_gram,))
    side = replicas // SIDE
    classes = [[x * SIDE + z for z in range(p, SIDE, 2) for x in range(side)] for p in range(2)]
    pieces = lax.all_to_all(
        partial_gram, "dp", split_axis=0, concat_axis=0, axis_index_groups=classes, tiled=True
    )
    own = jnp.sum(pieces, axis=0)
    halves = [(d + SIDE, d) for d in range(replicas) if d // SIDE % 2 == 0]
    other = lax.ppermute(own[:TIP], "dp", halves)
    scale = experts_each / (tokens.shape[0] * replicas)
    top, mid = first_panels(own, scale)
    result = last_panel(own, other, top, mid, scale)
    row_count = hidden_width // replicas
    sent = result.reshape(replicas, row_count, hidden_width)
    returned = lax.all_to_all(sent, "dp", split_axis=0, concat_axis=0, tiled=True)
    returned = returned.reshape(2, 2, 2, 2, row_count, hidden_width)[:, 0]
    returned = jnp.transpose(returned, (2, 1, 0, 3, 4))
    returned = returned.reshape(experts_each, row_count, hidden_width)
    return returned.astype(F32)


def solution(mesh):
    placed = (
        P(("dp", "expert"), None),
        P(("dp", "expert")),
        P("expert", None, None),
        P("expert", None, None),
    )

    return jax.shard_map(
        on_device, mesh=mesh, in_specs=placed, out_specs=P("expert", "dp", None), check_vma=False
    )
```

```python
import jax
import jax.numpy as jnp
from jax import lax
from jax.experimental import pallas as pl
from jax.experimental.pallas import tpu as pltpu
from jax.sharding import PartitionSpec as P


BLOCK = 128
RIDGE = 0.05
LANE = 128
TAG = 16
SIDE = 4
VMEM_BYTES = 20 << 20
EDGES = (0, 2, 4, 6, 7, 8)
STRIP = 64
F32 = jnp.float32
BF16 = jnp.bfloat16
HIGH = lax.Precision.HIGHEST
TN = (((0,), (0,)), ((), ()))
NN = (((1,), (0,)), ((), ()))
HALF = 64
QUARTER = 32
SECOND = HALF + LANE
THIRD = SECOND + HALF
TIP = THIRD + QUARTER


def near(x):
    return pltpu.with_memory_space_constraint(x, pltpu.VMEM)


def far(x):
    return pltpu.with_memory_space_constraint(x, pltpu.HBM)


def pack_kernel(member_ref, assign_hbm, tok_hbm, *rest, experts_each, shifts, chips):
    outs = rest[: len(shifts)]
    assign_ref, tok_ref, sem = rest[len(shifts) :]
    blocks, chunks = tok_ref.shape[0] // BLOCK, tok_ref.shape[1] // LANE
    fetch = [
        pltpu.make_async_copy(assign_hbm, assign_ref, sem.at[0]),
        pltpu.make_async_copy(tok_hbm, tok_ref, sem.at[1]),
    ]
    for copy in fetch:
        copy.start()
    for copy in fetch:
        copy.wait()
    chip = lax.div(member_ref[0], 2)
    core = lax.rem(member_ref[0], 2)
    for (dy, dc), out in zip(shifts, outs):
        dest = lax.rem(chip + dy, chips) * 2 + lax.rem(core + dc, 2)
        block = jnp.int32(0)
        code = jnp.int32(0)
        for b in range(blocks):
            expert = assign_ref[b]
            owner = lax.div(expert, experts_each)
            hit = owner == dest
            block = jnp.where(hit, b, block)
            code = jnp.where(hit, expert - owner * experts_each + 1, code)
        row = pl.multiple_of(block * BLOCK, BLOCK)
        for c in range(chunks):
            out[c * BLOCK : (c + 1) * BLOCK, :] = tok_ref[
                pl.ds(row, BLOCK), c * LANE : (c + 1) * LANE
            ]
        out[chunks * BLOCK :, :] = jnp.full((TAG, LANE), code.astype(F32), F32).astype(BF16)


def pack(assign, member, tokens, experts_each, shifts, chips):
    rows = BLOCK * tokens.shape[1] // LANE + TAG
    return pl.pallas_call(
        lambda *refs: pack_kernel(*refs, experts_each=experts_each, shifts=shifts, chips=chips),
        in_specs=[pl.BlockSpec(memory_space=pltpu.SMEM)]
        + [pl.BlockSpec(memory_space=pl.ANY)] * 2,
        out_specs=[pl.BlockSpec(memory_space=pltpu.VMEM)] * len(shifts),
        out_shape=[pltpu.VMEM((rows, LANE), BF16)] * len(shifts),
        scratch_shapes=[
            pltpu.SMEM(assign.shape, assign.dtype),
            pltpu.VMEM(tokens.shape, tokens.dtype),
            pltpu.SemaphoreType.DMA((2,)),
        ],
        compiler_params=pltpu.CompilerParams(vmem_limit_bytes=VMEM_BYTES),
        name="pack",
    )(member, far(assign), far(tokens))


def hidden_kernel(*refs, slots, model_width, fetch):
    xs = refs[:slots]
    gate_ref, up_ref, out_ref = refs[slots : slots + 3]
    chunks = model_width // LANE
    codes = []
    for s in range(slots):
        tag = xs[s][chunks * BLOCK : chunks * BLOCK + TAG, :].astype(F32)
        codes.append(jnp.max(tag).astype(jnp.int32))
    experts = [jnp.maximum(code - 1, 0) for code in codes]
    if fetch:
        gate_buf, up_buf, sem = refs[slots + 3 :]
        copies = []
        for s in range(slots):
            copies.append(
                (
                    pltpu.make_async_copy(gate_ref.at[experts[s]], gate_buf.at[s], sem.at[0, s]),
                    pltpu.make_async_copy(up_ref.at[experts[s]], up_buf.at[s], sem.at[1, s]),
                )
            )
            for copy in copies[-1]:
                copy.start()

    width = out_ref.shape[1]
    lane = lax.broadcasted_iota(jnp.int32, (TAG, width), 1)
    tags = jnp.zeros((TAG, width), F32)
    for s in range(slots):
        tags = jnp.where(lane == s, codes[s].astype(F32), tags)
    out_ref[slots * BLOCK :, :] = tags.astype(BF16)
    for s in range(slots):
        if fetch:
            for copy in copies[s]:
                copy.wait()

        @pl.when(codes[s] > 0)
        def _(s=s):
            x = jnp.concatenate(
                [xs[s][c * BLOCK : (c + 1) * BLOCK, :] for c in range(chunks)], axis=1
            )
            gate_part = gate_buf[s] if fetch else gate_ref[experts[s]]
            up_part = up_buf[s] if fetch else up_ref[experts[s]]
            gate = jnp.dot(x, gate_part, preferred_element_type=F32)
            up = jnp.dot(x, up_part, preferred_element_type=F32)
            hidden = gate / (1.0 + jnp.exp(-gate)) * up
            out_ref[s * BLOCK : (s + 1) * BLOCK, :] = hidden.astype(BF16)


def hidden_rows(arrived, gate_weight, up_weight, fetch=False):
    slots = len(arrived)
    _, model_width, hidden_width = gate_weight.shape
    place = far if fetch else near
    held = [pltpu.VMEM((slots, model_width, hidden_width), BF16)] * 2
    return pl.pallas_call(
        lambda *refs: hidden_kernel(*refs, slots=slots, model_width=model_width, fetch=fetch),
        in_specs=[pl.BlockSpec(memory_space=pltpu.VMEM)] * slots
        + [pl.BlockSpec(memory_space=pl.ANY if fetch else pltpu.VMEM)] * 2,
        out_specs=pl.BlockSpec(memory_space=pltpu.VMEM),
        out_shape=pltpu.VMEM((slots * BLOCK + TAG, hidden_width), BF16),
        scratch_shapes=held + [pltpu.SemaphoreType.DMA((2, slots))] if fetch else [],
        compiler_params=pltpu.CompilerParams(vmem_limit_bytes=VMEM_BYTES),
        name="hidden",
    )(*[near(x) for x in arrived], place(gate_weight), place(up_weight))


def bring_kernel(_, gate_ref, up_ref, gate_out, up_out, sem):
    copies = [
        pltpu.make_async_copy(gate_ref, gate_out, sem.at[0]),
        pltpu.make_async_copy(up_ref, up_out, sem.at[1]),
    ]
    for copy in copies:
        copy.start()
    for copy in copies:
        copy.wait()


def bring(after, gate_weight, up_weight):
    return pl.pallas_call(
        bring_kernel,
        in_specs=[pl.BlockSpec(memory_space=pl.ANY)] * 3,
        out_specs=[pl.BlockSpec(memory_space=pltpu.VMEM)] * 2,
        out_shape=[pltpu.VMEM(w.shape, w.dtype) for w in (gate_weight, up_weight)],
        scratch_shapes=[pltpu.SemaphoreType.DMA((2,))],
        compiler_params=pltpu.CompilerParams(vmem_limit_bytes=VMEM_BYTES),
        name="bring",
    )(after, far(gate_weight), far(up_weight))


def fold(tile):
    row = lax.broadcasted_iota(jnp.int32, (HALF, LANE), 0)
    lane = lax.broadcasted_iota(jnp.int32, (HALF, LANE), 1)
    upper, lower = tile[:HALF, :], tile[HALF:, :]
    folded = jnp.where((lane < HALF) & (lane < row), pltpu.roll(lower, HALF, 1), upper)
    corner = jnp.sum(jnp.where(lane == row + HALF, lower, 0.0), axis=0, keepdims=True)
    return folded, corner


def unfold(folded, corner):
    row = lax.broadcasted_iota(jnp.int32, (HALF, LANE), 0)
    lane = lax.broadcasted_iota(jnp.int32, (HALF, LANE), 1)
    flipped = jnp.concatenate([folded, jnp.zeros((HALF, LANE), F32)], axis=0).T
    upper = jnp.where(lane < row, flipped[:HALF, :], folded)
    below, above = pltpu.roll(folded, HALF, 1), pltpu.roll(flipped[:HALF, :], HALF, 1)
    inner = jnp.where(lane - HALF < row, below, jnp.where(lane - HALF == row, corner, above))
    return jnp.concatenate([upper, jnp.where(lane < HALF, flipped[HALF:, :], inner)], axis=0)


def gram_kernel(first_ref, *refs, counts, kept):
    groups, out_ref = refs[: len(counts)], refs[-1]
    out_ref[...] = refs[-2][...] if len(refs) > len(counts) + 1 else jnp.zeros(out_ref.shape, F32)
    lane = lax.broadcasted_iota(jnp.int32, (TAG, LANE), 1)
    where = [(ref, s, n) for ref, n in zip(groups, counts) for s in range(n)]
    codes = []
    for ref, s, n in where:
        tag = ref[n * BLOCK : n * BLOCK + TAG, :LANE].astype(F32)
        codes.append(jnp.max(jnp.where(lane == s, tag, 0.0)).astype(jnp.int32))
    for code, (ref, s, n) in zip(codes, where):
        local = code - 1 - first_ref[0]

        @pl.when((local >= 0) & (local < kept))
        def _(ref=ref, s=s, local=local):
            hidden = ref[s * BLOCK : (s + 1) * BLOCK, :]
            even, odd = 2 * local, 2 * local + 1
            parts = [
                lax.dot_general(
                    hidden[:, i * LANE : (i + 1) * LANE],
                    hidden[:, i * LANE :],
                    TN,
                    preferred_element_type=F32,
                )
                for i in range(3)
            ]
            folds = [fold(part[:, :LANE]) for part in parts]
            for i, (_, corner) in enumerate(folds):
                out_ref[even, TIP + i : TIP + i + 1, :] += corner
            out_ref[even, :HALF, :] += folds[0][0]
            out_ref[even, HALF:SECOND, :] += parts[0][:, LANE : 2 * LANE]
            out_ref[even, SECOND:THIRD, :] += folds[1][0]
            out_ref[even, THIRD:TIP, :] += folds[2][0][:QUARTER, :]
            out_ref[odd, :LANE, :] += parts[0][:, 2 * LANE :]
            out_ref[odd, LANE : 2 * LANE, :] += parts[1][:, LANE:]
            out_ref[odd, THIRD:TIP, :] += folds[2][0][QUARTER:, :]


def gram(first, kept, groups, prior=()):
    counts = [(g.shape[0] - TAG) // BLOCK for g in groups]
    return pl.pallas_call(
        lambda *refs: gram_kernel(*refs, counts=counts, kept=kept),
        in_specs=[pl.BlockSpec(memory_space=pltpu.SMEM)]
        + [pl.BlockSpec(memory_space=pltpu.VMEM)] * (len(groups) + len(prior)),
        out_specs=pl.BlockSpec(memory_space=pltpu.VMEM),
        out_shape=pltpu.VMEM((2 * kept, TIP + 8, LANE), F32),
        compiler_params=pltpu.CompilerParams(vmem_limit_bytes=VMEM_BYTES),
        name="gram",
    )(first, *[near(x) for x in (*groups, *prior)])


def factor_strip(groups, lane0, sub):
    wide = lambda v: jnp.concatenate([v] * (groups[0].shape[1] // LANE), axis=1)
    groups = list(groups)
    wide_sub = wide(sub)
    for b in range(len(groups)):
        base = lane0 + 8 * b
        cols = [
            [jnp.broadcast_to(g[:, base + j : base + j + 1], (8, LANE)) for g in groups[b:]]
            for j in range(8)
        ]
        for k in range(8):
            inv = lax.rsqrt(cols[k][0][k : k + 1, :])
            row = groups[b][k : k + 1, :] * wide(inv)
            mult = [jnp.where(sub > k, cols[k][0], 0.0)] + cols[k][1:]
            mult = [c * inv for c in mult]
            for g, m in enumerate(mult):
                groups[b + g] = groups[b + g] - wide(m) * row
            groups[b] = jnp.where(wide_sub == k, row, groups[b])
            for j in range(k + 1, 8):
                top = cols[j][0][k : k + 1, :] * inv
                cols[j] = [c - m * top for c, m in zip(cols[j], mult)]
    return groups


def dot_high(a, b, dims):
    return lax.dot_general(a, b, dims, precision=HIGH, preferred_element_type=F32)


def factor_panel(work):
    sub = lax.broadcasted_iota(jnp.int32, (8, LANE), 0)
    lane = lax.broadcasted_iota(jnp.int32, (8, LANE), 1)
    width = work.shape[1]
    for r0 in range(0, LANE, STRIP):
        r1 = r0 + STRIP
        groups = factor_strip([work[r : r + 8, :] for r in range(r0, r1, 8)], r0, sub)
        diag = jnp.concatenate(
            [
                jnp.where(lane >= r0 + 8 * g + sub, rows[:, :LANE], 0.0)
                for g, rows in enumerate(groups)
            ],
            axis=0,
        )
        strip = diag
        if width > LANE:
            right = jnp.concatenate([rows[:, LANE:] for rows in groups], axis=0)
            strip = jnp.concatenate([diag, right], axis=1)
        work[r0:r1, :] = strip
        if r1 < LANE:
            work[r1:, :] = work[r1:, :] - dot_high(diag.T[r1:, :], strip, NN)


def identity_tile():
    shape = (LANE, LANE)
    rows, cols = (lax.broadcasted_iota(jnp.int32, shape, axis) for axis in range(2))
    return jnp.where(rows == cols, 1.0, 0.0)


def diagonal(folded, corner, scale):
    return unfold(folded * scale, corner * scale) + RIDGE * identity_tile()


def first_kernel(part_ref, top_ref, mid_ref, *, scale):
    tip = lambda i: part_ref[TIP + i : TIP + i + 1, :]
    top_ref[:, :LANE] = diagonal(part_ref[:HALF, :], tip(0), scale)
    top_ref[:, LANE : 2 * LANE] = part_ref[HALF:SECOND, :] * scale
    top_ref[:, 2 * LANE :] = identity_tile()
    factor_panel(top_ref)
    side = top_ref[:, LANE : 2 * LANE]
    mid_ref[:, :LANE] = diagonal(part_ref[SECOND:THIRD, :], tip(1), scale) - dot_high(side, side, TN)
    mid_ref[:, LANE:] = identity_tile()
    factor_panel(mid_ref)


def first_panels(part, scale):
    return pl.pallas_call(
        lambda *refs: first_kernel(*refs, scale=scale),
        out_shape=[pltpu.VMEM((LANE, 3 * LANE), F32), pltpu.VMEM((LANE, 2 * LANE), F32)],
        compiler_params=pltpu.CompilerParams(vmem_limit_bytes=VMEM_BYTES),
        name="first_panels",
    )(near(part))


def last_kernel(part_ref, other_ref, top_ref, mid_ref, out_ref, low, *, scale):
    right = dot_high(top_ref[:, 2 * LANE :], other_ref[:LANE, :] * scale, NN)
    rest = other_ref[LANE : 2 * LANE, :] * scale - dot_high(top_ref[:, LANE : 2 * LANE], right, TN)
    below = dot_high(mid_ref[:, LANE:], rest, NN)
    folded = jnp.concatenate([part_ref[THIRD:TIP, :], other_ref[THIRD:TIP, :]], axis=0)
    low[...] = (
        diagonal(folded, part_ref[TIP + 2 : TIP + 3, :], scale)
        - dot_high(right, right, TN)
        - dot_high(below, below, TN)
    )
    factor_panel(low)
    kind = out_ref.dtype
    out_ref[:LANE, : 2 * LANE] = top_ref[:, : 2 * LANE].astype(kind)
    out_ref[:LANE, 2 * LANE :] = right.astype(kind)
    out_ref[LANE : 2 * LANE, :LANE] = jnp.zeros((LANE, LANE), kind)
    out_ref[LANE : 2 * LANE, LANE : 2 * LANE] = mid_ref[:, :LANE].astype(kind)
    out_ref[LANE : 2 * LANE, 2 * LANE :] = below.astype(kind)
    out_ref[2 * LANE :, : 2 * LANE] = jnp.zeros((LANE, 2 * LANE), kind)
    out_ref[2 * LANE :, 2 * LANE :] = low[...].astype(kind)


def last_panel(part, other, top, mid, scale):
    width = top.shape[1]
    return pl.pallas_call(
        lambda *refs: last_kernel(*refs, scale=scale),
        out_shape=pltpu.VMEM((width, width), BF16),
        scratch_shapes=[pltpu.VMEM((LANE, LANE), F32)],
        compiler_params=pltpu.CompilerParams(vmem_limit_bytes=VMEM_BYTES),
        name="last_panel",
    )(near(part), near(other), near(top), near(mid))


def on_device(tokens, block_expert, gate_weight, up_weight):
    owners = lax.axis_size("expert")
    replicas = lax.axis_size("dp")
    experts_each, _, hidden_width = gate_weight.shape
    chips = owners // 2
    shifts = [(0, 0), (0, 1)] + [(dy, dc) for dc in range(2) for dy in (1, chips - 1)]
    shifts += [(2, 0), (2, 1)]
    member = lax.axis_index("expert").reshape(1)
    outgoing = pack(block_expert, member, tokens, experts_each, shifts, chips)
    side = replicas // SIDE
    pairs = [(x * SIDE + z, (side - 1 - x) * SIDE + z) for x in range(side) for z in range(SIDE)]
    arrived, gathered = [], []
    weights = (gate_weight, up_weight)

    def swap_rows(g):
        rows = hidden_rows(arrived[EDGES[g] : EDGES[g + 1]], *weights, fetch=g == 0)
        gathered.append([rows, lax.ppermute(rows, "dp", pairs)])

    for (dy, dc), payload in zip(shifts, outgoing):
        route = [
            (y * 2 + c, ((y + dy) % chips) * 2 + (c + dc) % 2)
            for y in range(chips)
            for c in range(2)
        ]
        if dy == 2 and not gathered:
            swap_rows(0)
            weights = bring(gathered[0][0], gate_weight, up_weight)
        if dy == 2:
            payload, _ = lax.optimization_barrier((payload, gathered[0][0]))
        arrived.append(payload if dy == dc == 0 else lax.ppermute(payload, "expert", route))
    for g in range(1, len(EDGES) - 1):
        swap_rows(g)
    kept = experts_each // 2
    first = (lax.axis_index("dp") // (replicas // 2) * kept).reshape(1)
    partial_gram = gram(first, kept, [rows for pair in gathered[:-2] for rows in pair])
    tail = [rows for pair in gathered[-2:] for rows in pair]
    partial_gram = gram(first, kept, tail, (partial_gram,))
    classes = [
        [x * SIDE + z for z in range(SIDE) for x in (2 * p, 2 * p + 1)] for p in range(2)
    ]
    pieces = lax.all_to_all(
        partial_gram, "dp", split_axis=0, concat_axis=0, axis_index_groups=classes, tiled=True
    )
    own = jnp.sum(pieces, axis=0)
    halves = [(d + SIDE, d) for d in range(replicas) if d // SIDE % 2 == 0]
    other = lax.ppermute(own[:TIP], "dp", halves)
    scale = experts_each / (tokens.shape[0] * replicas)
    top, mid = first_panels(own, scale)
    result = last_panel(own, other, top, mid, scale)
    row_count = hidden_width // replicas
    sent = result.reshape(replicas, row_count, hidden_width)
    returned = lax.all_to_all(sent, "dp", split_axis=0, concat_axis=0, tiled=True)
    returned = returned.reshape(2, 2, SIDE, row_count, hidden_width)[:, 0]
    returned = returned.reshape(experts_each, row_count, hidden_width)
    return returned.astype(F32)


def solution(mesh):
    placed = (
        P(("dp", "expert"), None),
        P(("dp", "expert")),
        P("expert", None, None),
        P("expert", None, None),
    )

    return jax.shard_map(
        on_device, mesh=mesh, in_specs=placed, out_specs=P("expert", "dp", None), check_vma=False
    )
```

```python
import jax
import jax.numpy as jnp
from jax import lax
from jax.experimental import pallas as pl
from jax.experimental.pallas import tpu as pltpu
from jax.sharding import PartitionSpec as P


BLOCK = 128
RIDGE = 0.05
LANE = 128
TAG = 16
SIDE = 4
VMEM_BYTES = 20 << 20
EDGES = (0, 2, 6, 7, 8)
STRIP = 64
F32 = jnp.float32
BF16 = jnp.bfloat16
HIGH = lax.Precision.HIGHEST
TN = (((0,), (0,)), ((), ()))
NN = (((1,), (0,)), ((), ()))
HALF = 64
QUARTER = 32
SECOND = HALF + LANE
THIRD = SECOND + HALF
TIP = THIRD + QUARTER


def near(x):
    return pltpu.with_memory_space_constraint(x, pltpu.VMEM)


def far(x):
    return pltpu.with_memory_space_constraint(x, pltpu.HBM)


def pack_kernel(member_ref, assign_hbm, tok_hbm, *rest, experts_each, shifts, chips):
    outs = rest[: len(shifts)]
    assign_ref, tok_ref, sem = rest[len(shifts) :]
    blocks, chunks = tok_ref.shape[0] // BLOCK, tok_ref.shape[1] // LANE
    fetch = [
        pltpu.make_async_copy(assign_hbm, assign_ref, sem.at[0]),
        pltpu.make_async_copy(tok_hbm, tok_ref, sem.at[1]),
    ]
    for copy in fetch:
        copy.start()
    for copy in fetch:
        copy.wait()
    chip = lax.div(member_ref[0], 2)
    core = lax.rem(member_ref[0], 2)
    for (dy, dc), out in zip(shifts, outs):
        dest = lax.rem(chip + dy, chips) * 2 + lax.rem(core + dc, 2)
        block = jnp.int32(0)
        code = jnp.int32(0)
        for b in range(blocks):
            expert = assign_ref[b]
            owner = lax.div(expert, experts_each)
            hit = owner == dest
            block = jnp.where(hit, b, block)
            code = jnp.where(hit, expert - owner * experts_each + 1, code)
        row = pl.multiple_of(block * BLOCK, BLOCK)
        for c in range(chunks):
            out[c * BLOCK : (c + 1) * BLOCK, :] = tok_ref[
                pl.ds(row, BLOCK), c * LANE : (c + 1) * LANE
            ]
        out[chunks * BLOCK :, :] = jnp.full((TAG, LANE), code.astype(F32), F32).astype(BF16)


def pack(assign, member, tokens, experts_each, shifts, chips):
    rows = BLOCK * tokens.shape[1] // LANE + TAG
    return pl.pallas_call(
        lambda *refs: pack_kernel(*refs, experts_each=experts_each, shifts=shifts, chips=chips),
        in_specs=[pl.BlockSpec(memory_space=pltpu.SMEM)]
        + [pl.BlockSpec(memory_space=pl.ANY)] * 2,
        out_specs=[pl.BlockSpec(memory_space=pltpu.VMEM)] * len(shifts),
        out_shape=[pltpu.VMEM((rows, LANE), BF16)] * len(shifts),
        scratch_shapes=[
            pltpu.SMEM(assign.shape, assign.dtype),
            pltpu.VMEM(tokens.shape, tokens.dtype),
            pltpu.SemaphoreType.DMA((2,)),
        ],
        compiler_params=pltpu.CompilerParams(vmem_limit_bytes=VMEM_BYTES),
        name="pack",
    )(member, far(assign), far(tokens))


def hidden_kernel(*refs, slots, model_width, fetch):
    xs = refs[:slots]
    gate_ref, up_ref, out_ref = refs[slots : slots + 3]
    chunks = model_width // LANE
    codes = []
    for s in range(slots):
        tag = xs[s][chunks * BLOCK : chunks * BLOCK + TAG, :].astype(F32)
        codes.append(jnp.max(tag).astype(jnp.int32))
    experts = [jnp.maximum(code - 1, 0) for code in codes]
    if fetch:
        gate_buf, up_buf, sem = refs[slots + 3 :]
        copies = []
        for s in range(slots):
            copies.append(
                (
                    pltpu.make_async_copy(gate_ref.at[experts[s]], gate_buf.at[s], sem.at[0, s]),
                    pltpu.make_async_copy(up_ref.at[experts[s]], up_buf.at[s], sem.at[1, s]),
                )
            )
            for copy in copies[-1]:
                copy.start()

    width = out_ref.shape[1]
    lane = lax.broadcasted_iota(jnp.int32, (TAG, width), 1)
    tags = jnp.zeros((TAG, width), F32)
    for s in range(slots):
        tags = jnp.where(lane == s, codes[s].astype(F32), tags)
    out_ref[slots * BLOCK :, :] = tags.astype(BF16)
    for s in range(slots):
        if fetch:
            for copy in copies[s]:
                copy.wait()

        @pl.when(codes[s] > 0)
        def _(s=s):
            x = jnp.concatenate(
                [xs[s][c * BLOCK : (c + 1) * BLOCK, :] for c in range(chunks)], axis=1
            )
            gate_part = gate_buf[s] if fetch else gate_ref[experts[s]]
            up_part = up_buf[s] if fetch else up_ref[experts[s]]
            gate = jnp.dot(x, gate_part, preferred_element_type=F32)
            up = jnp.dot(x, up_part, preferred_element_type=F32)
            hidden = gate / (1.0 + jnp.exp(-gate)) * up
            out_ref[s * BLOCK : (s + 1) * BLOCK, :] = hidden.astype(BF16)


def hidden_rows(arrived, gate_weight, up_weight, fetch=False):
    slots = len(arrived)
    _, model_width, hidden_width = gate_weight.shape
    place = far if fetch else near
    held = [pltpu.VMEM((slots, model_width, hidden_width), BF16)] * 2
    return pl.pallas_call(
        lambda *refs: hidden_kernel(*refs, slots=slots, model_width=model_width, fetch=fetch),
        in_specs=[pl.BlockSpec(memory_space=pltpu.VMEM)] * slots
        + [pl.BlockSpec(memory_space=pl.ANY if fetch else pltpu.VMEM)] * 2,
        out_specs=pl.BlockSpec(memory_space=pltpu.VMEM),
        out_shape=pltpu.VMEM((slots * BLOCK + TAG, hidden_width), BF16),
        scratch_shapes=held + [pltpu.SemaphoreType.DMA((2, slots))] if fetch else [],
        compiler_params=pltpu.CompilerParams(vmem_limit_bytes=VMEM_BYTES),
        name="hidden",
    )(*[near(x) for x in arrived], place(gate_weight), place(up_weight))


def bring_kernel(_, gate_ref, up_ref, gate_out, up_out, sem):
    copies = [
        pltpu.make_async_copy(gate_ref, gate_out, sem.at[0]),
        pltpu.make_async_copy(up_ref, up_out, sem.at[1]),
    ]
    for copy in copies:
        copy.start()
    for copy in copies:
        copy.wait()


def bring(after, gate_weight, up_weight):
    return pl.pallas_call(
        bring_kernel,
        in_specs=[pl.BlockSpec(memory_space=pl.ANY)] * 3,
        out_specs=[pl.BlockSpec(memory_space=pltpu.VMEM)] * 2,
        out_shape=[pltpu.VMEM(w.shape, w.dtype) for w in (gate_weight, up_weight)],
        scratch_shapes=[pltpu.SemaphoreType.DMA((2,))],
        compiler_params=pltpu.CompilerParams(vmem_limit_bytes=VMEM_BYTES),
        name="bring",
    )(after, far(gate_weight), far(up_weight))


def fold(tile):
    row = lax.broadcasted_iota(jnp.int32, (HALF, LANE), 0)
    lane = lax.broadcasted_iota(jnp.int32, (HALF, LANE), 1)
    upper, lower = tile[:HALF, :], tile[HALF:, :]
    folded = jnp.where((lane < HALF) & (lane < row), pltpu.roll(lower, HALF, 1), upper)
    corner = jnp.sum(jnp.where(lane == row + HALF, lower, 0.0), axis=0, keepdims=True)
    return folded, corner


def unfold(folded, corner):
    row = lax.broadcasted_iota(jnp.int32, (HALF, LANE), 0)
    lane = lax.broadcasted_iota(jnp.int32, (HALF, LANE), 1)
    flipped = jnp.concatenate([folded, jnp.zeros((HALF, LANE), F32)], axis=0).T
    upper = jnp.where(lane < row, flipped[:HALF, :], folded)
    below, above = pltpu.roll(folded, HALF, 1), pltpu.roll(flipped[:HALF, :], HALF, 1)
    inner = jnp.where(lane - HALF < row, below, jnp.where(lane - HALF == row, corner, above))
    return jnp.concatenate([upper, jnp.where(lane < HALF, flipped[HALF:, :], inner)], axis=0)


def gram_kernel(first_ref, *refs, counts, kept):
    groups, out_ref = refs[: len(counts)], refs[-1]
    out_ref[...] = refs[-2][...] if len(refs) > len(counts) + 1 else jnp.zeros(out_ref.shape, F32)
    lane = lax.broadcasted_iota(jnp.int32, (TAG, LANE), 1)
    where = [(ref, s, n) for ref, n in zip(groups, counts) for s in range(n)]
    codes = []
    for ref, s, n in where:
        tag = ref[n * BLOCK : n * BLOCK + TAG, :LANE].astype(F32)
        codes.append(jnp.max(jnp.where(lane == s, tag, 0.0)).astype(jnp.int32))
    for code, (ref, s, n) in zip(codes, where):
        local = code - 1 - first_ref[0]

        @pl.when((local >= 0) & (local < kept))
        def _(ref=ref, s=s, local=local):
            hidden = ref[s * BLOCK : (s + 1) * BLOCK, :]
            even, odd = 2 * local, 2 * local + 1
            parts = [
                lax.dot_general(
                    hidden[:, i * LANE : (i + 1) * LANE],
                    hidden[:, i * LANE :],
                    TN,
                    preferred_element_type=F32,
                )
                for i in range(3)
            ]
            folds = [fold(part[:, :LANE]) for part in parts]
            for i, (_, corner) in enumerate(folds):
                out_ref[even, TIP + i : TIP + i + 1, :] += corner
            out_ref[even, :HALF, :] += folds[0][0]
            out_ref[even, HALF:SECOND, :] += parts[0][:, LANE : 2 * LANE]
            out_ref[even, SECOND:THIRD, :] += folds[1][0]
            out_ref[even, THIRD:TIP, :] += folds[2][0][:QUARTER, :]
            out_ref[odd, :LANE, :] += parts[0][:, 2 * LANE :]
            out_ref[odd, LANE : 2 * LANE, :] += parts[1][:, LANE:]
            out_ref[odd, THIRD:TIP, :] += folds[2][0][QUARTER:, :]


def gram(first, kept, groups, prior=()):
    counts = [(g.shape[0] - TAG) // BLOCK for g in groups]
    return pl.pallas_call(
        lambda *refs: gram_kernel(*refs, counts=counts, kept=kept),
        in_specs=[pl.BlockSpec(memory_space=pltpu.SMEM)]
        + [pl.BlockSpec(memory_space=pltpu.VMEM)] * (len(groups) + len(prior)),
        out_specs=pl.BlockSpec(memory_space=pltpu.VMEM),
        out_shape=pltpu.VMEM((2 * kept, TIP + 8, LANE), F32),
        compiler_params=pltpu.CompilerParams(vmem_limit_bytes=VMEM_BYTES),
        name="gram",
    )(first, *[near(x) for x in (*groups, *prior)])


def factor_strip(groups, lane0, sub):
    wide = lambda v: jnp.concatenate([v] * (groups[0].shape[1] // LANE), axis=1)
    groups = list(groups)
    wide_sub = wide(sub)
    for b in range(len(groups)):
        base = lane0 + 8 * b
        cols = [
            [jnp.broadcast_to(g[:, base + j : base + j + 1], (8, LANE)) for g in groups[b:]]
            for j in range(8)
        ]
        for k in range(8):
            inv = lax.rsqrt(cols[k][0][k : k + 1, :])
            row = groups[b][k : k + 1, :] * wide(inv)
            mult = [jnp.where(sub > k, cols[k][0], 0.0)] + cols[k][1:]
            mult = [c * inv for c in mult]
            for g, m in enumerate(mult):
                groups[b + g] = groups[b + g] - wide(m) * row
            groups[b] = jnp.where(wide_sub == k, row, groups[b])
            for j in range(k + 1, 8):
                top = cols[j][0][k : k + 1, :] * inv
                cols[j] = [c - m * top for c, m in zip(cols[j], mult)]
    return groups


def dot_high(a, b, dims):
    return lax.dot_general(a, b, dims, precision=HIGH, preferred_element_type=F32)


def factor_panel(work):
    sub = lax.broadcasted_iota(jnp.int32, (8, LANE), 0)
    lane = lax.broadcasted_iota(jnp.int32, (8, LANE), 1)
    width = work.shape[1]
    for r0 in range(0, LANE, STRIP):
        r1 = r0 + STRIP
        groups = factor_strip([work[r : r + 8, :] for r in range(r0, r1, 8)], r0, sub)
        diag = jnp.concatenate(
            [
                jnp.where(lane >= r0 + 8 * g + sub, rows[:, :LANE], 0.0)
                for g, rows in enumerate(groups)
            ],
            axis=0,
        )
        strip = diag
        if width > LANE:
            right = jnp.concatenate([rows[:, LANE:] for rows in groups], axis=0)
            strip = jnp.concatenate([diag, right], axis=1)
        work[r0:r1, :] = strip
        if r1 < LANE:
            work[r1:, :] = work[r1:, :] - dot_high(diag.T[r1:, :], strip, NN)


def identity_tile():
    shape = (LANE, LANE)
    rows, cols = (lax.broadcasted_iota(jnp.int32, shape, axis) for axis in range(2))
    return jnp.where(rows == cols, 1.0, 0.0)


def diagonal(folded, corner, scale):
    return unfold(folded * scale, corner * scale) + RIDGE * identity_tile()


def first_kernel(part_ref, top_ref, mid_ref, cross_ref, *, scale):
    tip = lambda i: part_ref[TIP + i : TIP + i + 1, :]
    top_ref[:, :LANE] = diagonal(part_ref[:HALF, :], tip(0), scale)
    top_ref[:, LANE : 2 * LANE] = part_ref[HALF:SECOND, :] * scale
    top_ref[:, 2 * LANE :] = identity_tile()
    factor_panel(top_ref)
    side = top_ref[:, LANE : 2 * LANE]
    mid_ref[:, :LANE] = diagonal(part_ref[SECOND:THIRD, :], tip(1), scale) - dot_high(side, side, TN)
    mid_ref[:, LANE:] = identity_tile()
    cross_ref[...] = dot_high(side, top_ref[:, 2 * LANE :], TN)
    factor_panel(mid_ref)


def first_panels(part, scale):
    return pl.pallas_call(
        lambda *refs: first_kernel(*refs, scale=scale),
        out_shape=[pltpu.VMEM((LANE, n * LANE), F32) for n in (3, 2, 1)],
        compiler_params=pltpu.CompilerParams(vmem_limit_bytes=VMEM_BYTES),
        name="first_panels",
    )(near(part))


def last_kernel(part_ref, other_ref, top_ref, mid_ref, cross_ref, out_ref, low, *, scale):
    corner = other_ref[:LANE, :] * scale
    right = dot_high(top_ref[:, 2 * LANE :], corner, NN)
    rest = other_ref[LANE : 2 * LANE, :] * scale - dot_high(cross_ref[...], corner, NN)
    below = dot_high(mid_ref[:, LANE:], rest, NN)
    folded = jnp.concatenate([part_ref[THIRD:TIP, :], other_ref[THIRD:TIP, :]], axis=0)
    low[...] = (
        diagonal(folded, part_ref[TIP + 2 : TIP + 3, :], scale)
        - dot_high(right, right, TN)
        - dot_high(below, below, TN)
    )
    factor_panel(low)
    kind = out_ref.dtype
    out_ref[:LANE, : 2 * LANE] = top_ref[:, : 2 * LANE].astype(kind)
    out_ref[:LANE, 2 * LANE :] = right.astype(kind)
    out_ref[LANE : 2 * LANE, :LANE] = jnp.zeros((LANE, LANE), kind)
    out_ref[LANE : 2 * LANE, LANE : 2 * LANE] = mid_ref[:, :LANE].astype(kind)
    out_ref[LANE : 2 * LANE, 2 * LANE :] = below.astype(kind)
    out_ref[2 * LANE :, : 2 * LANE] = jnp.zeros((LANE, 2 * LANE), kind)
    out_ref[2 * LANE :, 2 * LANE :] = low[...].astype(kind)


def last_panel(part, other, top, mid, cross, scale):
    width = top.shape[1]
    return pl.pallas_call(
        lambda *refs: last_kernel(*refs, scale=scale),
        out_shape=pltpu.VMEM((width, width), BF16),
        scratch_shapes=[pltpu.VMEM((LANE, LANE), F32)],
        compiler_params=pltpu.CompilerParams(vmem_limit_bytes=VMEM_BYTES),
        name="last_panel",
    )(*[near(x) for x in (part, other, top, mid, cross)])


def on_device(tokens, block_expert, gate_weight, up_weight):
    owners = lax.axis_size("expert")
    replicas = lax.axis_size("dp")
    experts_each, _, hidden_width = gate_weight.shape
    chips = owners // 2
    shifts = [(0, 0), (0, 1)] + [(dy, dc) for dc in range(2) for dy in (1, chips - 1)]
    shifts += [(2, 0), (2, 1)]
    member = lax.axis_index("expert").reshape(1)
    outgoing = pack(block_expert, member, tokens, experts_each, shifts, chips)
    pairs = [(d, d ^ 1) for d in range(replicas)]
    arrived, gathered = [], []
    weights = (gate_weight, up_weight)

    def swap_rows(g):
        rows = hidden_rows(arrived[EDGES[g] : EDGES[g + 1]], *weights, fetch=g == 0)
        gathered.append([rows, lax.ppermute(rows, "dp", pairs)])

    for (dy, dc), payload in zip(shifts, outgoing):
        route = [
            (y * 2 + c, ((y + dy) % chips) * 2 + (c + dc) % 2)
            for y in range(chips)
            for c in range(2)
        ]
        if dy == 2 and not gathered:
            swap_rows(0)
            weights = bring(gathered[0][0], gate_weight, up_weight)
        if dy == 2:
            payload, _ = lax.optimization_barrier((payload, gathered[0][0]))
        arrived.append(payload if dy == dc == 0 else lax.ppermute(payload, "expert", route))
    for g in range(1, len(EDGES) - 1):
        swap_rows(g)
    kept = experts_each // 2
    first = (lax.axis_index("dp") % 2 * kept).reshape(1)
    partial_gram = gram(first, kept, [rows for pair in gathered[:-2] for rows in pair])
    tail = [rows for pair in gathered[-2:] for rows in pair]
    partial_gram = gram(first, kept, tail, (partial_gram,))
    side = replicas // SIDE
    classes = [[x * SIDE + z for z in range(p, SIDE, 2) for x in range(side)] for p in range(2)]
    pieces = lax.all_to_all(
        partial_gram, "dp", split_axis=0, concat_axis=0, axis_index_groups=classes, tiled=True
    )
    own = jnp.sum(pieces, axis=0)
    halves = [(d + SIDE, d) for d in range(replicas) if d // SIDE % 2 == 0]
    other = lax.ppermute(own[:TIP], "dp", halves)
    scale = experts_each / (tokens.shape[0] * replicas)
    top, mid, cross = first_panels(own, scale)
    result = last_panel(own, other, top, mid, cross, scale)
    row_count = hidden_width // replicas
    sent = result.reshape(replicas, row_count, hidden_width)
    returned = lax.all_to_all(sent, "dp", split_axis=0, concat_axis=0, tiled=True)
    returned = returned.reshape(2, 2, 2, 2, row_count, hidden_width)[:, 0]
    returned = jnp.transpose(returned, (2, 1, 0, 3, 4))
    returned = returned.reshape(experts_each, row_count, hidden_width)
    return returned.astype(F32)


def solution(mesh):
    placed = (
        P(("dp", "expert"), None),
        P(("dp", "expert")),
        P("expert", None, None),
        P("expert", None, None),
    )

    return jax.shard_map(
        on_device, mesh=mesh, in_specs=placed, out_specs=P("expert", "dp", None), check_vma=False
    )
```

```python
import jax
import jax.numpy as jnp
from jax import lax
from jax.experimental import pallas as pl
from jax.experimental.pallas import tpu as pltpu
from jax.sharding import PartitionSpec as P


BLOCK = 128
RIDGE = 0.05
LANE = 128
TAG = 16
SIDE = 4
VMEM_BYTES = 20 << 20
EDGES = (0, 2, 4, 6, 7, 8)
STRIP = 64
F32 = jnp.float32
BF16 = jnp.bfloat16
HIGH = lax.Precision.HIGHEST
TN = (((0,), (0,)), ((), ()))
NN = (((1,), (0,)), ((), ()))
HALF = 64
QUARTER = 32
SECOND = HALF + LANE
THIRD = SECOND + HALF
TIP = THIRD + QUARTER


def near(x):
    return pltpu.with_memory_space_constraint(x, pltpu.VMEM)


def far(x):
    return pltpu.with_memory_space_constraint(x, pltpu.HBM)


def pack_kernel(member_ref, assign_hbm, tok_hbm, *rest, experts_each, shifts, chips):
    outs = rest[: len(shifts)]
    assign_ref, tok_ref, sem = rest[len(shifts) :]
    blocks, chunks = tok_ref.shape[0] // BLOCK, tok_ref.shape[1] // LANE
    fetch = [
        pltpu.make_async_copy(assign_hbm, assign_ref, sem.at[0]),
        pltpu.make_async_copy(tok_hbm, tok_ref, sem.at[1]),
    ]
    for copy in fetch:
        copy.start()
    for copy in fetch:
        copy.wait()
    chip = lax.div(member_ref[0], 2)
    core = lax.rem(member_ref[0], 2)
    for (dy, dc), out in zip(shifts, outs):
        dest = lax.rem(chip + dy, chips) * 2 + lax.rem(core + dc, 2)
        block = jnp.int32(0)
        code = jnp.int32(0)
        for b in range(blocks):
            expert = assign_ref[b]
            owner = lax.div(expert, experts_each)
            hit = owner == dest
            block = jnp.where(hit, b, block)
            code = jnp.where(hit, expert - owner * experts_each + 1, code)
        row = pl.multiple_of(block * BLOCK, BLOCK)
        for c in range(chunks):
            out[c * BLOCK : (c + 1) * BLOCK, :] = tok_ref[
                pl.ds(row, BLOCK), c * LANE : (c + 1) * LANE
            ]
        out[chunks * BLOCK :, :] = jnp.full((TAG, LANE), code.astype(F32), F32).astype(BF16)


def pack(assign, member, tokens, experts_each, shifts, chips):
    rows = BLOCK * tokens.shape[1] // LANE + TAG
    return pl.pallas_call(
        lambda *refs: pack_kernel(*refs, experts_each=experts_each, shifts=shifts, chips=chips),
        in_specs=[pl.BlockSpec(memory_space=pltpu.SMEM)]
        + [pl.BlockSpec(memory_space=pl.ANY)] * 2,
        out_specs=[pl.BlockSpec(memory_space=pltpu.VMEM)] * len(shifts),
        out_shape=[pltpu.VMEM((rows, LANE), BF16)] * len(shifts),
        scratch_shapes=[
            pltpu.SMEM(assign.shape, assign.dtype),
            pltpu.VMEM(tokens.shape, tokens.dtype),
            pltpu.SemaphoreType.DMA((2,)),
        ],
        compiler_params=pltpu.CompilerParams(vmem_limit_bytes=VMEM_BYTES),
        name="pack",
    )(member, far(assign), far(tokens))


def hidden_kernel(*refs, slots, model_width, fetch):
    xs = refs[:slots]
    gate_ref, up_ref, out_ref = refs[slots : slots + 3]
    chunks = model_width // LANE
    codes = []
    for s in range(slots):
        tag = xs[s][chunks * BLOCK : chunks * BLOCK + TAG, :].astype(F32)
        codes.append(jnp.max(tag).astype(jnp.int32))
    experts = [jnp.maximum(code - 1, 0) for code in codes]
    if fetch:
        gate_buf, up_buf, sem = refs[slots + 3 :]
        copies = []
        for s in range(slots):
            copies.append(
                (
                    pltpu.make_async_copy(gate_ref.at[experts[s]], gate_buf.at[s], sem.at[0, s]),
                    pltpu.make_async_copy(up_ref.at[experts[s]], up_buf.at[s], sem.at[1, s]),
                )
            )
            for copy in copies[-1]:
                copy.start()

    width = out_ref.shape[1]
    lane = lax.broadcasted_iota(jnp.int32, (TAG, width), 1)
    tags = jnp.zeros((TAG, width), F32)
    for s in range(slots):
        tags = jnp.where(lane == s, codes[s].astype(F32), tags)
    out_ref[slots * BLOCK :, :] = tags.astype(BF16)
    for s in range(slots):
        if fetch:
            for copy in copies[s]:
                copy.wait()

        @pl.when(codes[s] > 0)
        def _(s=s):
            x = jnp.concatenate(
                [xs[s][c * BLOCK : (c + 1) * BLOCK, :] for c in range(chunks)], axis=1
            )
            gate_part = gate_buf[s] if fetch else gate_ref[experts[s]]
            up_part = up_buf[s] if fetch else up_ref[experts[s]]
            gate = jnp.dot(x, gate_part, preferred_element_type=F32)
            up = jnp.dot(x, up_part, preferred_element_type=F32)
            hidden = gate / (1.0 + jnp.exp(-gate)) * up
            out_ref[s * BLOCK : (s + 1) * BLOCK, :] = hidden.astype(BF16)


def hidden_rows(arrived, gate_weight, up_weight, fetch=False):
    slots = len(arrived)
    _, model_width, hidden_width = gate_weight.shape
    place = far if fetch else near
    held = [pltpu.VMEM((slots, model_width, hidden_width), BF16)] * 2
    return pl.pallas_call(
        lambda *refs: hidden_kernel(*refs, slots=slots, model_width=model_width, fetch=fetch),
        in_specs=[pl.BlockSpec(memory_space=pltpu.VMEM)] * slots
        + [pl.BlockSpec(memory_space=pl.ANY if fetch else pltpu.VMEM)] * 2,
        out_specs=pl.BlockSpec(memory_space=pltpu.VMEM),
        out_shape=pltpu.VMEM((slots * BLOCK + TAG, hidden_width), BF16),
        scratch_shapes=held + [pltpu.SemaphoreType.DMA((2, slots))] if fetch else [],
        compiler_params=pltpu.CompilerParams(vmem_limit_bytes=VMEM_BYTES),
        name="hidden",
    )(*[near(x) for x in arrived], place(gate_weight), place(up_weight))


def bring_kernel(_, gate_ref, up_ref, gate_out, up_out, sem):
    copies = [
        pltpu.make_async_copy(gate_ref, gate_out, sem.at[0]),
        pltpu.make_async_copy(up_ref, up_out, sem.at[1]),
    ]
    for copy in copies:
        copy.start()
    for copy in copies:
        copy.wait()


def bring(after, gate_weight, up_weight):
    return pl.pallas_call(
        bring_kernel,
        in_specs=[pl.BlockSpec(memory_space=pl.ANY)] * 3,
        out_specs=[pl.BlockSpec(memory_space=pltpu.VMEM)] * 2,
        out_shape=[pltpu.VMEM(w.shape, w.dtype) for w in (gate_weight, up_weight)],
        scratch_shapes=[pltpu.SemaphoreType.DMA((2,))],
        compiler_params=pltpu.CompilerParams(vmem_limit_bytes=VMEM_BYTES),
        name="bring",
    )(after, far(gate_weight), far(up_weight))


def fold(tile):
    row = lax.broadcasted_iota(jnp.int32, (HALF, LANE), 0)
    lane = lax.broadcasted_iota(jnp.int32, (HALF, LANE), 1)
    upper, lower = tile[:HALF, :], tile[HALF:, :]
    folded = jnp.where((lane < HALF) & (lane < row), pltpu.roll(lower, HALF, 1), upper)
    corner = jnp.sum(jnp.where(lane == row + HALF, lower, 0.0), axis=0, keepdims=True)
    return folded, corner


def unfold(folded, corner):
    row = lax.broadcasted_iota(jnp.int32, (HALF, LANE), 0)
    lane = lax.broadcasted_iota(jnp.int32, (HALF, LANE), 1)
    flipped = jnp.concatenate([folded, jnp.zeros((HALF, LANE), F32)], axis=0).T
    upper = jnp.where(lane < row, flipped[:HALF, :], folded)
    below, above = pltpu.roll(folded, HALF, 1), pltpu.roll(flipped[:HALF, :], HALF, 1)
    inner = jnp.where(lane - HALF < row, below, jnp.where(lane - HALF == row, corner, above))
    return jnp.concatenate([upper, jnp.where(lane < HALF, flipped[HALF:, :], inner)], axis=0)


def gram_kernel(first_ref, *refs, counts, kept):
    groups, out_ref = refs[: len(counts)], refs[-1]
    out_ref[...] = refs[-2][...] if len(refs) > len(counts) + 1 else jnp.zeros(out_ref.shape, F32)
    lane = lax.broadcasted_iota(jnp.int32, (TAG, LANE), 1)
    where = [(ref, s, n) for ref, n in zip(groups, counts) for s in range(n)]
    codes = []
    for ref, s, n in where:
        tag = ref[n * BLOCK : n * BLOCK + TAG, :LANE].astype(F32)
        codes.append(jnp.max(jnp.where(lane == s, tag, 0.0)).astype(jnp.int32))
    for code, (ref, s, n) in zip(codes, where):
        local = code - 1 - first_ref[0]

        @pl.when((local >= 0) & (local < kept))
        def _(ref=ref, s=s, local=local):
            hidden = ref[s * BLOCK : (s + 1) * BLOCK, :]
            even, odd = 2 * local, 2 * local + 1
            parts = [
                lax.dot_general(
                    hidden[:, i * LANE : (i + 1) * LANE],
                    hidden[:, i * LANE :],
                    TN,
                    preferred_element_type=F32,
                )
                for i in range(3)
            ]
            folds = [fold(part[:, :LANE]) for part in parts]
            for i, (_, corner) in enumerate(folds):
                out_ref[even, TIP + i : TIP + i + 1, :] += corner
            out_ref[even, :HALF, :] += folds[0][0]
            out_ref[even, HALF:SECOND, :] += parts[0][:, LANE : 2 * LANE]
            out_ref[even, SECOND:THIRD, :] += folds[1][0]
            out_ref[even, THIRD:TIP, :] += folds[2][0][:QUARTER, :]
            out_ref[odd, :LANE, :] += parts[0][:, 2 * LANE :]
            out_ref[odd, LANE : 2 * LANE, :] += parts[1][:, LANE:]
            out_ref[odd, THIRD:TIP, :] += folds[2][0][QUARTER:, :]


def gram(first, kept, groups, prior=()):
    counts = [(g.shape[0] - TAG) // BLOCK for g in groups]
    return pl.pallas_call(
        lambda *refs: gram_kernel(*refs, counts=counts, kept=kept),
        in_specs=[pl.BlockSpec(memory_space=pltpu.SMEM)]
        + [pl.BlockSpec(memory_space=pltpu.VMEM)] * (len(groups) + len(prior)),
        out_specs=pl.BlockSpec(memory_space=pltpu.VMEM),
        out_shape=pltpu.VMEM((2 * kept, TIP + 8, LANE), F32),
        compiler_params=pltpu.CompilerParams(vmem_limit_bytes=VMEM_BYTES),
        name="gram",
    )(first, *[near(x) for x in (*groups, *prior)])


def factor_strip(groups, lane0, sub):
    wide = lambda v: jnp.concatenate([v] * (groups[0].shape[1] // LANE), axis=1)
    groups = list(groups)
    wide_sub = wide(sub)
    for b in range(len(groups)):
        base = lane0 + 8 * b
        cols = [
            [jnp.broadcast_to(g[:, base + j : base + j + 1], (8, LANE)) for g in groups[b:]]
            for j in range(8)
        ]
        for k in range(8):
            inv = lax.rsqrt(cols[k][0][k : k + 1, :])
            row = groups[b][k : k + 1, :] * wide(inv)
            mult = [jnp.where(sub > k, cols[k][0], 0.0)] + cols[k][1:]
            mult = [c * inv for c in mult]
            for g, m in enumerate(mult):
                groups[b + g] = groups[b + g] - wide(m) * row
            groups[b] = jnp.where(wide_sub == k, row, groups[b])
            for j in range(k + 1, 8):
                top = cols[j][0][k : k + 1, :] * inv
                cols[j] = [c - m * top for c, m in zip(cols[j], mult)]
    return groups


def dot_high(a, b, dims):
    return lax.dot_general(a, b, dims, precision=HIGH, preferred_element_type=F32)


def factor_panel(work):
    sub = lax.broadcasted_iota(jnp.int32, (8, LANE), 0)
    lane = lax.broadcasted_iota(jnp.int32, (8, LANE), 1)
    width = work.shape[1]
    for r0 in range(0, LANE, STRIP):
        r1 = r0 + STRIP
        groups = factor_strip([work[r : r + 8, :] for r in range(r0, r1, 8)], r0, sub)
        diag = jnp.concatenate(
            [
                jnp.where(lane >= r0 + 8 * g + sub, rows[:, :LANE], 0.0)
                for g, rows in enumerate(groups)
            ],
            axis=0,
        )
        strip = diag
        if width > LANE:
            right = jnp.concatenate([rows[:, LANE:] for rows in groups], axis=0)
            strip = jnp.concatenate([diag, right], axis=1)
        work[r0:r1, :] = strip
        if r1 < LANE:
            work[r1:, :] = work[r1:, :] - dot_high(diag.T[r1:, :], strip, NN)


def identity_tile():
    shape = (LANE, LANE)
    rows, cols = (lax.broadcasted_iota(jnp.int32, shape, axis) for axis in range(2))
    return jnp.where(rows == cols, 1.0, 0.0)


def diagonal(folded, corner, scale):
    return unfold(folded * scale, corner * scale) + RIDGE * identity_tile()


def first_kernel(part_ref, top_ref, mid_ref, cross_ref, *, scale):
    tip = lambda i: part_ref[TIP + i : TIP + i + 1, :]
    top_ref[:, :LANE] = diagonal(part_ref[:HALF, :], tip(0), scale)
    top_ref[:, LANE : 2 * LANE] = part_ref[HALF:SECOND, :] * scale
    top_ref[:, 2 * LANE :] = identity_tile()
    factor_panel(top_ref)
    side = top_ref[:, LANE : 2 * LANE]
    mid_ref[:, :LANE] = diagonal(part_ref[SECOND:THIRD, :], tip(1), scale) - dot_high(side, side, TN)
    mid_ref[:, LANE:] = identity_tile()
    cross_ref[...] = dot_high(side, top_ref[:, 2 * LANE :], TN)
    factor_panel(mid_ref)


def first_panels(part, scale):
    return pl.pallas_call(
        lambda *refs: first_kernel(*refs, scale=scale),
        out_shape=[pltpu.VMEM((LANE, n * LANE), F32) for n in (3, 2, 1)],
        compiler_params=pltpu.CompilerParams(vmem_limit_bytes=VMEM_BYTES),
        name="first_panels",
    )(near(part))


def last_kernel(part_ref, other_ref, top_ref, mid_ref, cross_ref, out_ref, low, *, scale):
    corner = other_ref[:LANE, :] * scale
    right = dot_high(top_ref[:, 2 * LANE :], corner, NN)
    rest = other_ref[LANE : 2 * LANE, :] * scale - dot_high(cross_ref[...], corner, NN)
    below = dot_high(mid_ref[:, LANE:], rest, NN)
    folded = jnp.concatenate([part_ref[THIRD:TIP, :], other_ref[THIRD:TIP, :]], axis=0)
    low[...] = (
        diagonal(folded, part_ref[TIP + 2 : TIP + 3, :], scale)
        - dot_high(right, right, TN)
        - dot_high(below, below, TN)
    )
    factor_panel(low)
    kind = out_ref.dtype
    out_ref[:LANE, : 2 * LANE] = top_ref[:, : 2 * LANE].astype(kind)
    out_ref[:LANE, 2 * LANE :] = right.astype(kind)
    out_ref[LANE : 2 * LANE, :LANE] = jnp.zeros((LANE, LANE), kind)
    out_ref[LANE : 2 * LANE, LANE : 2 * LANE] = mid_ref[:, :LANE].astype(kind)
    out_ref[LANE : 2 * LANE, 2 * LANE :] = below.astype(kind)
    out_ref[2 * LANE :, : 2 * LANE] = jnp.zeros((LANE, 2 * LANE), kind)
    out_ref[2 * LANE :, 2 * LANE :] = low[...].astype(kind)


def last_panel(part, other, top, mid, cross, scale):
    width = top.shape[1]
    return pl.pallas_call(
        lambda *refs: last_kernel(*refs, scale=scale),
        out_shape=pltpu.VMEM((width, width), BF16),
        scratch_shapes=[pltpu.VMEM((LANE, LANE), F32)],
        compiler_params=pltpu.CompilerParams(vmem_limit_bytes=VMEM_BYTES),
        name="last_panel",
    )(*[near(x) for x in (part, other, top, mid, cross)])


def on_device(tokens, block_expert, gate_weight, up_weight):
    owners = lax.axis_size("expert")
    replicas = lax.axis_size("dp")
    experts_each, _, hidden_width = gate_weight.shape
    chips = owners // 2
    shifts = [(0, 0), (0, 1)] + [(dy, dc) for dc in range(2) for dy in (1, chips - 1)]
    shifts += [(2, 0), (2, 1)]
    member = lax.axis_index("expert").reshape(1)
    outgoing = pack(block_expert, member, tokens, experts_each, shifts, chips)
    pairs = [(d, d ^ 1) for d in range(replicas)]
    arrived, gathered = [], []
    weights = (gate_weight, up_weight)

    def swap_rows(g):
        rows = hidden_rows(arrived[EDGES[g] : EDGES[g + 1]], *weights, fetch=g == 0)
        gathered.append([rows, lax.ppermute(rows, "dp", pairs)])

    for (dy, dc), payload in zip(shifts, outgoing):
        route = [
            (y * 2 + c, ((y + dy) % chips) * 2 + (c + dc) % 2)
            for y in range(chips)
            for c in range(2)
        ]
        if dy == 2 and not gathered:
            swap_rows(0)
            weights = bring(gathered[0][0], gate_weight, up_weight)
        if dy == 2:
            payload, _ = lax.optimization_barrier((payload, gathered[0][0]))
        arrived.append(payload if dy == dc == 0 else lax.ppermute(payload, "expert", route))
    for g in range(1, len(EDGES) - 1):
        swap_rows(g)
    kept = experts_each // 2
    first = (lax.axis_index("dp") % 2 * kept).reshape(1)
    partial_gram = gram(first, kept, [rows for pair in gathered[:-1] for rows in pair])
    tail = [rows for pair in gathered[-1:] for rows in pair]
    partial_gram = gram(first, kept, tail, (partial_gram,))
    side = replicas // SIDE
    classes = [[x * SIDE + z for z in range(p, SIDE, 2) for x in range(side)] for p in range(2)]
    pieces = lax.all_to_all(
        partial_gram, "dp", split_axis=0, concat_axis=0, axis_index_groups=classes, tiled=True
    )
    own = jnp.sum(pieces, axis=0)
    halves = [(d + SIDE, d) for d in range(replicas) if d // SIDE % 2 == 0]
    other = lax.ppermute(own[:TIP], "dp", halves)
    scale = experts_each / (tokens.shape[0] * replicas)
    top, mid, cross = first_panels(own, scale)
    result = last_panel(own, other, top, mid, cross, scale)
    row_count = hidden_width // replicas
    sent = result.reshape(replicas, row_count, hidden_width)
    returned = lax.all_to_all(sent, "dp", split_axis=0, concat_axis=0, tiled=True)
    returned = returned.reshape(2, 2, 2, 2, row_count, hidden_width)[:, 0]
    returned = jnp.transpose(returned, (2, 1, 0, 3, 4))
    returned = returned.reshape(experts_each, row_count, hidden_width)
    return returned.astype(F32)


def solution(mesh):
    placed = (
        P(("dp", "expert"), None),
        P(("dp", "expert")),
        P("expert", None, None),
        P("expert", None, None),
    )

    return jax.shard_map(
        on_device, mesh=mesh, in_specs=placed, out_specs=P("expert", "dp", None), check_vma=False
    )
```
